32 devices in a mesh: dp: 8 (over y, x, core), seq: 4 (over z).
Axes of the slice: x: 2, y: 2, z: 4, core: 2. Of those that a mesh axis runs over, the one named last changes fastest.
Arguments:
- hidden_in: bfloat16 [8192, 768], P(('dp', 'seq')), may hold values from -6 to 6
- skip_values: bfloat16 [8192, 384], P(('dp', 'seq')), may hold values from -6 to 6
- out_grad: bfloat16 [8192, 768], P(('dp', 'seq')), may hold values from -6 to 6
- doc_lens: int32 [8, 3], P('dp'), may hold values from 0 to 1024, as said below
- valid: int32 [8192], P('dp'), may hold values from 0 to 1, as said below
- norm1_gain: float32 [768], replicated, may hold values from 0.5 to 1.5
- norm1_shift: float32 [768], replicated, may hold values from -1.25 to 1.25
- query_w: bfloat16 [768, 768], replicated, may hold values from -0.3125 to 0.3125
- query_b: float32 [768], replicated, may hold values from -1.25 to 1.25
- key_w: bfloat16 [768, 768], replicated, may hold values from -0.3125 to 0.3125
- value_w: bfloat16 [768, 384], replicated, may hold values from -0.21875 to 0.21875
- value_b: float32 [384], replicated, may hold values from -1.25 to 1.25
- proj_w: bfloat16 [768, 768], replicated, may hold values from -0.625 to 0.625
- proj_b: float32 [768], replicated, may hold values from -1.25 to 1.25
- norm2_gain: float32 [768], replicated, may hold values from 0.5 to 1.5
- norm2_shift: float32 [768], replicated, may hold values from -1.25 to 1.25
- fc_w: bfloat16 [768, 3072], replicated, may hold values from -0.21875 to 0.21875
- fc_b: float32 [3072], replicated, may hold values from -1.25 to 1.25
- out_w: bfloat16 [3072, 768], replicated, may hold values from -0.109375 to 0.109375
- out_b: float32 [768], replicated, may hold values from -1.25 to 1.25
Outputs:
- output: bfloat16 [8192, 768], P(('dp', 'seq'))
- grad_input: bfloat16 [8192, 768], P(('dp', 'seq'))
- grad_skip: bfloat16 [8192, 384], P(('dp', 'seq'))
- grad_norm1_gain: float32 [768], replicated
- grad_norm1_shift: float32 [768], replicated
- grad_query_w: float32 [768, 768], replicated
- grad_query_b: float32 [768], replicated
- grad_key_w: float32 [768, 768], replicated
- grad_value_w: float32 [768, 384], replicated
- grad_value_b: float32 [384], replicated
- grad_proj_w: float32 [768, 768], replicated
- grad_proj_b: float32 [768], replicated
- grad_norm2_gain: float32 [768], replicated
- grad_norm2_shift: float32 [768], replicated
- grad_fc_w: float32 [768, 3072], replicated
- grad_fc_b: float32 [3072], replicated
- grad_out_w: float32 [3072, 768], replicated
- grad_out_b: float32 [768], replicated
- norms: float32 [8, 3], P('dp')
The draws below stay inside these ranges and needn't reach their ends.
Inputs may be any that keep to these rules, and one draw needn't show every extreme that they name: `doc_lens`: row g lists the lengths of the sequences packed in order into group g and sums to 1024. In 8 // 2 groups one sequence fills the whole group and the other entries are 0; every other group holds three sequences, the longest of 512 tokens. Of the two tokens 2 i and 2 i + 1, at least one has valid = 1.
All inputs are finite; a program needn't handle non-finite values.
Results may differ from the reference program's by a relative error of at most 0.014.
The reference program's roundings to bfloat16 on the way count: a program that leaves them out, or rounds other values in their place, can miss the bound.
Values may be sent and summed in bfloat16 or wider, within the bound.
A program may use at most 192 MiB of HBM per device.

```python
import math
import jax
import jax.numpy as jnp
from jax import lax

D = 768
HEADS = 12
HDIM = 64
FF = 3072
GTOK = 1024
TOKENS = 8192
VFRESH = 384
VSKIP = 384
N_DP = 8


def draw_valid(key, part):
    pair_codes = jax.random.randint(key, (TOKENS // 2,), 0, 4)
    first_valid = (pair_codes != 1).astype(jnp.int32)
    second_valid = (pair_codes != 0).astype(jnp.int32)
    return jnp.stack([first_valid, second_valid], axis=1).reshape(TOKENS)


def draw_doc_lens(key, part):
    order_key = jax.random.fold_in(key, 11)
    split_key = jax.random.fold_in(key, 12)
    turn_key = jax.random.fold_in(key, 13)
    order = jax.random.permutation(order_key, N_DP)
    whole_group = order < N_DP // 2
    half = GTOK // 2
    middle_len = jax.random.randint(split_key, (N_DP,), 1, half)
    short_rows = jnp.stack([jnp.full((N_DP,), half, jnp.int32), middle_len.astype(jnp.int32), (half - middle_len).astype(jnp.int32)], axis=1)
    turns = jax.random.randint(turn_key, (N_DP,), 0, 3)
    places = (jnp.arange(3, dtype=jnp.int32)[None, :] - turns[:, None]) % 3
    short_rows = jnp.take_along_axis(short_rows, places, axis=1)
    long_rows = jnp.zeros((N_DP, 3), jnp.int32).at[:, 0].set(GTOK)
    return jnp.where(whole_group[:, None], long_rows, short_rows).astype(jnp.int32)


def levels(own_key, dims, split, low, top_value):
    level, own = 1.0, jax.random.fold_in(own_key, 6)
    for position, shards_of in split:
        steps = jnp.exp(jax.random.uniform(jax.random.fold_in(own, position), (shards_of,), jnp.float32, low / len(split), top_value / len(split)))
        level = level * jnp.repeat(steps, dims[position] // shards_of).reshape([-1 if axis == position else 1 for axis in range(len(dims))])
    return level


def scatter_about(key, shape, width, most, pieces=(), kind=jnp.bfloat16):
    level = levels(key, shape, pieces, -0.22, 0.18) if pieces else 1.0
    values = jax.random.normal(key, shape, jnp.float32) * width * level
    return jnp.minimum(jnp.maximum(values, -most), most).astype(kind)


def setup_inputs(seed: int = 0) -> dict:
    streams_of = jax.random.split(jax.random.key(seed), 21)
    return {
        "hidden_in": scatter_about(streams_of[0], (TOKENS, D), 1.0, 6.0, ((0, 32),)),
        "skip_values": scatter_about(streams_of[1], (TOKENS, VSKIP), 1.0, 6.0, ((0, 32),)),
        "out_grad": scatter_about(streams_of[2], (TOKENS, D), 1.0, 6.0, ((0, 32),)),
        "doc_lens": draw_doc_lens(jax.random.fold_in(streams_of[20], 71), 0),
        "valid": draw_valid(jax.random.fold_in(streams_of[20], 71), 0),
        "norm1_gain": jnp.clip(1.0 + 0.1 * jax.random.normal(streams_of[5], (D,), jnp.float32), 0.5, 1.5),
        "norm1_shift": scatter_about(streams_of[6], (D,), 0.2, 1.25, (), jnp.float32),
        "query_w": scatter_about(streams_of[7], (D, D), (D // 2) ** -0.5, 0.3125),
        "query_b": scatter_about(streams_of[8], (D,), 0.2, 1.25, (), jnp.float32),
        "key_w": scatter_about(streams_of[9], (D, D), (D // 2) ** -0.5, 0.3125),
        "value_w": scatter_about(streams_of[10], (D, VFRESH), D ** -0.5, 0.21875),
        "value_b": scatter_about(streams_of[11], (VFRESH,), 0.2, 1.25, (), jnp.float32),
        "proj_w": scatter_about(streams_of[12], (D, D), (D // 8) ** -0.5, 0.625),
        "proj_b": scatter_about(streams_of[13], (D,), 0.2, 1.25, (), jnp.float32),
        "norm2_gain": jnp.clip(1.0 + 0.1 * jax.random.normal(streams_of[14], (D,), jnp.float32), 0.5, 1.5),
        "norm2_shift": scatter_about(streams_of[15], (D,), 0.2, 1.25, (), jnp.float32),
        "fc_w": scatter_about(streams_of[16], (D, FF), D ** -0.5, 0.21875),
        "fc_b": scatter_about(streams_of[17], (FF,), 0.2, 1.25, (), jnp.float32),
        "out_w": scatter_about(streams_of[18], (FF, D), FF ** -0.5, 0.109375),
        "out_b": scatter_about(streams_of[19], (D,), 0.2, 1.25, (), jnp.float32),
    }


@jax.custom_vjp
def low(v):
    return lax.optimization_barrier(v.astype(jnp.bfloat16)).astype(jnp.float32)

@jax.custom_vjp
def low_back(v):
    return v

def low_keep(v):
    return (low(v), None)

def low_pass(kept, grad):
    return (grad,)

def back_keep(v):
    return (v, None)

def back_low(kept, grad):
    return (low(grad),)
low.defvjp(low_keep, low_pass)
low_back.defvjp(back_keep, back_low)
norm_eps = 1e-05
square_eps = 1e-06
tanh_coef = 0.7978845608028654
masked_score = -1e+30

def rounded(values):
    return low(low_back(values))

def product(former, latter):
    return jnp.dot(former, latter, precision=lax.Precision.HIGHEST)

def gelu_tanh(values):
    inner_arg = tanh_coef * (values + 0.044715 * values * values * values)
    return 0.5 * values * (1.0 + jnp.tanh(inner_arg))

def layer_norm(values, norm_gain, norm_shift):
    centre = lax.optimization_barrier(jnp.mean(values, axis=-1, keepdims=True))
    spread = values - centre
    second = lax.optimization_barrier(jnp.mean(spread * spread, axis=-1, keepdims=True))
    return spread * lax.rsqrt(second + norm_eps) * norm_gain + norm_shift

def segment_ids(lengths, row_count):
    bounds = jnp.cumsum(lengths.astype(jnp.int32))[:-1]
    places = jnp.arange(row_count, dtype=jnp.int32)
    return lax.optimization_barrier(jnp.sum((places[:, None] >= bounds[None, :]).astype(jnp.int32), axis=1))

def attend_block(query_block, first_row, key_heads, value_heads, segments, valid_row):
    block_rows = query_block.shape[0]
    total_rows = key_heads.shape[0]
    scores = jnp.einsum('qhd,khd->hqk', query_block, key_heads, precision=lax.Precision.HIGHEST) * (1.0 / math.sqrt(HDIM))
    row_index = first_row + jnp.arange(block_rows, dtype=jnp.int32)
    columns = jnp.arange(total_rows, dtype=jnp.int32)
    row_segments = lax.dynamic_slice_in_dim(segments, first_row, block_rows, 0)
    allowed = (row_segments[:, None] == segments[None, :]) & (columns[None, :] <= row_index[:, None])
    allowed = allowed & ((valid_row[None, :] > 0) | (columns[None, :] == row_index[:, None]))
    scores = low_back(jnp.where(allowed[None], scores, masked_score))
    row_top = lax.optimization_barrier(jnp.max(scores, axis=-1, keepdims=True))
    powered = jnp.where(allowed[None], jnp.exp(scores - row_top), 0.0)
    weights = low(powered / lax.optimization_barrier(jnp.sum(powered, axis=-1, keepdims=True)))
    return jnp.einsum('hqk,khd->qhd', weights, value_heads, precision=lax.Precision.HIGHEST)

def attention(query_heads, key_heads, value_heads, segments, valid_row):
    block_rows = min(512, GTOK)
    block_count = GTOK // block_rows
    blocks = query_heads.reshape(block_count, block_rows, HEADS, HDIM)
    first_rows = jnp.arange(block_count, dtype=jnp.int32) * block_rows
    checked = jax.checkpoint(attend_block)
    mixed_rows = lax.map(lambda element: checked(element[0], element[1], key_heads, value_heads, segments, valid_row), (blocks, first_rows))
    return mixed_rows.reshape(GTOK, D)

def forward(hidden, skip_rows, weights, segments, valid_row):
    norm1_gain, norm1_shift, query_w, query_b, key_w, value_w, value_b, proj_w, proj_b, norm2_gain, norm2_shift, fc_w, fc_b, out_w, out_b = weights
    normed = low(layer_norm(hidden, norm1_gain, norm1_shift))
    queries = rounded(product(normed, query_w) + query_b)
    keys_all = rounded(product(normed, key_w))
    fresh_values = low(product(normed, value_w) + value_b)
    values_all = low_back(jnp.concatenate([fresh_values, skip_rows], axis=1))
    mixed_rows = attention(queries.reshape(GTOK, HEADS, HDIM), keys_all.reshape(GTOK, HEADS, HDIM), values_all.reshape(GTOK, HEADS, HDIM), segments, valid_row)
    mixed_rows = rounded(mixed_rows)
    attn_out = low_back(product(mixed_rows, proj_w)) + proj_b
    middle = hidden + attn_out
    normed_two = low(layer_norm(middle, norm2_gain, norm2_shift))
    hidden_pre = low_back(product(normed_two, fc_w)) + fc_b
    active = low(gelu_tanh(hidden_pre))
    mlp_out = low_back(product(active, out_w)) + out_b
    return (middle + mlp_out, attn_out, mlp_out)

def reference(hidden_in, skip_values, out_grad, doc_lens, valid, norm1_gain, norm1_shift, query_w, query_b, key_w, value_w, value_b, proj_w, proj_b, norm2_gain, norm2_shift, fc_w, fc_b, out_w, out_b):
    weights = tuple((weight.astype(jnp.float32) for weight in (norm1_gain, norm1_shift, query_w, query_b, key_w, value_w, value_b, proj_w, proj_b, norm2_gain, norm2_shift, fc_w, fc_b, out_w, out_b)))
    stacked = (hidden_in.astype(jnp.float32).reshape(N_DP, GTOK, D), skip_values.astype(jnp.float32).reshape(N_DP, GTOK, VSKIP), out_grad.astype(jnp.float32).reshape(N_DP, GTOK, D), doc_lens.astype(jnp.int32), valid.astype(jnp.int32).reshape(N_DP, GTOK))

    def group_step(totals, element):
        hidden, skip_rows, cotangent, lengths, valid_row = element
        segments = segment_ids(lengths, GTOK)

        def closed(hidden_arg, skip_arg, weight_arg):
            return forward(hidden_arg, skip_arg, weight_arg, segments, valid_row)
        outs_now, pullback = jax.vjp(closed, hidden, skip_rows, weights)
        result, attn_out, mlp_out = outs_now
        grad_hidden, grad_skip_rows, grad_weights = pullback((cotangent, jnp.zeros_like(attn_out), jnp.zeros_like(mlp_out)))
        totals = jax.tree.map(lambda former, latter: former + latter, totals, grad_weights)
        weighting = valid_row.astype(jnp.float32)
        valid_count = jnp.sum(weighting)

        def square_sum(values):
            return jnp.sum(weighting * lax.optimization_barrier(jnp.sum(values * values, axis=1)))
        square_sums = jnp.stack([square_sum(hidden), square_sum(attn_out), square_sum(mlp_out)])
        norm_values = jnp.sqrt(square_sums / (valid_count * D) + square_eps)
        return (totals, (result.astype(jnp.bfloat16), grad_hidden.astype(jnp.bfloat16), grad_skip_rows.astype(jnp.bfloat16), norm_values))
    zero_grads = jax.tree.map(jnp.zeros_like, weights)
    totals, (result, grad_hidden, grad_skip_rows, norm_values) = lax.scan(group_step, zero_grads, stacked)
    return (result.reshape(TOKENS, D), grad_hidden.reshape(TOKENS, D), grad_skip_rows.reshape(TOKENS, VSKIP), totals[0], totals[1], totals[2], totals[3], totals[4], totals[5], totals[6], totals[7], totals[8], totals[9], totals[10], totals[11], totals[12], totals[13], totals[14], norm_values)
```

```python
import functools
import math

import jax
import jax.numpy as jnp
from jax import lax
from jax.experimental import pallas as pl
from jax.experimental.pallas import tpu as pltpu
from jax.sharding import PartitionSpec as P

D = 768
HEADS = 12
HDIM = 64
VFRESH = 384


norm_eps = 1e-05
square_eps = 1e-06
tanh_coef = 0.7978845608028654
masked_score = -1e30


MESH = pl.DeviceIdType.MESH
SHARES = [(k, 1) for k in "ababzabababababzab"]
SUB = 16
WID = 768
UNIT_BYTES = SUB * WID * 2


def bits_of(n):
    return n.bit_length() - 1


def partner(dim, dp, sq):
    kind, j = dim
    step = 1 << j
    if kind == "dp":
        bit = (dp // step) % 2
        return bit, (dp + step - 2 * step * bit, sq)
    bit = (sq // step) % 2
    return bit, (dp, sq + step - 2 * step * bit)


def plan_streams(n_dp, n_seq, half_units, shares):
    dpb = [("dp", j) for j in range(1, bits_of(n_dp))]
    sqb = [("seq", j) for j in range(bits_of(n_seq))]
    mid = len(dpb) // 2
    orders = {"a": dpb + sqb, "b": dpb[mid:] + dpb[:mid] + sqb, "z": sqb + dpb}
    quantum = (n_dp // 2) * n_seq
    total = half_units // quantum
    weight = sum(w for _, w in shares)
    streams, first, used, acc = [], 0, 0, 0
    for kind, w in shares:
        acc += w
        upto = round(total * acc / weight)
        n = (upto - used) * quantum
        used = upto
        if n:
            streams.append((first, n, orders[kind]))
            first += n
    return streams


def schedule(streams, n_dp):
    rate = 45e3
    free = {}
    now = []
    out = []
    stages = []
    for first, n, order in streams:
        seq = []
        size = n
        seq.append((("dp", 0), size))
        for d in order:
            size //= 2
            seq.append((d, size))
        for d in reversed(order):
            seq.append((d, size))
            size *= 2
        seq.append((("dp", 0), size))
        stages.append(seq)
    ready = [0.0] * len(streams)
    at = [0] * len(streams)
    pending = []

    def launch(s, t):
        d, size = stages[s][at[s]]
        b = size * UNIT_BYTES / 1e6
        if d == ("dp", 0):
            res, dur = "c", b / 0.5
        elif d[0] == "dp":
            res, dur = d, b / 0.045
        else:
            res, dur = "seq", b / 0.045 * (1 << d[1])
        st = max(t, free.get(res, 0.0))
        free[res] = st + dur
        pending.append((st + dur + 2.5, s))

    for s in range(len(streams)):
        launch(s, 0.0)
    while pending:
        pending.sort()
        t, s = pending.pop(0)
        out.append((s, at[s]))
        at[s] += 1
        if at[s] < len(stages[s]):
            launch(s, t + 0.5)
    return out, t


class Exchange:
    def __init__(self, streams, half_units, dp, sq, part, out, acc, recv, gat, sems):
        self.streams, self.half_units = streams, half_units
        self.dp, self.sq = dp, sq
        self.part, self.out, self.acc, self.recv, self.gat = part, out, acc, recv, gat
        self.send_sem, self.recv_sem, self.local_sem = sems
        self.cbit, self.cdev = partner(("dp", 0), dp, sq)
        self.off = [[s[0]] for s in streams]
        self.roff = []
        r = half_units
        for first, n, order in streams:
            rows = [first]
            size = n
            for d in order:
                size //= 2
                rows.append(r)
                r += size
            self.roff.append(rows)
        self.recv_units = r

    @staticmethod
    def recv_total(streams, half_units):
        r = half_units
        for first, n, order in streams:
            size = n
            for d in order:
                size //= 2
                r += size
        return r

    def n_stages(self, s):
        return 2 * (len(self.streams[s][2]) + 1)

    def remote(self, s, k, src, dst, dev):
        return pltpu.make_async_remote_copy(
            src_ref=src, dst_ref=dst, send_sem=self.send_sem.at[s, k], recv_sem=self.recv_sem.at[s, k],
            device_id=dev, device_id_type=MESH)

    def copies(self, s, k):
        first, n, order = self.streams[s]
        depth = len(order)
        if k == 0:
            other = (1 - self.cbit) * self.half_units + first
            mine = self.cbit * self.half_units + first
            return (self.remote(s, k, self.part.at[pl.ds(other, n)], self.recv.at[pl.ds(first, n)], self.cdev),
                    pltpu.make_async_copy(self.part.at[pl.ds(mine, n)], self.acc.at[pl.ds(first, n)], self.local_sem.at[s, 0]))
        if k <= depth:
            half = n >> k
            bit, dev = partner(order[k - 1], self.dp, self.sq)
            base = self.off[s][k - 1]
            return (self.remote(s, k, self.acc.at[pl.ds(base + (1 - bit) * half, half)],
                                self.recv.at[pl.ds(self.roff[s][k], half)], dev), None)
        g = 2 * depth + 1 - k
        if g >= 1:
            half = n >> g
            bit, dev = partner(order[g - 1], self.dp, self.sq)
            here = self.gat.at[pl.ds(self.off[s][g], half)]
            return (self.remote(s, k, here, here, dev), None)
        mine = self.cbit * self.half_units + first
        here = self.gat.at[pl.ds(first, n)]
        there = self.out.at[pl.ds(mine, n)]
        return (self.remote(s, k, here, there, self.cdev),
                pltpu.make_async_copy(here, there, self.local_sem.at[s, 1]))

    def start(self, s, k):
        for c in self.copies(s, k):
            if c is not None:
                c.start()

    def finish(self, s, k):
        first, n, order = self.streams[s]
        depth = len(order)
        remote, local = self.copies(s, k)
        remote.wait()
        if local is not None:
            local.wait()
        if k <= depth:
            half = n >> k
            if k == 0:
                off = first
            else:
                bit, _ = partner(order[k - 1], self.dp, self.sq)
                off = self.off[s][k - 1] + bit * half
                self.off[s].append(off)
            roff = self.roff[s][k]
            self.add(off, roff, half, self.gat if k == depth else self.acc)

    def add(self, off, roff, n, to):
        acc, recv = self.acc, self.recv
        step = 4 if n % 4 == 0 else (3 if n % 3 == 0 else (2 if n % 2 == 0 else 1))

        def body(i, c):
            a = pl.ds(off + i * step, step)
            b = pl.ds(roff + i * step, step)
            to[a] = acc[a] + recv[b]
            return c

        lax.fori_loop(0, n // step, body, 0)

    def step(self, s, k):
        self.finish(s, k)
        if k + 1 < self.n_stages(s):
            self.start(s, k + 1)


def ar_kernel(cfg, part, small, out, small_z, small_out, acc, recv, gat, srecv, send_sem, recv_sem, local_sem, ssend, srecv_sem):
    n_dp, n_seq, half_units, streams, order = cfg
    dp, sq = lax.axis_index("dp"), lax.axis_index("seq")
    sdims = [("seq", j) for j in range(bits_of(n_seq))] + [("dp", j) for j in range(bits_of(n_dp))]
    nz = bits_of(n_seq)
    barrier = pltpu.get_barrier_semaphore()
    for d in sdims:
        _, dev = partner(d, dp, sq)
        pl.semaphore_signal(barrier, inc=1, device_id=dev, device_id_type=MESH)
    pl.semaphore_wait(barrier, len(sdims))
    ex = Exchange(streams, half_units, dp, sq, part, out, acc, recv, gat, (send_sem, recv_sem, local_sem))
    small_out[...] = small[...]

    def small_copy(i):
        _, dev = partner(sdims[i], dp, sq)
        return pltpu.make_async_remote_copy(src_ref=srecv.at[2 * i], dst_ref=srecv.at[2 * i + 1], send_sem=ssend.at[i],
                                            recv_sem=srecv_sem.at[i], device_id=dev, device_id_type=MESH)

    for s in range(len(streams)):
        ex.start(s, 0)
    srecv[0] = small[...]
    small_copy(0).start()
    done = 0
    n_small = len(sdims)
    gap = max(1, len(order) // (n_small + 2))
    for idx, (s, k) in enumerate(order):
        ex.step(s, k)
        if done < n_small and (idx % gap == gap - 1 or idx == len(order) - 1):
            while done < n_small:
                small_copy(done).wait()
                total = srecv[2 * done] + srecv[2 * done + 1]
                done += 1
                if done == nz:
                    small_z[...] = total
                if done < n_small:
                    srecv[2 * done] = total
                    small_copy(done).start()
                else:
                    small_out[...] = total
                if idx != len(order) - 1:
                    break


def all_reduce(mesh, part, small, shares, collective_id):
    n_dp, n_seq = mesh.shape["dp"], mesh.shape["seq"]
    units = part.shape[0]
    half = units // 2
    streams = plan_streams(n_dp, n_seq, half, shares)
    order, est = schedule(streams, n_dp)
    n_st = 2 * (bits_of(n_dp) + bits_of(n_seq))
    recv_units = Exchange.recv_total(streams, half)
    n_small = bits_of(n_dp) + bits_of(n_seq)
    vmem = pl.BlockSpec(memory_space=pltpu.VMEM)
    hbm = pl.BlockSpec(memory_space=pl.ANY)
    ns = len(streams)
    return pl.pallas_call(
        functools.partial(ar_kernel, (n_dp, n_seq, half, streams, order)),
        out_shape=(jax.ShapeDtypeStruct(part.shape, part.dtype), jax.ShapeDtypeStruct(small.shape, small.dtype),
                   jax.ShapeDtypeStruct(small.shape, small.dtype)),
        in_specs=[hbm, vmem], out_specs=(hbm, vmem, vmem),
        scratch_shapes=[
            pltpu.VMEM((half, SUB, WID), jnp.bfloat16), pltpu.VMEM((recv_units, SUB, WID), jnp.bfloat16), pltpu.VMEM((half, SUB, WID), jnp.bfloat16),
            pltpu.VMEM((2 * n_small,) + small.shape, small.dtype),
            pltpu.SemaphoreType.DMA((ns, n_st)), pltpu.SemaphoreType.DMA((ns, n_st)), pltpu.SemaphoreType.DMA((ns, 2)),
            pltpu.SemaphoreType.DMA((n_small,)), pltpu.SemaphoreType.DMA((n_small,))],
        compiler_params=pltpu.CompilerParams(collective_id=collective_id, has_side_effects=True, vmem_limit_bytes=56 * 2**20),
        name="grad_all_reduce",
    )(part, small)


def gelu_tanh(values):
    inner_arg = tanh_coef * (values + 0.044715 * values * values * values)
    return 0.5 * values * (1.0 + jnp.tanh(inner_arg))


def layer_norm(values, norm_gain, norm_shift):
    centre = jnp.mean(values, axis=-1, keepdims=True)
    spread = values - centre
    second = jnp.mean(spread * spread, axis=-1, keepdims=True)
    return spread * lax.rsqrt(second + norm_eps) * norm_gain + norm_shift


def matmul(former, latter):
    return jnp.dot(former, latter, preferred_element_type=jnp.float32)


def matmul_right_t(former, latter):
    return lax.dot_general(
        former, latter, (((1,), (1,)), ((), ())), preferred_element_type=jnp.float32
    )


def matmul_left_t(former, latter):
    return lax.dot_general(
        former, latter, (((0,), (0,)), ((), ())), preferred_element_type=jnp.float32
    )


def segment_ids(lengths, row_count):
    bounds = jnp.cumsum(lengths)[:-1]
    places = jnp.arange(row_count, dtype=jnp.int32)
    return jnp.sum((places[:, None] >= bounds[None, :]).astype(jnp.int32), axis=1)


def block_scores(query_block, key_heads, segments, valid_row, first_row, score_scale):
    block_rows = query_block.shape[0]
    total_rows = key_heads.shape[0]
    scores = (
        jnp.einsum("qhd,khd->hqk", query_block, key_heads, preferred_element_type=jnp.float32)
        * score_scale
    )
    row_index = first_row + jnp.arange(block_rows, dtype=jnp.int32)
    columns = jnp.arange(total_rows, dtype=jnp.int32)
    row_segments = lax.dynamic_slice_in_dim(segments, first_row, block_rows, 0)
    allowed = (row_segments[:, None] == segments[None, :]) & (
        columns[None, :] <= row_index[:, None]
    )
    allowed = allowed & ((valid_row[None, :] > 0) | (columns[None, :] == row_index[:, None]))
    return (jnp.where(allowed[None], scores, masked_score), allowed)


def attend_forward(
    query_heads, key_heads, value_heads, segments, valid_row, block_rows, score_scale
):
    total_rows = query_heads.shape[0]

    def one_block(block):
        first_row = block * block_rows
        query_block = lax.dynamic_slice_in_dim(query_heads, first_row, block_rows, 0)
        scores, allowed = block_scores(
            query_block, key_heads, segments, valid_row, first_row, score_scale
        )
        row_top = jnp.max(scores, axis=-1, keepdims=True)
        powered = jnp.where(allowed[None], jnp.exp(scores - row_top), 0.0)
        row_totals = jnp.sum(powered, axis=-1, keepdims=True)
        weights = (powered / row_totals).astype(jnp.bfloat16)
        mixed_block = jnp.einsum(
            "hqk,khd->qhd", weights, value_heads, preferred_element_type=jnp.float32
        )
        return (mixed_block.astype(jnp.bfloat16), (row_top + jnp.log(row_totals))[..., 0])

    mixed_blocks, log_totals = lax.map(
        one_block, jnp.arange(total_rows // block_rows, dtype=jnp.int32)
    )
    return (mixed_blocks.reshape(total_rows, -1), log_totals)


def attend_backward(
    query_heads,
    key_heads,
    value_heads,
    grad_heads,
    log_totals,
    segments,
    valid_row,
    block_rows,
    score_scale,
):
    total_rows = query_heads.shape[0]

    def one_block(carry, element):
        key_acc, value_acc = carry
        block, block_totals = element
        first_row = block * block_rows
        query_block = lax.dynamic_slice_in_dim(query_heads, first_row, block_rows, 0)
        grad_block = lax.dynamic_slice_in_dim(grad_heads, first_row, block_rows, 0)
        scores, allowed = block_scores(
            query_block, key_heads, segments, valid_row, first_row, score_scale
        )
        probs = jnp.where(allowed[None], jnp.exp(scores - block_totals[:, :, None]), 0.0)
        prob_grad = jnp.einsum(
            "qhd,khd->hqk", grad_block, value_heads, preferred_element_type=jnp.float32
        )
        centre = jnp.sum(probs * prob_grad, axis=-1, keepdims=True)
        score_grad = (probs * (prob_grad - centre)).astype(jnp.bfloat16)
        query_part = (
            jnp.einsum("hqk,khd->qhd", score_grad, key_heads, preferred_element_type=jnp.float32)
            * score_scale
        )
        key_acc = (
            key_acc
            + jnp.einsum(
                "hqk,qhd->khd", score_grad, query_block, preferred_element_type=jnp.float32
            )
            * score_scale
        )
        value_acc = value_acc + jnp.einsum(
            "hqk,qhd->khd",
            probs.astype(jnp.bfloat16),
            grad_block,
            preferred_element_type=jnp.float32,
        )
        return ((key_acc, value_acc), query_part.astype(jnp.bfloat16))

    zero_heads = jnp.zeros(key_heads.shape, jnp.float32)
    block_ids = jnp.arange(total_rows // block_rows, dtype=jnp.int32)
    (key_acc, value_acc), query_parts = lax.scan(
        one_block, (zero_heads, zero_heads), (block_ids, log_totals)
    )
    flat_shape = (total_rows, key_heads.shape[1] * key_heads.shape[2])
    return (
        query_parts.reshape(flat_shape),
        key_acc.astype(jnp.bfloat16).reshape(flat_shape),
        value_acc.astype(jnp.bfloat16).reshape(flat_shape),
    )


def local(
    mesh,
    hidden_in,
    skip_values,
    out_grad,
    doc_lens,
    valid,
    norm1_gain,
    norm1_shift,
    query_w,
    query_b,
    key_w,
    value_w,
    value_b,
    proj_w,
    proj_b,
    norm2_gain,
    norm2_shift,
    fc_w,
    fc_b,
    out_w,
    out_b,
):
    tok_rows = hidden_in.shape[0]
    seq_size = lax.axis_size("seq")
    seq_rank = lax.axis_index("seq")
    group_rows = tok_rows * seq_size
    heads_here = HEADS // seq_size
    block_rows = min(512, group_rows)
    score_scale = 1.0 / math.sqrt(HDIM)
    head_shape = (group_rows, heads_here, HDIM)
    segments = segment_ids(doc_lens[0], group_rows)
    hidden = hidden_in.astype(jnp.float32)
    normed, norm1_pull = jax.vjp(layer_norm, hidden, norm1_gain, norm1_shift)
    normed_low = normed.astype(jnp.bfloat16)
    fresh_values = (matmul(normed_low, value_w) + value_b).astype(jnp.bfloat16)
    value_rows = jnp.concatenate([fresh_values, skip_values], axis=1)
    query_rows = (matmul(normed_low, query_w) + query_b).astype(jnp.bfloat16)
    key_rows = matmul(normed_low, key_w).astype(jnp.bfloat16)
    query_heads, key_heads, value_heads = (
        lax.all_to_all(query_rows, "seq", split_axis=1, concat_axis=0, tiled=True),
        lax.all_to_all(key_rows, "seq", split_axis=1, concat_axis=0, tiled=True),
        lax.all_to_all(value_rows, "seq", split_axis=1, concat_axis=0, tiled=True),
    )
    query_split = query_heads.reshape(head_shape)
    key_split = key_heads.reshape(head_shape)
    value_split = value_heads.reshape(head_shape)
    mixed_heads, log_totals = attend_forward(
        query_split, key_split, value_split, segments, valid, block_rows, score_scale
    )
    mixed_rows = lax.all_to_all(mixed_heads, "seq", split_axis=0, concat_axis=1, tiled=True)
    attn_out = matmul(mixed_rows, proj_w) + proj_b
    middle = hidden + attn_out
    normed_two, norm2_pull = jax.vjp(layer_norm, middle, norm2_gain, norm2_shift)
    normed_two_low = normed_two.astype(jnp.bfloat16)
    hidden_pre = matmul(normed_two_low, fc_w) + fc_b
    active, gelu_pull = jax.vjp(gelu_tanh, hidden_pre)
    active_low = active.astype(jnp.bfloat16)
    mlp_out = matmul(active_low, out_w) + out_b
    output = (middle + mlp_out).astype(jnp.bfloat16)
    valid_here = lax.dynamic_slice_in_dim(valid, seq_rank * tok_rows, tok_rows, 0).astype(
        jnp.float32
    )

    def square_sum(values):
        return jnp.sum(valid_here * jnp.sum(values * values, axis=1))

    square_parts = jnp.stack(
        [square_sum(hidden), square_sum(attn_out), square_sum(mlp_out), jnp.sum(valid_here)]
    )
    cotangent = out_grad.astype(jnp.float32)
    grad_out_b = jnp.sum(cotangent, axis=0)
    grad_out_w = matmul_left_t(active_low, out_grad)
    active_grad = matmul_right_t(out_grad, out_w)
    pre_grad = gelu_pull(active_grad)[0]
    grad_fc_b = jnp.sum(pre_grad, axis=0)
    pre_grad_low = pre_grad.astype(jnp.bfloat16)
    grad_fc_w = matmul_left_t(normed_two_low, pre_grad_low)
    two_grad = matmul_right_t(pre_grad_low, fc_w)
    middle_part, grad_norm2_gain, grad_norm2_shift = norm2_pull(two_grad)
    middle_grad = cotangent + middle_part
    grad_proj_b = jnp.sum(middle_grad, axis=0)
    middle_low = middle_grad.astype(jnp.bfloat16)
    grad_proj_w = matmul_left_t(mixed_rows, middle_low)
    mixed_grad = matmul_right_t(middle_low, proj_w).astype(jnp.bfloat16)
    grad_heads = lax.all_to_all(mixed_grad, "seq", split_axis=1, concat_axis=0, tiled=True)
    query_grad, key_grad, value_grad = attend_backward(
        query_split,
        key_split,
        value_split,
        grad_heads.reshape(head_shape),
        log_totals,
        segments,
        valid,
        block_rows,
        score_scale,
    )
    query_grad_rows, key_grad_rows, value_grad_rows = (
        lax.all_to_all(query_grad, "seq", split_axis=0, concat_axis=1, tiled=True),
        lax.all_to_all(key_grad, "seq", split_axis=0, concat_axis=1, tiled=True),
        lax.all_to_all(value_grad, "seq", split_axis=0, concat_axis=1, tiled=True),
    )
    grad_query_w = matmul_left_t(normed_low, query_grad_rows)
    grad_key_w = matmul_left_t(normed_low, key_grad_rows)
    grad_query_b = jnp.sum(query_grad_rows.astype(jnp.float32), axis=0)
    normed_grad = matmul_right_t(query_grad_rows, query_w) + matmul_right_t(key_grad_rows, key_w)
    fresh_grad = value_grad_rows[:, :VFRESH]
    grad_skip = value_grad_rows[:, VFRESH:]
    grad_value_w = matmul_left_t(normed_low, fresh_grad)
    grad_value_b = jnp.sum(fresh_grad.astype(jnp.float32), axis=0)
    normed_grad = normed_grad + matmul_right_t(fresh_grad, value_w)
    hidden_part, grad_norm1_gain, grad_norm1_shift = norm1_pull(normed_grad)
    grad_input = (middle_grad + hidden_part).astype(jnp.bfloat16)
    big = [grad_query_w, grad_key_w, grad_value_w, grad_proj_w, grad_fc_w, grad_out_w]
    little = [
        grad_norm1_gain, grad_norm1_shift, grad_query_b, grad_value_b, grad_proj_b,
        grad_norm2_gain, grad_norm2_shift, grad_fc_b, grad_out_b,
    ]
    n_dev = lax.axis_size("dp") * seq_size
    rows = sum(g.size for g in big) // WID
    quantum = n_dev * SUB
    padded = -(-rows // quantum) * quantum
    part = jnp.concatenate(
        [g.astype(jnp.bfloat16).reshape(-1, WID) for g in big]
        + [jnp.zeros((padded - rows, WID), jnp.bfloat16)]
    ).reshape(-1, SUB, WID)
    flat = jnp.concatenate(little + [square_parts])
    small = jnp.pad(flat, (0, SUB * WID - flat.size)).reshape(SUB, WID)
    summed, small_z, small_all = all_reduce(mesh, part, small, SHARES, 0)
    summed = summed.reshape(padded, WID)
    at = 0
    outs = []
    for g in big:
        n = g.size // WID
        outs.append(summed[at : at + n].reshape(g.shape).astype(jnp.float32))
        at += n
    grad_query_w, grad_key_w, grad_value_w, grad_proj_w, grad_fc_w, grad_out_w = outs
    at = 0
    outs = []
    flat_all = small_all.reshape(-1)
    for g in little:
        outs.append(flat_all[at : at + g.size])
        at += g.size
    (
        grad_norm1_gain, grad_norm1_shift, grad_query_b, grad_value_b, grad_proj_b,
        grad_norm2_gain, grad_norm2_shift, grad_fc_b, grad_out_b,
    ) = outs
    sums = small_z.reshape(-1)[at : at + 4]
    norm_values = jnp.sqrt(sums[:3] / (sums[3] * D) + square_eps)[None, :]
    return (
        output,
        grad_input,
        grad_skip,
        grad_norm1_gain,
        grad_norm1_shift,
        grad_query_w,
        grad_query_b,
        grad_key_w,
        grad_value_w,
        grad_value_b,
        grad_proj_w,
        grad_proj_b,
        grad_norm2_gain,
        grad_norm2_shift,
        grad_fc_w,
        grad_fc_b,
        grad_out_w,
        grad_out_b,
        norm_values,
    )


def solution(mesh):
    placed = (
        P(("dp", "seq"), None),
        P(("dp", "seq"), None),
        P(("dp", "seq"), None),
        P("dp", None),
        P("dp"),
        P(),
        P(),
        P(),
        P(),
        P(),
        P(),
        P(),
        P(),
        P(),
        P(),
        P(),
        P(),
        P(),
        P(),
        P(),
    )
    return jax.shard_map(
        functools.partial(local, mesh),
        mesh=mesh,
        in_specs=placed,
        out_specs=(
            P(("dp", "seq"), None),
            P(("dp", "seq"), None),
            P(("dp", "seq"), None),
            P(),
            P(),
            P(),
            P(),
            P(),
            P(),
            P(),
            P(),
            P(),
            P(),
            P(),
            P(),
            P(),
            P(),
            P(),
            P("dp", None),
        ),
        check_vma=False,
    )
```

```python
import functools
import math

import jax
import jax.numpy as jnp
from jax import lax
from jax.experimental import pallas as pl
from jax.experimental.pallas import tpu as pltpu
from jax.sharding import PartitionSpec as P

D = 768
HEADS = 12
HDIM = 64
VFRESH = 384


norm_eps = 1e-05
square_eps = 1e-06
tanh_coef = 0.7978845608028654
masked_score = -1e30


MESH = pl.DeviceIdType.MESH
SUB = 16
WID = 768
UNIT_BYTES = SUB * WID * 2
SHARES = ("ababzababzab", "ababab")


def bits_of(n):
    return n.bit_length() - 1


def partner(dim, dp, sq):
    kind, j = dim
    step = 1 << j
    if kind == "dp":
        bit = (dp // step) % 2
        return bit, (dp + step - 2 * step * bit, sq)
    bit = (sq // step) % 2
    return bit, (dp, sq + step - 2 * step * bit)


def plan_streams(n_dp, n_seq, phases, starts):
    dpb = [("dp", j) for j in range(1, bits_of(n_dp))]
    sqb = [("seq", j) for j in range(bits_of(n_seq))]
    mid = len(dpb) // 2
    orders = {"a": dpb + sqb, "b": dpb[mid:] + dpb[:mid] + sqb, "z": sqb + dpb}
    quantum = (n_dp // 2) * n_seq
    streams = []
    for phase, (half_units, kinds) in enumerate(phases):
        total = half_units // quantum
        first = used = 0
        for i, kind in enumerate(kinds):
            upto = round(total * (i + 1) / len(kinds))
            n = (upto - used) * quantum
            used = upto
            if n:
                streams.append((phase, first, n, orders[kind], starts[phase]))
                first += n
    return streams


def schedule(streams, busy=()):
    free = {}
    for res, upto in busy:
        free[res] = upto
    out = []
    stages = []
    for phase, first, n, order, start in streams:
        seq = []
        size = n
        seq.append((("dp", 0), size))
        for d in order:
            size //= 2
            seq.append((d, size))
        for d in reversed(order):
            seq.append((d, size))
            size *= 2
        seq.append((("dp", 0), size))
        stages.append(seq)
    at = [0] * len(streams)
    waiting = [(st[4], s) for s, st in enumerate(streams)]
    pending = []

    def launch(s, t):
        d, size = stages[s][at[s]]
        b = size * UNIT_BYTES / 1e6
        if d == ("dp", 0):
            res, dur = "c", b / 0.5
        elif d[0] == "dp":
            res, dur = d, b / 0.045
        else:
            res, dur = "seq", b / 0.045 * (1 << d[1])
        st = max(t, free.get(res, 0.0))
        free[res] = st + dur
        pending.append((st + dur + 2.0, s))

    while pending or waiting:
        pending.sort()
        waiting.sort()
        if waiting and (not pending or waiting[0][0] <= pending[0][0]):
            t, s = waiting.pop(0)
            launch(s, t)
            continue
        t, s = pending.pop(0)
        out.append((t, s, at[s]))
        at[s] += 1
        if at[s] < len(stages[s]):
            launch(s, t + 0.3)
    return out


class Exchange:
    def __init__(self, streams, halves, dp, sq, parts, out, acc, recv, gat, sems):
        self.streams, self.halves = streams, halves
        self.dp, self.sq = dp, sq
        self.parts, self.out, self.acc, self.recv, self.gat = parts, out, acc, recv, gat
        self.send_sem, self.recv_sem, self.local_sem = sems
        self.cbit, self.cdev = partner(("dp", 0), dp, sq)
        self.base = [sum(halves[:p]) for p in range(len(halves))]
        self.off = [[self.base[s[0]] + s[1]] for s in streams]
        self.roff = []
        r = sum(halves)
        for phase, first, n, order, _ in streams:
            rows = [self.base[phase] + first]
            size = n
            for _ in order:
                size //= 2
                rows.append(r)
                r += size
            self.roff.append(rows)

    @staticmethod
    def recv_total(streams, halves):
        r = sum(halves)
        for phase, first, n, order, _ in streams:
            size = n
            for _ in order:
                size //= 2
                r += size
        return r

    def n_stages(self, s):
        return 2 * (len(self.streams[s][3]) + 1)

    def remote(self, s, k, src, dst, dev):
        return pltpu.make_async_remote_copy(
            src_ref=src, dst_ref=dst, send_sem=self.send_sem.at[s, k], recv_sem=self.recv_sem.at[s, k],
            device_id=dev, device_id_type=MESH)

    def copies(self, s, k):
        phase, first, n, order, _ = self.streams[s]
        depth = len(order)
        half_units, base = self.halves[phase], self.base[phase]
        here = base + first
        if k == 0:
            part = self.parts[phase]
            other = (1 - self.cbit) * half_units + first
            mine = self.cbit * half_units + first
            return (self.remote(s, k, part.at[pl.ds(other, n)], self.recv.at[pl.ds(here, n)], self.cdev),
                    pltpu.make_async_copy(part.at[pl.ds(mine, n)], self.acc.at[pl.ds(here, n)], self.local_sem.at[s, 0]))
        if k <= depth:
            half = n >> k
            bit, dev = partner(order[k - 1], self.dp, self.sq)
            at = self.off[s][k - 1]
            return (self.remote(s, k, self.acc.at[pl.ds(at + (1 - bit) * half, half)],
                                self.recv.at[pl.ds(self.roff[s][k], half)], dev), None)
        g = 2 * depth + 1 - k
        if g >= 1:
            half = n >> g
            bit, dev = partner(order[g - 1], self.dp, self.sq)
            piece = self.gat.at[pl.ds(self.off[s][g], half)]
            return (self.remote(s, k, piece, piece, dev), None)
        piece = self.gat.at[pl.ds(here, n)]
        there = self.out.at[pl.ds(2 * base + self.cbit * half_units + first, n)]
        return (self.remote(s, k, piece, there, self.cdev),
                pltpu.make_async_copy(piece, there, self.local_sem.at[s, 1]))

    def start(self, s, k):
        for c in self.copies(s, k):
            if c is not None:
                c.start()

    def finish(self, s, k):
        phase, first, n, order, _ = self.streams[s]
        depth = len(order)
        remote, local = self.copies(s, k)
        remote.wait()
        if local is not None:
            local.wait()
        if k <= depth:
            half = n >> k
            if k == 0:
                off = self.off[s][0]
            else:
                bit, _ = partner(order[k - 1], self.dp, self.sq)
                off = self.off[s][k - 1] + bit * half
                self.off[s].append(off)
            self.add(off, self.roff[s][k], half, self.gat if k == depth else self.acc)

    def add(self, off, roff, n, to):
        acc, recv = self.acc, self.recv
        step = 4 if n % 4 == 0 else (3 if n % 3 == 0 else (2 if n % 2 == 0 else 1))

        def body(i, c):
            a = pl.ds(off + i * step, step)
            b = pl.ds(roff + i * step, step)
            to[a] = acc[a] + recv[b]
            return c

        lax.fori_loop(0, n // step, body, 0)

    def step(self, s, k):
        self.finish(s, k)
        if k + 1 < self.n_stages(s):
            self.start(s, k + 1)


class Small:
    def __init__(self, n_dp, n_seq, dp, sq, buf, ssend, srecv, small_z, small_out):
        self.dims = [("seq", j) for j in range(bits_of(n_seq))] + [("dp", j) for j in range(bits_of(n_dp))]
        self.nz = bits_of(n_seq)
        self.dp, self.sq, self.buf, self.ssend, self.srecv = dp, sq, buf, ssend, srecv
        self.small_z, self.small_out = small_z, small_out
        self.done = 0

    def copy(self, i):
        _, dev = partner(self.dims[i], self.dp, self.sq)
        return pltpu.make_async_remote_copy(
            src_ref=self.buf.at[2 * i], dst_ref=self.buf.at[2 * i + 1], send_sem=self.ssend.at[i],
            recv_sem=self.srecv.at[i], device_id=dev, device_id_type=MESH)

    def begin(self, value):
        self.buf[0] = value
        self.copy(0).start()

    def step(self):
        i = self.done
        if i == len(self.dims):
            return
        self.copy(i).wait()
        total = self.buf[2 * i] + self.buf[2 * i + 1]
        self.done = i + 1
        if self.done == self.nz:
            self.small_z[...] = total
        if self.done < len(self.dims):
            self.buf[2 * self.done] = total
            self.copy(self.done).start()
        else:
            self.small_out[...] = total

    def rest(self):
        while self.done < len(self.dims):
            self.step()


def entry_barrier(n_dp, n_seq, dp, sq, all_seq):
    barrier = pltpu.get_barrier_semaphore()
    peers = [partner(("dp", j), dp, sq)[1] for j in range(bits_of(n_dp))]
    if all_seq:
        peers += [(dp, (sq + d) % n_seq) for d in range(1, n_seq)]
    else:
        peers += [partner(("seq", j), dp, sq)[1] for j in range(bits_of(n_seq))]
    for dev in peers:
        pl.semaphore_signal(barrier, inc=1, device_id=dev, device_id_type=MESH)
    return barrier, len(peers)


def gelu_tanh(values):
    inner_arg = tanh_coef * (values + 0.044715 * values * values * values)
    return 0.5 * values * (1.0 + jnp.tanh(inner_arg))


def layer_norm(values, norm_gain, norm_shift):
    centre = jnp.mean(values, axis=-1, keepdims=True)
    spread = values - centre
    second = jnp.mean(spread * spread, axis=-1, keepdims=True)
    return spread * lax.rsqrt(second + norm_eps) * norm_gain + norm_shift


def matmul(former, latter):
    return jnp.dot(former, latter, preferred_element_type=jnp.float32)


def matmul_right_t(former, latter):
    return lax.dot_general(
        former, latter, (((1,), (1,)), ((), ())), preferred_element_type=jnp.float32
    )


def matmul_left_t(former, latter):
    return lax.dot_general(
        former, latter, (((0,), (0,)), ((), ())), preferred_element_type=jnp.float32
    )


def segment_ids(lengths, row_count):
    bounds = jnp.cumsum(lengths)[:-1]
    places = jnp.arange(row_count, dtype=jnp.int32)
    return jnp.sum((places[:, None] >= bounds[None, :]).astype(jnp.int32), axis=1)


def block_scores(query_block, key_heads, segments, valid_row, first_row, score_scale):
    block_rows = query_block.shape[0]
    total_rows = key_heads.shape[0]
    scores = (
        jnp.einsum("qhd,khd->hqk", query_block, key_heads, preferred_element_type=jnp.float32)
        * score_scale
    )
    row_index = first_row + jnp.arange(block_rows, dtype=jnp.int32)
    columns = jnp.arange(total_rows, dtype=jnp.int32)
    row_segments = lax.dynamic_slice_in_dim(segments, first_row, block_rows, 0)
    allowed = (row_segments[:, None] == segments[None, :]) & (
        columns[None, :] <= row_index[:, None]
    )
    allowed = allowed & ((valid_row[None, :] > 0) | (columns[None, :] == row_index[:, None]))
    return (jnp.where(allowed[None], scores, masked_score), allowed)


def attend_forward(
    query_heads, key_heads, value_heads, segments, valid_row, block_rows, score_scale
):
    total_rows = query_heads.shape[0]

    def one_block(block):
        first_row = block * block_rows
        query_block = lax.dynamic_slice_in_dim(query_heads, first_row, block_rows, 0)
        scores, allowed = block_scores(
            query_block, key_heads, segments, valid_row, first_row, score_scale
        )
        row_top = jnp.max(scores, axis=-1, keepdims=True)
        powered = jnp.where(allowed[None], jnp.exp(scores - row_top), 0.0)
        row_totals = jnp.sum(powered, axis=-1, keepdims=True)
        weights = (powered / row_totals).astype(jnp.bfloat16)
        mixed_block = jnp.einsum(
            "hqk,khd->qhd", weights, value_heads, preferred_element_type=jnp.float32
        )
        return (mixed_block.astype(jnp.bfloat16), (row_top + jnp.log(row_totals))[..., 0])

    mixed_blocks, log_totals = lax.map(
        one_block, jnp.arange(total_rows // block_rows, dtype=jnp.int32)
    )
    return (mixed_blocks.reshape(total_rows, -1), log_totals)


def attend_backward(
    query_heads,
    key_heads,
    value_heads,
    grad_heads,
    log_totals,
    segments,
    valid_row,
    block_rows,
    score_scale,
):
    total_rows = query_heads.shape[0]

    def one_block(carry, element):
        key_acc, value_acc = carry
        block, block_totals = element
        first_row = block * block_rows
        query_block = lax.dynamic_slice_in_dim(query_heads, first_row, block_rows, 0)
        grad_block = lax.dynamic_slice_in_dim(grad_heads, first_row, block_rows, 0)
        scores, allowed = block_scores(
            query_block, key_heads, segments, valid_row, first_row, score_scale
        )
        probs = jnp.where(allowed[None], jnp.exp(scores - block_totals[:, :, None]), 0.0)
        prob_grad = jnp.einsum(
            "qhd,khd->hqk", grad_block, value_heads, preferred_element_type=jnp.float32
        )
        centre = jnp.sum(probs * prob_grad, axis=-1, keepdims=True)
        score_grad = (probs * (prob_grad - centre)).astype(jnp.bfloat16)
        query_part = (
            jnp.einsum("hqk,khd->qhd", score_grad, key_heads, preferred_element_type=jnp.float32)
            * score_scale
        )
        key_acc = (
            key_acc
            + jnp.einsum(
                "hqk,qhd->khd", score_grad, query_block, preferred_element_type=jnp.float32
            )
            * score_scale
        )
        value_acc = value_acc + jnp.einsum(
            "hqk,qhd->khd",
            probs.astype(jnp.bfloat16),
            grad_block,
            preferred_element_type=jnp.float32,
        )
        return ((key_acc, value_acc), query_part.astype(jnp.bfloat16))

    zero_heads = jnp.zeros(key_heads.shape, jnp.float32)
    block_ids = jnp.arange(total_rows // block_rows, dtype=jnp.int32)
    (key_acc, value_acc), query_parts = lax.scan(
        one_block, (zero_heads, zero_heads), (block_ids, log_totals)
    )
    flat_shape = (total_rows, key_heads.shape[1] * key_heads.shape[2])
    return (
        query_parts.reshape(flat_shape),
        key_acc.astype(jnp.bfloat16).reshape(flat_shape),
        value_acc.astype(jnp.bfloat16).reshape(flat_shape),
    )


FCH = 768
GELU_A = 0.044715


def row_sum(v):
    return jnp.sum(v, axis=0, keepdims=True)


def mlp_kernel(steps, mixed, hidden, og, valid, proj_w, proj_b, n2g, n2s, fc_w, fc_b, out_w, out_b,
               output, mid_grad, mixed_grad, part, proj_part, small,
               nt_ref, xhat_ref, inv_ref, mid_ref, mlp_acc, two_acc):
    j = pl.program_id(0)

    @pl.when(j == 0)
    def _():
        x = hidden[...].astype(jnp.float32)
        attn = matmul(mixed[...], proj_w[...]) + proj_b[...]
        middle = x + attn
        mid_ref[...] = middle
        v = valid[...]
        spread = middle - jnp.mean(middle, axis=-1, keepdims=True)
        inv = lax.rsqrt(jnp.mean(spread * spread, axis=-1, keepdims=True) + norm_eps)
        xhat = spread * inv
        xhat_ref[...] = xhat
        inv_ref[...] = jnp.broadcast_to(inv, inv_ref.shape)
        nt_ref[...] = (xhat * n2g[...] + n2s[...]).astype(jnp.bfloat16)
        small[...] = jnp.zeros_like(small)
        s0 = row_sum(jnp.sum(x * x, axis=-1, keepdims=True) * v)
        s1 = row_sum(jnp.sum(attn * attn, axis=-1, keepdims=True) * v)
        s3 = row_sum(v)
        lane = lax.broadcasted_iota(jnp.int32, (1, WID), 1)
        small[12:13, :] = jnp.where(lane == 0, s0, jnp.where(lane == 1, s1, jnp.where(lane == 3, s3, 0.0)))
        small[7:8, :] = row_sum(og[...].astype(jnp.float32))

    nt = nt_ref[...]
    fw = fc_w[...]
    ow = out_w[...]
    g_low = og[...]
    pre = matmul(nt, fw) + fc_b[...]
    sq = pre * pre
    t = jnp.tanh(tanh_coef * (pre + GELU_A * sq * pre))
    act = (0.5 * pre * (1.0 + t)).astype(jnp.bfloat16)
    slope = 0.5 * (1.0 + t) + 0.5 * pre * (1.0 - t * t) * (tanh_coef * (1.0 + 3.0 * GELU_A * sq))
    pre_grad = matmul_right_t(g_low, ow) * slope
    fcb = row_sum(pre_grad)
    for i in range(steps):
        @pl.when(j == i)
        def _():
            small[8 + i : 9 + i, :] = fcb
    low = pre_grad.astype(jnp.bfloat16)
    part[0, 0] = matmul_left_t(act, g_low).astype(jnp.bfloat16)
    part[0, 1] = matmul_left_t(nt, low).astype(jnp.bfloat16)
    mlp = matmul(act, ow)
    two = matmul_right_t(low, fw)

    @pl.when(j == 0)
    def _():
        mlp_acc[...] = mlp
        two_acc[...] = two

    @pl.when(j > 0)
    def _():
        mlp_acc[...] = mlp_acc[...] + mlp
        two_acc[...] = two_acc[...] + two

    @pl.when(j == steps - 1)
    def _():
        mlp_out = mlp_acc[...] + out_b[...]
        output[...] = (mid_ref[...] + mlp_out).astype(jnp.bfloat16)
        s2 = row_sum(jnp.sum(mlp_out * mlp_out, axis=-1, keepdims=True) * valid[...])
        lane = lax.broadcasted_iota(jnp.int32, (1, WID), 1)
        small[12:13, :] = small[12:13, :] + jnp.where(lane == 2, s2, 0.0)
        two_grad = two_acc[...]
        xhat = xhat_ref[...]
        small[5:6, :] = row_sum(two_grad * xhat)
        small[6:7, :] = row_sum(two_grad)
        e = two_grad * n2g[...]
        centre = jnp.mean(e, axis=-1, keepdims=True)
        along = jnp.mean(e * xhat, axis=-1, keepdims=True)
        grad = og[...].astype(jnp.float32) + (e - centre - xhat * along) * inv_ref[:, 0:1]
        mid_grad[...] = grad
        small[4:5, :] = row_sum(grad)
        grad_low = grad.astype(jnp.bfloat16)
        mixed_grad[...] = matmul_right_t(grad_low, proj_w[...]).astype(jnp.bfloat16)
        proj_part[...] = matmul_left_t(mixed[...], grad_low).astype(jnp.bfloat16)


def mlp_block(mixed, hidden, og, valid_col, proj_w, proj_b, n2g, n2s, fc_w, fc_b, out_w, out_b):
    rows, d = hidden.shape
    ff = fc_w.shape[1]
    steps = ff // FCH
    whole = lambda shape: pl.BlockSpec(shape, lambda j: (0,) * len(shape))
    vec = lambda v: v.reshape(1, -1)
    f32, bf = jnp.float32, jnp.bfloat16
    return pl.pallas_call(
        functools.partial(mlp_kernel, steps),
        grid=(steps,),
        in_specs=[whole((rows, d)), whole((rows, d)), whole((rows, d)), whole((rows, 1)), whole((d, d)), whole((1, d)),
                  whole((1, d)), whole((1, d)), pl.BlockSpec((d, FCH), lambda j: (0, j)), pl.BlockSpec((1, FCH), lambda j: (0, j)),
                  pl.BlockSpec((FCH, d), lambda j: (j, 0)), whole((1, d))],
        out_specs=(whole((rows, d)), whole((rows, d)), whole((rows, d)), pl.BlockSpec((1, 2, FCH, d), lambda j: (j, 0, 0, 0)),
                   whole((d, d)), whole((16, d))),
        out_shape=(jax.ShapeDtypeStruct((rows, d), bf), jax.ShapeDtypeStruct((rows, d), f32), jax.ShapeDtypeStruct((rows, d), bf),
                   jax.ShapeDtypeStruct((steps, 2, FCH, d), bf), jax.ShapeDtypeStruct((d, d), bf), jax.ShapeDtypeStruct((16, d), f32)),
        scratch_shapes=[pltpu.VMEM((rows, d), bf), pltpu.VMEM((rows, d), f32), pltpu.VMEM((rows, 128), f32),
                        pltpu.VMEM((rows, d), f32), pltpu.VMEM((rows, d), f32), pltpu.VMEM((rows, d), f32)],
        compiler_params=pltpu.CompilerParams(vmem_limit_bytes=48 * 2**20, dimension_semantics=("arbitrary",)),
        name="mlp_block",
    )(mixed, hidden, og, valid_col, proj_w, vec(proj_b), vec(n2g), vec(n2s), fc_w, vec(fc_b), out_w, vec(out_b))


PIECE = 384


def widen_kernel(pieces, src, *refs):
    n_out = 6
    outs, (inbuf, stage, in_sem, out_sem) = refs[:n_out], refs[n_out:]
    depth = inbuf.shape[0]

    def fetch(i):
        return pltpu.make_async_copy(src.at[pl.ds(pieces[i][0], PIECE)], inbuf.at[i % depth], in_sem.at[i % depth])

    def put(i):
        slot = i % depth
        _, which, row, col, half = pieces[i]
        out = outs[which]
        if half:
            return [pltpu.make_async_copy(stage.at[slot, :, pl.ds(h * PIECE, PIECE)],
                                          out.at[pl.ds(h * PIECE, PIECE)], out_sem.at[slot, h]) for h in range(2)]
        return [pltpu.make_async_copy(stage.at[slot], out.at[pl.ds(row, PIECE), pl.ds(col, WID)], out_sem.at[slot, 0])]

    n = len(pieces)
    for i in range(min(depth, n)):
        fetch(i).start()
    for i in range(n):
        slot = i % depth
        fetch(i).wait()
        if i >= depth:
            for c in put(i - depth):
                c.wait()

        def body(r, c):
            rows = pl.ds(r * 32, 32)
            stage[slot, rows] = inbuf[slot, rows].astype(jnp.float32)
            return c

        lax.fori_loop(0, PIECE // 32, body, 0)
        for c in put(i):
            c.start()
        if i + depth < n:
            fetch(i + depth).start()
    for i in range(max(0, n - depth), n):
        for c in put(i):
            c.wait()


def widen(summed, row0, d, ff, vf):
    pieces = []
    for j in range(ff // FCH):
        for h in range(2):
            pieces.append((j * 2 * FCH + h * PIECE, 0, j * FCH + h * PIECE, 0, False))
        for h in range(2):
            pieces.append((j * 2 * FCH + FCH + h * PIECE, 1, h * PIECE, j * FCH, False))
    for w in range(3):
        for h in range(2):
            pieces.append((row0 + w * d + h * PIECE, 2 + w, h * PIECE, 0, False))
    pieces.append((row0 + 3 * d, 5, 0, 0, True))
    f32 = jnp.float32
    depth = 3
    hbm = pl.BlockSpec(memory_space=pl.ANY)
    shapes = [(ff, d), (d, ff), (d, d), (d, d), (d, d), (d, vf)]
    return pl.pallas_call(
        functools.partial(widen_kernel, pieces),
        in_specs=[hbm], out_specs=(hbm,) * 6, out_shape=tuple(jax.ShapeDtypeStruct(s, f32) for s in shapes),
        scratch_shapes=[pltpu.VMEM((depth, PIECE, WID), jnp.bfloat16), pltpu.VMEM((depth, PIECE, WID), f32),
                        pltpu.SemaphoreType.DMA((depth,)), pltpu.SemaphoreType.DMA((depth, 2))],
        compiler_params=pltpu.CompilerParams(vmem_limit_bytes=32 * 2**20),
        name="widen",
    )(summed)


def ar_kernel(cfg, part1, part2, small, out, small_z, small_out, acc, recv, gat, sbuf, send_sem, recv_sem, local_sem, ssend, srecv_sem):
    n_dp, n_seq, halves, streams, order = cfg
    dp, sq = lax.axis_index("dp"), lax.axis_index("seq")
    barrier, count = entry_barrier(n_dp, n_seq, dp, sq, False)
    pl.semaphore_wait(barrier, count)
    ex = Exchange(streams, halves, dp, sq, (part1, part2), out, acc, recv, gat, (send_sem, recv_sem, local_sem))
    tiny = Small(n_dp, n_seq, dp, sq, sbuf, ssend, srecv_sem, small_z, small_out)
    for s in range(len(streams)):
        ex.start(s, 0)
    tiny.begin(small[...])
    gap = max(1, len(order) // (len(tiny.dims) + 2))
    for idx, (_, s, k) in enumerate(order):
        ex.step(s, k)
        if idx % gap == gap - 1:
            tiny.step()
    tiny.rest()


def all_reduce(mesh, part1, part2, small, shares, collective_id):
    n_dp, n_seq = mesh.shape["dp"], mesh.shape["seq"]
    halves = (part1.shape[0] // 2, part2.shape[0] // 2)
    streams = plan_streams(n_dp, n_seq, list(zip(halves, shares)), (0.0, 0.0))
    order = schedule(streams)
    n_st = 2 * (bits_of(n_dp) + bits_of(n_seq))
    n_small = bits_of(n_dp) + bits_of(n_seq)
    vmem = pl.BlockSpec(memory_space=pltpu.VMEM)
    hbm = pl.BlockSpec(memory_space=pl.ANY)
    ns = len(streams)
    bf = jnp.bfloat16
    units = lambda n: pltpu.VMEM((n, SUB, WID), bf)
    sshape = jax.ShapeDtypeStruct(small.shape, small.dtype)
    return pl.pallas_call(
        functools.partial(ar_kernel, (n_dp, n_seq, halves, streams, order)),
        out_shape=(jax.ShapeDtypeStruct((2 * sum(halves), SUB, WID), bf), sshape, sshape),
        in_specs=[hbm, hbm, vmem], out_specs=(hbm, vmem, vmem),
        scratch_shapes=[
            units(sum(halves)), units(Exchange.recv_total(streams, halves)), units(sum(halves)),
            pltpu.VMEM((2 * n_small,) + small.shape, small.dtype),
            pltpu.SemaphoreType.DMA((ns, n_st)), pltpu.SemaphoreType.DMA((ns, n_st)), pltpu.SemaphoreType.DMA((ns, 2)),
            pltpu.SemaphoreType.DMA((n_small,)), pltpu.SemaphoreType.DMA((n_small,))],
        compiler_params=pltpu.CompilerParams(collective_id=collective_id, has_side_effects=True, vmem_limit_bytes=60 * 2**20),
        name="grad_all_reduce",
    )(part1, part2, small)


def local(
    mesh,
    hidden_in,
    skip_values,
    out_grad,
    doc_lens,
    valid,
    norm1_gain,
    norm1_shift,
    query_w,
    query_b,
    key_w,
    value_w,
    value_b,
    proj_w,
    proj_b,
    norm2_gain,
    norm2_shift,
    fc_w,
    fc_b,
    out_w,
    out_b,
):
    tok_rows = hidden_in.shape[0]
    seq_size = lax.axis_size("seq")
    seq_rank = lax.axis_index("seq")
    group_rows = tok_rows * seq_size
    heads_here = HEADS // seq_size
    block_rows = min(512, group_rows)
    score_scale = 1.0 / math.sqrt(HDIM)
    head_shape = (group_rows, heads_here, HDIM)
    segments = segment_ids(doc_lens[0], group_rows)
    hidden = hidden_in.astype(jnp.float32)
    normed, norm1_pull = jax.vjp(layer_norm, hidden, norm1_gain, norm1_shift)
    normed_low = normed.astype(jnp.bfloat16)
    fresh_values = (matmul(normed_low, value_w) + value_b).astype(jnp.bfloat16)
    value_rows = jnp.concatenate([fresh_values, skip_values], axis=1)
    query_rows = (matmul(normed_low, query_w) + query_b).astype(jnp.bfloat16)
    key_rows = matmul(normed_low, key_w).astype(jnp.bfloat16)
    query_heads, key_heads, value_heads = (
        lax.all_to_all(query_rows, "seq", split_axis=1, concat_axis=0, tiled=True),
        lax.all_to_all(key_rows, "seq", split_axis=1, concat_axis=0, tiled=True),
        lax.all_to_all(value_rows, "seq", split_axis=1, concat_axis=0, tiled=True),
    )
    query_split = query_heads.reshape(head_shape)
    key_split = key_heads.reshape(head_shape)
    value_split = value_heads.reshape(head_shape)
    mixed_heads, log_totals = attend_forward(
        query_split, key_split, value_split, segments, valid, block_rows, score_scale
    )
    mixed_rows = lax.all_to_all(mixed_heads, "seq", split_axis=0, concat_axis=1, tiled=True)
    valid_col = lax.dynamic_slice_in_dim(valid, seq_rank * tok_rows, tok_rows, 0).astype(jnp.float32)[:, None]
    output, middle_grad, mixed_grad, part, proj_part, small = mlp_block(
        mixed_rows, hidden_in, out_grad, valid_col, proj_w, proj_b, norm2_gain, norm2_shift, fc_w, fc_b, out_w, out_b
    )
    grad_heads = lax.all_to_all(mixed_grad, "seq", split_axis=1, concat_axis=0, tiled=True)
    query_grad, key_grad, value_grad = attend_backward(
        query_split,
        key_split,
        value_split,
        grad_heads.reshape(head_shape),
        log_totals,
        segments,
        valid,
        block_rows,
        score_scale,
    )
    query_grad_rows, key_grad_rows, value_grad_rows = (
        lax.all_to_all(query_grad, "seq", split_axis=0, concat_axis=1, tiled=True),
        lax.all_to_all(key_grad, "seq", split_axis=0, concat_axis=1, tiled=True),
        lax.all_to_all(value_grad, "seq", split_axis=0, concat_axis=1, tiled=True),
    )
    grad_query_w = matmul_left_t(normed_low, query_grad_rows)
    grad_key_w = matmul_left_t(normed_low, key_grad_rows)
    grad_query_b = jnp.sum(query_grad_rows.astype(jnp.float32), axis=0)
    normed_grad = matmul_right_t(query_grad_rows, query_w) + matmul_right_t(key_grad_rows, key_w)
    fresh_grad = value_grad_rows[:, :VFRESH]
    grad_skip = value_grad_rows[:, VFRESH:]
    grad_value_w = matmul_left_t(normed_low, fresh_grad)
    grad_value_b = jnp.sum(fresh_grad.astype(jnp.float32), axis=0)
    normed_grad = normed_grad + matmul_right_t(fresh_grad, value_w)
    hidden_part, grad_norm1_gain, grad_norm1_shift = norm1_pull(normed_grad)
    grad_input = (middle_grad + hidden_part).astype(jnp.bfloat16)
    n_dev = lax.axis_size("dp") * seq_size
    half = D // 2
    value_part = jnp.concatenate([grad_value_w[:half], grad_value_w[half:]], axis=1)
    low = jnp.bfloat16
    part2 = [proj_part, grad_query_w.astype(low), grad_key_w.astype(low), value_part.astype(low)]
    rows = sum(g.shape[0] for g in part2)
    quantum = n_dev * SUB
    padded = -(-rows // quantum) * quantum
    part2 = jnp.concatenate(part2 + [jnp.zeros((padded - rows, WID), low)]).reshape(-1, SUB, WID)
    part1 = part.reshape(-1, SUB, WID)
    head = jnp.stack([grad_norm1_gain, grad_norm1_shift, grad_query_b, jnp.pad(grad_value_b, (0, half))])
    small = small + jnp.pad(head, ((0, 12), (0, 0)))
    summed, small_z, small_all = all_reduce(mesh, part1, part2, small, SHARES, 0)
    row0 = part1.shape[0] * SUB
    grad_out_w, grad_fc_w, grad_proj_w, grad_query_w, grad_key_w, grad_value_w = widen(
        summed.reshape(-1, WID), row0, D, fc_w.shape[1], VFRESH
    )
    grad_norm1_gain, grad_norm1_shift, grad_query_b = small_all[0], small_all[1], small_all[2]
    grad_value_b = small_all[3, :VFRESH]
    grad_proj_b, grad_norm2_gain, grad_norm2_shift, grad_out_b = (small_all[i] for i in (4, 5, 6, 7))
    grad_fc_b = small_all[8:12].reshape(-1)
    sums = small_z[12, :4]
    norm_values = jnp.sqrt(sums[:3] / (sums[3] * D) + square_eps)[None, :]
    return (
        output,
        grad_input,
        grad_skip,
        grad_norm1_gain,
        grad_norm1_shift,
        grad_query_w,
        grad_query_b,
        grad_key_w,
        grad_value_w,
        grad_value_b,
        grad_proj_w,
        grad_proj_b,
        grad_norm2_gain,
        grad_norm2_shift,
        grad_fc_w,
        grad_fc_b,
        grad_out_w,
        grad_out_b,
        norm_values,
    )


def solution(mesh):
    placed = (
        P(("dp", "seq"), None),
        P(("dp", "seq"), None),
        P(("dp", "seq"), None),
        P("dp", None),
        P("dp"),
        P(),
        P(),
        P(),
        P(),
        P(),
        P(),
        P(),
        P(),
        P(),
        P(),
        P(),
        P(),
        P(),
        P(),
        P(),
    )
    return jax.shard_map(
        functools.partial(local, mesh),
        mesh=mesh,
        in_specs=placed,
        out_specs=(
            P(("dp", "seq"), None),
            P(("dp", "seq"), None),
            P(("dp", "seq"), None),
            P(),
            P(),
            P(),
            P(),
            P(),
            P(),
            P(),
            P(),
            P(),
            P(),
            P(),
            P(),
            P(),
            P(),
            P(),
            P("dp", None),
        ),
        check_vma=False,
    )
```

```python
import functools
import math

import jax
import jax.numpy as jnp
from jax import lax
from jax.experimental import pallas as pl
from jax.experimental.pallas import tpu as pltpu
from jax.sharding import PartitionSpec as P

D = 768
HEADS = 12
HDIM = 64
VFRESH = 384


norm_eps = 1e-05
square_eps = 1e-06
tanh_coef = 0.7978845608028654
masked_score = -1e30


MESH = pl.DeviceIdType.MESH
SUB = 16
WID = 768
UNIT_BYTES = SUB * WID * 2
SHARES = ("ababzababzab", "ababab")
STARTS = (3.0, 50.0)
MARKS = (8.0, 13.0, 16.0, 18.0, 19.0, 22.0, 25.0, 27.0, 28.0, 40.0, 50.0)


def bits_of(n):
    return n.bit_length() - 1


def partner(dim, dp, sq):
    kind, j = dim
    step = 1 << j
    if kind == "dp":
        bit = (dp // step) % 2
        return bit, (dp + step - 2 * step * bit, sq)
    bit = (sq // step) % 2
    return bit, (dp, sq + step - 2 * step * bit)


def plan_streams(n_dp, n_seq, phases, starts):
    dpb = [("dp", j) for j in range(1, bits_of(n_dp))]
    sqb = [("seq", j) for j in range(bits_of(n_seq))]
    mid = len(dpb) // 2
    orders = {"a": dpb + sqb, "b": dpb[mid:] + dpb[:mid] + sqb, "z": sqb + dpb}
    quantum = (n_dp // 2) * n_seq
    streams = []
    for phase, (half_units, kinds) in enumerate(phases):
        total = half_units // quantum
        first = used = 0
        for i, kind in enumerate(kinds):
            upto = round(total * (i + 1) / len(kinds))
            n = (upto - used) * quantum
            used = upto
            if n:
                streams.append((phase, first, n, orders[kind], starts[phase]))
                first += n
    return streams


def schedule(streams, busy=()):
    free = {}
    for res, upto in busy:
        free[res] = upto
    out = []
    stages = []
    for phase, first, n, order, start in streams:
        seq = []
        size = n
        seq.append((("dp", 0), size))
        for d in order:
            size //= 2
            seq.append((d, size))
        for d in reversed(order):
            seq.append((d, size))
            size *= 2
        seq.append((("dp", 0), size))
        stages.append(seq)
    at = [0] * len(streams)
    waiting = [(st[4], s) for s, st in enumerate(streams)]
    pending = []

    def launch(s, t):
        d, size = stages[s][at[s]]
        b = size * UNIT_BYTES / 1e6
        if d == ("dp", 0):
            res, dur = "c", b / 0.5
        elif d[0] == "dp":
            res, dur = d, b / 0.045
        else:
            res, dur = "seq", b / 0.045 * (1 << d[1])
        st = max(t, free.get(res, 0.0))
        free[res] = st + dur
        pending.append((st + dur + 2.0, s))

    while pending or waiting:
        pending.sort()
        waiting.sort()
        if waiting and (not pending or waiting[0][0] <= pending[0][0]):
            t, s = waiting.pop(0)
            launch(s, t)
            continue
        t, s = pending.pop(0)
        out.append((t, s, at[s]))
        at[s] += 1
        if at[s] < len(stages[s]):
            launch(s, t + 0.3)
    return out


class Exchange:
    def __init__(self, streams, halves, dp, sq, parts, out, acc, recv, gat, sems):
        self.streams, self.halves = streams, halves
        self.dp, self.sq = dp, sq
        self.parts, self.out, self.acc, self.recv, self.gat = parts, out, acc, recv, gat
        self.send_sem, self.recv_sem, self.local_sem = sems
        self.cbit, self.cdev = partner(("dp", 0), dp, sq)
        self.base = [sum(halves[:p]) for p in range(len(halves))]
        self.off = [[self.base[s[0]] + s[1]] for s in streams]
        self.roff = []
        r = sum(halves)
        for phase, first, n, order, _ in streams:
            rows = [self.base[phase] + first]
            size = n
            for _ in order:
                size //= 2
                rows.append(r)
                r += size
            self.roff.append(rows)

    @staticmethod
    def recv_total(streams, halves):
        r = sum(halves)
        for phase, first, n, order, _ in streams:
            size = n
            for _ in order:
                size //= 2
                r += size
        return r

    def n_stages(self, s):
        return 2 * (len(self.streams[s][3]) + 1)

    def remote(self, s, k, src, dst, dev):
        return pltpu.make_async_remote_copy(
            src_ref=src, dst_ref=dst, send_sem=self.send_sem.at[s, k], recv_sem=self.recv_sem.at[s, k],
            device_id=dev, device_id_type=MESH)

    def copies(self, s, k):
        phase, first, n, order, _ = self.streams[s]
        depth = len(order)
        half_units, base = self.halves[phase], self.base[phase]
        here = base + first
        if k == 0:
            part = self.parts[phase]
            other = (1 - self.cbit) * half_units + first
            mine = self.cbit * half_units + first
            return (self.remote(s, k, part.at[pl.ds(other, n)], self.recv.at[pl.ds(here, n)], self.cdev),
                    pltpu.make_async_copy(part.at[pl.ds(mine, n)], self.acc.at[pl.ds(here, n)], self.local_sem.at[s, 0]))
        if k <= depth:
            half = n >> k
            bit, dev = partner(order[k - 1], self.dp, self.sq)
            at = self.off[s][k - 1]
            return (self.remote(s, k, self.acc.at[pl.ds(at + (1 - bit) * half, half)],
                                self.recv.at[pl.ds(self.roff[s][k], half)], dev), None)
        g = 2 * depth + 1 - k
        if g >= 1:
            half = n >> g
            bit, dev = partner(order[g - 1], self.dp, self.sq)
            piece = self.gat.at[pl.ds(self.off[s][g], half)]
            return (self.remote(s, k, piece, piece, dev), None)
        piece = self.gat.at[pl.ds(here, n)]
        there = self.out.at[pl.ds(2 * base + self.cbit * half_units + first, n)]
        return (self.remote(s, k, piece, there, self.cdev),
                pltpu.make_async_copy(piece, there, self.local_sem.at[s, 1]))

    def start(self, s, k):
        for c in self.copies(s, k):
            if c is not None:
                c.start()

    def finish(self, s, k):
        phase, first, n, order, _ = self.streams[s]
        depth = len(order)
        remote, local = self.copies(s, k)
        remote.wait()
        if local is not None:
            local.wait()
        if k <= depth:
            half = n >> k
            if k == 0:
                off = self.off[s][0]
            else:
                bit, _ = partner(order[k - 1], self.dp, self.sq)
                off = self.off[s][k - 1] + bit * half
                self.off[s].append(off)
            self.add(off, self.roff[s][k], half, self.gat if k == depth else self.acc)

    def add(self, off, roff, n, to):
        acc, recv = self.acc, self.recv
        step = 4 if n % 4 == 0 else (3 if n % 3 == 0 else (2 if n % 2 == 0 else 1))

        def body(i, c):
            a = pl.ds(off + i * step, step)
            b = pl.ds(roff + i * step, step)
            to[a] = acc[a] + recv[b]
            return c

        lax.fori_loop(0, n // step, body, 0)

    def step(self, s, k):
        self.finish(s, k)
        if k + 1 < self.n_stages(s):
            self.start(s, k + 1)


class Small:
    def __init__(self, n_dp, n_seq, dp, sq, buf, ssend, srecv, small_z, small_out):
        self.dims = [("seq", j) for j in range(bits_of(n_seq))] + [("dp", j) for j in range(bits_of(n_dp))]
        self.nz = bits_of(n_seq)
        self.dp, self.sq, self.buf, self.ssend, self.srecv = dp, sq, buf, ssend, srecv
        self.small_z, self.small_out = small_z, small_out
        self.done = 0

    def copy(self, i):
        _, dev = partner(self.dims[i], self.dp, self.sq)
        return pltpu.make_async_remote_copy(
            src_ref=self.buf.at[2 * i], dst_ref=self.buf.at[2 * i + 1], send_sem=self.ssend.at[i],
            recv_sem=self.srecv.at[i], device_id=dev, device_id_type=MESH)

    def begin(self, value):
        self.buf[0] = value
        self.copy(0).start()

    def step(self):
        i = self.done
        if i == len(self.dims):
            return
        self.copy(i).wait()
        total = self.buf[2 * i] + self.buf[2 * i + 1]
        self.done = i + 1
        if self.done == self.nz:
            self.small_z[...] = total
        if self.done < len(self.dims):
            self.buf[2 * self.done] = total
            self.copy(self.done).start()
        else:
            self.small_out[...] = total

    def rest(self):
        while self.done < len(self.dims):
            self.step()


def entry_barrier(n_dp, n_seq, dp, sq, all_seq):
    barrier = pltpu.get_barrier_semaphore()
    peers = [partner(("dp", j), dp, sq)[1] for j in range(bits_of(n_dp))]
    if all_seq:
        peers += [(dp, (sq + d) % n_seq) for d in range(1, n_seq)]
    else:
        peers += [partner(("seq", j), dp, sq)[1] for j in range(bits_of(n_seq))]
    for dev in peers:
        pl.semaphore_signal(barrier, inc=1, device_id=dev, device_id_type=MESH)
    return barrier, len(peers)


def matmul(former, latter):
    return jnp.dot(former, latter, preferred_element_type=jnp.float32)


def matmul_right_t(former, latter):
    return lax.dot_general(
        former, latter, (((1,), (1,)), ((), ())), preferred_element_type=jnp.float32
    )


def matmul_left_t(former, latter):
    return lax.dot_general(
        former, latter, (((0,), (0,)), ((), ())), preferred_element_type=jnp.float32
    )


FCH = 768
GELU_A = 0.044715


def row_sum(v):
    return jnp.sum(v, axis=0, keepdims=True)


def mlp_kernel(steps, mixed, hidden, og, valid, proj_w, proj_b, n2g, n2s, fc_w, fc_b, out_w, out_b,
               output, mid_grad, mixed_grad, part, proj_part, small,
               nt_ref, xhat_ref, inv_ref, mid_ref, mlp_acc, two_acc):
    j = pl.program_id(0)

    @pl.when(j == 0)
    def _():
        x = hidden[...].astype(jnp.float32)
        attn = matmul(mixed[...], proj_w[...]) + proj_b[...]
        middle = x + attn
        mid_ref[...] = middle
        v = valid[...]
        spread = middle - jnp.mean(middle, axis=-1, keepdims=True)
        inv = lax.rsqrt(jnp.mean(spread * spread, axis=-1, keepdims=True) + norm_eps)
        xhat = spread * inv
        xhat_ref[...] = xhat
        inv_ref[...] = jnp.broadcast_to(inv, inv_ref.shape)
        nt_ref[...] = (xhat * n2g[...] + n2s[...]).astype(jnp.bfloat16)
        small[...] = jnp.zeros_like(small)
        s0 = row_sum(jnp.sum(x * x, axis=-1, keepdims=True) * v)
        s1 = row_sum(jnp.sum(attn * attn, axis=-1, keepdims=True) * v)
        s3 = row_sum(v)
        lane = lax.broadcasted_iota(jnp.int32, (1, WID), 1)
        small[12:13, :] = jnp.where(lane == 0, s0, jnp.where(lane == 1, s1, jnp.where(lane == 3, s3, 0.0)))
        small[7:8, :] = row_sum(og[...].astype(jnp.float32))

    nt = nt_ref[...]
    fw = fc_w[...]
    ow = out_w[...]
    g_low = og[...]
    pre = matmul(nt, fw) + fc_b[...]
    sq = pre * pre
    t = jnp.tanh(tanh_coef * (pre + GELU_A * sq * pre))
    act = (0.5 * pre * (1.0 + t)).astype(jnp.bfloat16)
    slope = 0.5 * (1.0 + t) + 0.5 * pre * (1.0 - t * t) * (tanh_coef * (1.0 + 3.0 * GELU_A * sq))
    pre_grad = matmul_right_t(g_low, ow) * slope
    fcb = row_sum(pre_grad)
    for i in range(steps):
        @pl.when(j == i)
        def _():
            small[8 + i : 9 + i, :] = fcb
    low = pre_grad.astype(jnp.bfloat16)
    part[0, 0] = matmul_left_t(act, g_low).astype(jnp.bfloat16)
    part[0, 1] = matmul_left_t(nt, low).astype(jnp.bfloat16)
    mlp = matmul(act, ow)
    two = matmul_right_t(low, fw)

    @pl.when(j == 0)
    def _():
        mlp_acc[...] = mlp
        two_acc[...] = two

    @pl.when(j > 0)
    def _():
        mlp_acc[...] = mlp_acc[...] + mlp
        two_acc[...] = two_acc[...] + two

    @pl.when(j == steps - 1)
    def _():
        mlp_out = mlp_acc[...] + out_b[...]
        output[...] = (mid_ref[...] + mlp_out).astype(jnp.bfloat16)
        s2 = row_sum(jnp.sum(mlp_out * mlp_out, axis=-1, keepdims=True) * valid[...])
        lane = lax.broadcasted_iota(jnp.int32, (1, WID), 1)
        small[12:13, :] = small[12:13, :] + jnp.where(lane == 2, s2, 0.0)
        two_grad = two_acc[...]
        xhat = xhat_ref[...]
        small[5:6, :] = row_sum(two_grad * xhat)
        small[6:7, :] = row_sum(two_grad)
        e = two_grad * n2g[...]
        centre = jnp.mean(e, axis=-1, keepdims=True)
        along = jnp.mean(e * xhat, axis=-1, keepdims=True)
        grad = og[...].astype(jnp.float32) + (e - centre - xhat * along) * inv_ref[:, 0:1]
        mid_grad[...] = grad
        small[4:5, :] = row_sum(grad)
        grad_low = grad.astype(jnp.bfloat16)
        mixed_grad[...] = matmul_right_t(grad_low, proj_w[...]).astype(jnp.bfloat16)
        proj_part[...] = matmul_left_t(mixed[...], grad_low).astype(jnp.bfloat16)


def mlp_block(mixed, hidden, og, valid_col, proj_w, proj_b, n2g, n2s, fc_w, fc_b, out_w, out_b):
    rows, d = hidden.shape
    ff = fc_w.shape[1]
    steps = ff // FCH
    whole = lambda shape: pl.BlockSpec(shape, lambda j: (0,) * len(shape))
    vec = lambda v: v.reshape(1, -1)
    f32, bf = jnp.float32, jnp.bfloat16
    return pl.pallas_call(
        functools.partial(mlp_kernel, steps),
        grid=(steps,),
        in_specs=[whole((rows, d)), whole((rows, d)), whole((rows, d)), whole((rows, 1)), whole((d, d)), whole((1, d)),
                  whole((1, d)), whole((1, d)), pl.BlockSpec((d, FCH), lambda j: (0, j)), pl.BlockSpec((1, FCH), lambda j: (0, j)),
                  pl.BlockSpec((FCH, d), lambda j: (j, 0)), whole((1, d))],
        out_specs=(whole((rows, d)), whole((rows, d)), whole((rows, d)), pl.BlockSpec((1, 2, FCH, d), lambda j: (j, 0, 0, 0)),
                   whole((d, d)), whole((16, d))),
        out_shape=(jax.ShapeDtypeStruct((rows, d), bf), jax.ShapeDtypeStruct((rows, d), f32), jax.ShapeDtypeStruct((rows, d), bf),
                   jax.ShapeDtypeStruct((steps, 2, FCH, d), bf), jax.ShapeDtypeStruct((d, d), bf), jax.ShapeDtypeStruct((16, d), f32)),
        scratch_shapes=[pltpu.VMEM((rows, d), bf), pltpu.VMEM((rows, d), f32), pltpu.VMEM((rows, 128), f32),
                        pltpu.VMEM((rows, d), f32), pltpu.VMEM((rows, d), f32), pltpu.VMEM((rows, d), f32)],
        compiler_params=pltpu.CompilerParams(vmem_limit_bytes=48 * 2**20, dimension_semantics=("arbitrary",)),
        name="mlp_block",
    )(mixed, hidden, og, valid_col, proj_w, vec(proj_b), vec(n2g), vec(n2s), fc_w, vec(fc_b), out_w, vec(out_b))


PIECE = 384


def widen_kernel(pieces, src, *refs):
    n_out = 6
    outs, (inbuf, stage, in_sem, out_sem) = refs[:n_out], refs[n_out:]
    depth = inbuf.shape[0]

    def fetch(i):
        return pltpu.make_async_copy(src.at[pl.ds(pieces[i][0], PIECE)], inbuf.at[i % depth], in_sem.at[i % depth])

    def put(i):
        slot = i % depth
        _, which, row, col, half = pieces[i]
        out = outs[which]
        if half:
            return [pltpu.make_async_copy(stage.at[slot, :, pl.ds(h * PIECE, PIECE)],
                                          out.at[pl.ds(h * PIECE, PIECE)], out_sem.at[slot, h]) for h in range(2)]
        return [pltpu.make_async_copy(stage.at[slot], out.at[pl.ds(row, PIECE), pl.ds(col, WID)], out_sem.at[slot, 0])]

    n = len(pieces)
    for i in range(min(depth, n)):
        fetch(i).start()
    for i in range(n):
        slot = i % depth
        fetch(i).wait()
        if i >= depth:
            for c in put(i - depth):
                c.wait()

        def body(r, c):
            rows = pl.ds(r * 32, 32)
            stage[slot, rows] = inbuf[slot, rows].astype(jnp.float32)
            return c

        lax.fori_loop(0, PIECE // 32, body, 0)
        for c in put(i):
            c.start()
        if i + depth < n:
            fetch(i + depth).start()
    for i in range(max(0, n - depth), n):
        for c in put(i):
            c.wait()


def widen(summed, row0, d, ff, vf):
    pieces = []
    for j in range(ff // FCH):
        for h in range(2):
            pieces.append((j * 2 * FCH + h * PIECE, 0, j * FCH + h * PIECE, 0, False))
        for h in range(2):
            pieces.append((j * 2 * FCH + FCH + h * PIECE, 1, h * PIECE, j * FCH, False))
    for w in range(3):
        for h in range(2):
            pieces.append((row0 + w * d + h * PIECE, 2 + w, h * PIECE, 0, False))
    pieces.append((row0 + 3 * d, 5, 0, 0, True))
    f32 = jnp.float32
    depth = 3
    hbm = pl.BlockSpec(memory_space=pl.ANY)
    shapes = [(ff, d), (d, ff), (d, d), (d, d), (d, d), (d, vf)]
    return pl.pallas_call(
        functools.partial(widen_kernel, pieces),
        in_specs=[hbm], out_specs=(hbm,) * 6, out_shape=tuple(jax.ShapeDtypeStruct(s, f32) for s in shapes),
        scratch_shapes=[pltpu.VMEM((depth, PIECE, WID), jnp.bfloat16), pltpu.VMEM((depth, PIECE, WID), f32),
                        pltpu.SemaphoreType.DMA((depth,)), pltpu.SemaphoreType.DMA((depth, 2))],
        compiler_params=pltpu.CompilerParams(vmem_limit_bytes=32 * 2**20),
        name="widen",
    )(summed)


LANES = 128
PAIR_TILE = (0, 2, 3, 5)
THIRD_TILE = (1, 1, 4, 4)


def low_lanes():
    return lax.broadcasted_iota(jnp.int32, (1, LANES), 1) < HDIM


def turn(v):
    return pltpu.roll(v, HDIM, 1)


def pack_third(first, second, upper):
    first, second = first.astype(jnp.float32), second.astype(jnp.float32)
    if upper:
        both = jnp.where(low_lanes(), turn(first), second)
    else:
        both = jnp.where(low_lanes(), first, turn(second))
    return both.astype(jnp.bfloat16)


def unpack_third(both):
    wide = both.astype(jnp.float32)
    low = low_lanes()
    first = jnp.where(low, wide, 0.0).astype(jnp.bfloat16)
    second = jnp.where(low, turn(wide), 0.0).astype(jnp.bfloat16)
    return first, second


def join_thirds(one, two):
    one, two = one.astype(jnp.float32), two.astype(jnp.float32)
    low = low_lanes()
    first = jnp.where(low, one, turn(two)).astype(jnp.bfloat16)
    second = jnp.where(low, turn(one), two).astype(jnp.bfloat16)
    return first, second


def split_tiles(tiles, pair_dst, third_dst, rows, n_seq):
    half = rows // 2
    for r in range(n_seq):
        pair_dst(r, tiles[PAIR_TILE[r]])
        t = tiles[THIRD_TILE[r]]
        third_dst(r, pack_third(t[:half], t[half:], r % 2))


def mask_bias(lens, valid_row, first, rows, cols):
    one = lens[0, 0]
    two = one + lens[0, 1]
    i = first + lax.broadcasted_iota(jnp.int32, (rows, 1), 0)
    j = lax.broadcasted_iota(jnp.int32, (1, cols), 1)
    seg_i = (i >= one).astype(jnp.int32) + (i >= two).astype(jnp.int32)
    seg_j = (j >= one).astype(jnp.int32) + (j >= two).astype(jnp.int32)
    real = valid_row[:, 0:cols] > 0
    code = jnp.where(real, seg_j, -1)
    same = (code == seg_i) & (j <= i)
    return jnp.where(same | (i == j), 0.0, masked_score)


class Swap:
    def __init__(self, n_seq, dp, sq, send, recv, ssem, rsem):
        self.n_seq, self.dp, self.sq = n_seq, dp, sq
        self.send, self.recv, self.ssem, self.rsem = send, recv, ssem, rsem

    def copy(self, d):
        to = (self.sq + d) % self.n_seq
        return pltpu.make_async_remote_copy(
            src_ref=self.send(to), dst_ref=self.recv(self.sq), send_sem=self.ssem(d), recv_sem=self.rsem(d),
            device_id=(self.dp, to), device_id_type=MESH)

    def start(self):
        for d in range(1, self.n_seq):
            self.copy(d).start()

    def wait(self):
        for d in range(1, self.n_seq):
            self.copy(d).wait()


class Gather:
    def __init__(self, n_seq, dp, sq, send, recv, ssem, rsem):
        self.n_seq, self.dp, self.sq = n_seq, dp, sq
        self.send, self.recv, self.ssem, self.rsem = send, recv, ssem, rsem

    def copy(self, to, slot):
        return pltpu.make_async_remote_copy(
            src_ref=self.send(to), dst_ref=self.recv(slot), send_sem=self.ssem(to), recv_sem=self.rsem(slot),
            device_id=(self.dp, to), device_id_type=MESH)

    def start(self, to):
        @pl.when(self.sq != to)
        def _():
            self.copy(to, self.sq).start()

    def wait(self):
        for i in range(self.n_seq):
            @pl.when(self.sq != i)
            def _():
                self.copy(i, i).wait()


def front_kernel(cfg, lens, hidden, skip, valid_row, n1g, n1s, qw, qb, kw, vw, vb,
                 normed_out, mixed_out, pair_out, third_out, lse_out,
                 sp, st, rp, rt, smp, smt, rmp, rmt, bias, ssem, rsem, mssem, mrsem):
    n_dp, n_seq = cfg
    dp, sq = lax.axis_index("dp"), lax.axis_index("seq")
    rows = hidden.shape[0]
    half = rows // 2
    barrier = pltpu.get_barrier_semaphore()
    for d in range(1, n_seq):
        pl.semaphore_signal(barrier, inc=1, device_id=(dp, (sq + d) % n_seq), device_id_type=MESH)
    x = hidden[...].astype(jnp.float32)
    spread = x - jnp.mean(x, axis=-1, keepdims=True)
    inv = lax.rsqrt(jnp.mean(spread * spread, axis=-1, keepdims=True) + norm_eps)
    normed = (spread * inv * n1g[...] + n1s[...]).astype(jnp.bfloat16)
    normed_out[...] = normed
    swaps = [[Swap(n_seq, dp, sq, lambda to, t=t: sp.at[to, t], lambda me, t=t: rp.at[t, pl.ds(me * rows, rows)],
                   lambda d, t=t: ssem.at[0, t, d], lambda d, t=t: rsem.at[0, t, d]),
              Swap(n_seq, dp, sq, lambda to, t=t: st.at[to, t], lambda me, t=t: rt.at[t, me],
                   lambda d, t=t: ssem.at[1, t, d], lambda d, t=t: rsem.at[1, t, d])] for t in range(3)]
    first = True
    for t in range(3):
        if t == 0:
            full = (matmul(normed, qw[...]) + qb[...]).astype(jnp.bfloat16)
        elif t == 1:
            full = matmul(normed, kw[...]).astype(jnp.bfloat16)
        else:
            full = (matmul(normed, vw[...]) + vb[...]).astype(jnp.bfloat16)
        tiles = [full[:, c * LANES : (c + 1) * LANES] for c in range(full.shape[1] // LANES)]
        if t == 2:
            tiles += [skip[:, c * LANES : (c + 1) * LANES] for c in range(skip.shape[1] // LANES)]

        def pair_dst(r, v):
            sp[r, t] = v

        def third_dst(r, v):
            st[r, t] = v

        split_tiles(tiles, pair_dst, third_dst, rows, n_seq)
        if first:
            pl.semaphore_wait(barrier, n_seq - 1)
            first = False
        swaps[t][0].start()
    for t in range(3):
        swaps[t][1].start()
        rp[t, pl.ds(pl.multiple_of(sq * rows, rows), rows)] = sp[sq, t]
        rt[t, sq] = st[sq, t]
    for i in range(n_seq):
        cols = (i + 1) * rows
        bias[i * rows : (i + 1) * rows, 0:cols] = mask_bias(lens, valid_row, i * rows, rows, cols)
    back = [Gather(n_seq, dp, sq, lambda to: smp.at[to], lambda s: rmp.at[s], lambda i: mssem.at[0, i], lambda i: mrsem.at[0, i]),
            Gather(n_seq, dp, sq, lambda to: smt.at[to], lambda s: rmt.at[s], lambda i: mssem.at[1, i], lambda i: mrsem.at[1, i])]
    low = low_lanes()
    scale = 1.0 / math.sqrt(HDIM)
    keep = (jnp.where(low, scale, 0.0).astype(jnp.bfloat16), jnp.where(low, 0.0, scale).astype(jnp.bfloat16))

    def attend(q, k, v, block):
        scores = matmul_right_t(q, k) + block
        top = jnp.max(scores, axis=-1, keepdims=True)
        powered = jnp.exp(scores - top)
        total = jnp.sum(powered, axis=-1, keepdims=True)
        probs = (powered * (1.0 / total)).astype(jnp.bfloat16)
        return matmul(probs, v), top + jnp.log(total)

    for t in range(3):
        swaps[t][0].wait()
    lane = lax.broadcasted_iota(jnp.int32, (1, LANES), 1)
    for i in range(n_seq):
        here = slice(i * rows, (i + 1) * rows)
        cols = (i + 1) * rows
        block = bias[here, 0:cols]
        q, k, v = rp[0, here], rp[1, 0:cols], rp[2, 0:cols]
        o0, l0 = attend(q * keep[0], k, v, block)
        o1, l1 = attend(q * keep[1], k, v, block)
        smp[i] = jnp.where(low, o0, o1).astype(jnp.bfloat16)
        lse_out[here] = jnp.where(lane == 0, l0, l1)
        back[0].start(i)
    for t in range(3):
        swaps[t][1].wait()
        for s in range(n_seq):
            a, b = unpack_third(rt[t, s])
            third_out[t, s * rows : s * rows + half] = a
            third_out[t, s * rows + half : (s + 1) * rows] = b
    for i in range(n_seq):
        here = slice(i * rows, (i + 1) * rows)
        cols = (i + 1) * rows
        block = bias[here, 0:cols]
        o2, l2 = attend(third_out[0, here] * keep[0], third_out[1, 0:cols], third_out[2, 0:cols], block)
        smt[i] = pack_third(o2[:half], o2[half:], False)
        lse_out[here] = jnp.where(lane == 2, l2, lse_out[here])
        back[1].start(i)
    pair_out[...] = rp[...]
    rmp[sq] = smp[sq]
    rmt[sq] = smt[sq]
    back[0].wait()
    back[1].wait()
    for r in range(n_seq):
        c = PAIR_TILE[r] * LANES
        mixed_out[:, c : c + LANES] = rmp[r]
    for r in range(0, n_seq, 2):
        a, b = join_thirds(rmt[r], rmt[r + 1])
        c = THIRD_TILE[r] * LANES
        mixed_out[0:half, c : c + LANES] = a
        mixed_out[half:rows, c : c + LANES] = b


def front(mesh, hidden, skip, lens, valid, n1g, n1s, qw, qb, kw, vw, vb, collective_id):
    n_dp, n_seq = mesh.shape["dp"], mesh.shape["seq"]
    rows, d = hidden.shape
    group = rows * n_seq
    bf, f32 = jnp.bfloat16, jnp.float32
    vec = lambda v: v.reshape(1, -1)
    vmem = pl.BlockSpec(memory_space=pltpu.VMEM)
    half = rows // 2
    dma = pltpu.SemaphoreType.DMA
    return pl.pallas_call(
        functools.partial(front_kernel, (n_dp, n_seq)),
        in_specs=[pl.BlockSpec(memory_space=pltpu.SMEM)] + [vmem] * 10,
        out_specs=(vmem,) * 5,
        out_shape=(jax.ShapeDtypeStruct((rows, d), bf), jax.ShapeDtypeStruct((rows, d), bf),
                   jax.ShapeDtypeStruct((3, group, LANES), bf), jax.ShapeDtypeStruct((3, group, LANES), bf),
                   jax.ShapeDtypeStruct((group, LANES), f32)),
        scratch_shapes=[
            pltpu.VMEM((n_seq, 3, rows, LANES), bf), pltpu.VMEM((n_seq, 3, half, LANES), bf),
            pltpu.VMEM((3, group, LANES), bf), pltpu.VMEM((3, n_seq, half, LANES), bf),
            pltpu.VMEM((n_seq, rows, LANES), bf), pltpu.VMEM((n_seq, half, LANES), bf),
            pltpu.VMEM((n_seq, rows, LANES), bf), pltpu.VMEM((n_seq, half, LANES), bf),
            pltpu.VMEM((group, group), f32),
            dma((2, 3, n_seq)), dma((2, 3, n_seq)), dma((2, n_seq)), dma((2, n_seq))],
        compiler_params=pltpu.CompilerParams(collective_id=collective_id, has_side_effects=True, vmem_limit_bytes=56 * 2**20),
        name="front",
    )(lens, hidden, skip, vec(valid), vec(n1g), vec(n1s), qw, vec(qb), kw, vw, vec(vb))


def back_kernel(cfg, lens, valid_row, mixed_grad, pair, third, lse, normed, hidden, n1g, mid_grad, qw, kw, vw, proj_part, small, part1,
                out, grad_input, grad_skip, small_z, small_out,
                gs, gst, gp, gt, gthird, bias, dk_acc, dv_acc, dsp, dst, drp, drt, rows_in, part2,
                acc, recv, gat, sbuf, gssem, grsem, dssem, drsem, send_sem, recv_sem, local_sem, ssend, srecv_sem):
    n_dp, n_seq, halves, streams, order, marks = cfg
    dp, sq = lax.axis_index("dp"), lax.axis_index("seq")
    rows, d = hidden.shape
    half = rows // 2
    bf, f32 = jnp.bfloat16, jnp.float32
    barrier, count = entry_barrier(n_dp, n_seq, dp, sq, True)
    full = mixed_grad[...]
    tiles = [full[:, c * LANES : (c + 1) * LANES] for c in range(d // LANES)]

    def pair_dst(r, v):
        gs[r] = v

    def third_dst(r, v):
        gst[r] = v

    split_tiles(tiles, pair_dst, third_dst, rows, n_seq)
    pl.semaphore_wait(barrier, count)
    swap_pair = Swap(n_seq, dp, sq, lambda to: gs.at[to], lambda me: gp.at[pl.ds(me * rows, rows)], lambda i: gssem.at[0, i], lambda i: grsem.at[0, i])
    swap_third = Swap(n_seq, dp, sq, lambda to: gst.at[to], lambda me: gt.at[me], lambda i: gssem.at[1, i], lambda i: grsem.at[1, i])
    swap_pair.start()
    swap_third.start()
    ex = Exchange(streams, halves, dp, sq, (part1, part2), out, acc, recv, gat, (send_sem, recv_sem, local_sem))
    tiny = Small(n_dp, n_seq, dp, sq, sbuf, ssend, srecv_sem, small_z, small_out)
    for s, st in enumerate(streams):
        if st[0] == 0:
            ex.start(s, 0)
    todo = list(order)

    def advance(upto):
        while todo and todo[0][0] <= upto:
            _, s, k = todo.pop(0)
            ex.step(s, k)

    gp[pl.ds(pl.multiple_of(sq * rows, rows), rows)] = gs[sq]
    gt[sq] = gst[sq]
    for i in range(n_seq):
        cols = (i + 1) * rows
        bias[i * rows : (i + 1) * rows, 0:cols] = mask_bias(lens, valid_row, i * rows, rows, cols)
    units_d = d // SUB
    part2[0:units_d] = proj_part[...].reshape(units_d, SUB, WID)
    send = [Gather(n_seq, dp, sq, lambda to: dsp.at[to], lambda s: drp.at[s], lambda i: dssem.at[0, i], lambda i: drsem.at[0, i]),
            Gather(n_seq, dp, sq, lambda to: dst.at[to], lambda s: drt.at[s], lambda i: dssem.at[1, i], lambda i: drsem.at[1, i])]
    low = low_lanes()
    scale = 1.0 / math.sqrt(HDIM)
    keep = (jnp.where(low, scale, 0.0).astype(bf), jnp.where(low, 0.0, scale).astype(bf))
    ones = (jnp.where(low, 1.0, 0.0).astype(bf), jnp.where(low, 0.0, 1.0).astype(bf))

    def backward(q, k, v, g, block, total):
        probs = jnp.exp(matmul_right_t(q, k) + block - total)
        prob_grad = matmul_right_t(g, v)
        centre = jnp.sum(probs * prob_grad, axis=-1, keepdims=True)
        score_grad = (probs * (prob_grad - centre)).astype(bf)
        return matmul(score_grad, k), matmul_left_t(score_grad, q), matmul_left_t(probs.astype(bf), g)

    mark = iter(marks)
    advance(next(mark))
    swap_pair.wait()
    for i in reversed(range(n_seq)):
        here = slice(i * rows, (i + 1) * rows)
        cols = (i + 1) * rows
        block = bias[here, 0:cols]
        q, k, v, g = pair[0, here], pair[1, 0:cols], pair[2, 0:cols], gp[here]
        dq0, dk0, dv0 = backward(q * keep[0], k, v, g * ones[0], block, lse[here, 0:1])
        dq1, dk1, dv1 = backward(q * keep[1], k, v, g * ones[1], block, lse[here, 1:2])
        if i == n_seq - 1:
            dk_acc[...] = dk0 + dk1
            dv_acc[...] = dv0 + dv1
        else:
            dk_acc[0:cols] = dk_acc[0:cols] + (dk0 + dk1)
            dv_acc[0:cols] = dv_acc[0:cols] + (dv0 + dv1)
        dsp[i, 0] = (jnp.where(low, dq0, dq1) * scale).astype(bf)
        dsp[i, 1] = dk_acc[here].astype(bf)
        dsp[i, 2] = dv_acc[here].astype(bf)
        send[0].start(i)
        advance(next(mark))
    swap_third.wait()
    for s in range(n_seq):
        a, b = unpack_third(gt[s])
        gthird[s * rows : s * rows + half] = a
        gthird[s * rows + half : (s + 1) * rows] = b
    for i in reversed(range(n_seq)):
        here = slice(i * rows, (i + 1) * rows)
        cols = (i + 1) * rows
        block = bias[here, 0:cols]
        dq, dk, dv = backward(third[0, here] * keep[0], third[1, 0:cols], third[2, 0:cols], gthird[here], block, lse[here, 2:3])
        if i == n_seq - 1:
            dk_acc[...] = dk
            dv_acc[...] = dv
        else:
            dk_acc[0:cols] = dk_acc[0:cols] + dk
            dv_acc[0:cols] = dv_acc[0:cols] + dv
        dq = dq * scale
        dst[i, 0] = pack_third(dq[:half], dq[half:], False)
        for t, a in ((1, dk_acc), (2, dv_acc)):
            dst[i, t] = pack_third(a[i * rows : i * rows + half], a[i * rows + half : (i + 1) * rows], False)
        send[1].start(i)
        advance(next(mark))
    drp[sq] = dsp[sq]
    drt[sq] = dst[sq]
    x = hidden[...].astype(f32)
    spread = x - jnp.mean(x, axis=-1, keepdims=True)
    inv = lax.rsqrt(jnp.mean(spread * spread, axis=-1, keepdims=True) + norm_eps)
    xhat = spread * inv
    send[0].wait()
    advance(next(mark))
    send[1].wait()
    for t in range(3):
        for r in range(n_seq):
            c = PAIR_TILE[r] * LANES
            rows_in[t, :, c : c + LANES] = drp[r, t]
        for r in range(0, n_seq, 2):
            a, b = join_thirds(drt[r, t], drt[r + 1, t])
            c = THIRD_TILE[r] * LANES
            rows_in[t, 0:half, c : c + LANES] = a
            rows_in[t, half:rows, c : c + LANES] = b
    nl = normed[...]
    dq, dk, dv = rows_in[0], rows_in[1], rows_in[2]
    fresh = dv[:, 0:VFRESH]
    grad_skip[...] = dv[:, VFRESH:]
    part2[units_d : 2 * units_d] = matmul_left_t(nl, dq).astype(bf).reshape(units_d, SUB, WID)
    part2[2 * units_d : 3 * units_d] = matmul_left_t(nl, dk).astype(bf).reshape(units_d, SUB, WID)
    gv = matmul_left_t(nl, fresh).astype(bf)
    uv = d // 2 // SUB
    part2[3 * units_d : 3 * units_d + uv, :, 0:VFRESH] = gv[: d // 2].reshape(uv, SUB, VFRESH)
    part2[3 * units_d : 3 * units_d + uv, :, VFRESH:] = gv[d // 2 :].reshape(uv, SUB, VFRESH)
    extra = 2 * halves[1] - 3 * units_d - uv
    if extra:
        part2[3 * units_d + uv :] = jnp.zeros((extra, SUB, WID), bf)
    for s, st in enumerate(streams):
        if st[0] == 1:
            ex.start(s, 0)
    advance(next(mark))
    normed_grad = matmul_right_t(dq, qw[...]) + matmul_right_t(dk, kw[...]) + matmul_right_t(fresh, vw[...])
    f = normed_grad * n1g[...]
    centre = jnp.mean(f, axis=-1, keepdims=True)
    along = jnp.mean(f * xhat, axis=-1, keepdims=True)
    grad_input[...] = (mid_grad[...] + (f - centre - xhat * along) * inv).astype(bf)
    sbuf[0] = small[...]
    sbuf[0, 0:1] = row_sum(normed_grad * xhat)
    sbuf[0, 1:2] = row_sum(normed_grad)
    sbuf[0, 2:3] = row_sum(dq.astype(f32))
    sbuf[0, 3:4, 0:VFRESH] = row_sum(fresh.astype(f32))
    tiny.copy(0).start()
    gap = max(1, len(todo) // (len(tiny.dims) + 2))
    left = 0
    while todo:
        _, s, k = todo.pop(0)
        ex.step(s, k)
        left += 1
        if left % gap == 0:
            tiny.step()
    tiny.rest()


def back(mesh, lens, valid, mixed_grad, pair, third, lse, normed, hidden, n1g, mid_grad, qw, kw, vw, proj_part, small, part1, collective_id):
    n_dp, n_seq = mesh.shape["dp"], mesh.shape["seq"]
    rows, d = hidden.shape
    group = rows * n_seq
    half = rows // 2
    bf, f32 = jnp.bfloat16, jnp.float32
    quantum = n_dp * n_seq
    rows2 = 3 * d + d // 2
    units2 = -(-rows2 // SUB // quantum) * quantum
    halves = (part1.shape[0] // 2, units2 // 2)
    streams = plan_streams(n_dp, n_seq, list(zip(halves, SHARES)), STARTS)
    order = schedule(streams, (("seq", 9.0),))
    n_st = 2 * (bits_of(n_dp) + bits_of(n_seq))
    n_small = bits_of(n_dp) + bits_of(n_seq)
    ns = len(streams)
    vmem = pl.BlockSpec(memory_space=pltpu.VMEM)
    hbm = pl.BlockSpec(memory_space=pl.ANY)
    dma = pltpu.SemaphoreType.DMA
    units = lambda n: pltpu.VMEM((n, SUB, WID), bf)
    sshape = jax.ShapeDtypeStruct(small.shape, f32)
    return pl.pallas_call(
        functools.partial(back_kernel, (n_dp, n_seq, halves, streams, order, MARKS)),
        in_specs=[pl.BlockSpec(memory_space=pltpu.SMEM)] + [vmem] * 14 + [hbm],
        out_specs=(hbm, vmem, vmem, vmem, vmem),
        out_shape=(jax.ShapeDtypeStruct((2 * sum(halves), SUB, WID), bf), jax.ShapeDtypeStruct((rows, d), bf),
                   jax.ShapeDtypeStruct((rows, d - VFRESH), bf), sshape, sshape),
        scratch_shapes=[
            pltpu.VMEM((n_seq, rows, LANES), bf), pltpu.VMEM((n_seq, half, LANES), bf),
            pltpu.VMEM((group, LANES), bf), pltpu.VMEM((n_seq, half, LANES), bf), pltpu.VMEM((group, LANES), bf),
            pltpu.VMEM((group, group), f32), pltpu.VMEM((group, LANES), f32), pltpu.VMEM((group, LANES), f32),
            pltpu.VMEM((n_seq, 3, rows, LANES), bf), pltpu.VMEM((n_seq, 3, half, LANES), bf),
            pltpu.VMEM((n_seq, 3, rows, LANES), bf), pltpu.VMEM((n_seq, 3, half, LANES), bf),
            pltpu.VMEM((3, rows, d), bf), units(units2),
            units(sum(halves)), units(Exchange.recv_total(streams, halves)), units(sum(halves)),
            pltpu.VMEM((2 * n_small,) + small.shape, f32),
            dma((2, n_seq)), dma((2, n_seq)), dma((2, n_seq)), dma((2, n_seq)),
            dma((ns, n_st)), dma((ns, n_st)), dma((ns, 2)), dma((n_small,)), dma((n_small,))],
        compiler_params=pltpu.CompilerParams(collective_id=collective_id, has_side_effects=True, vmem_limit_bytes=63 * 2**20),
        name="back",
    )(lens, valid.reshape(1, -1), mixed_grad, pair, third, lse, normed, hidden, n1g.reshape(1, -1), mid_grad, qw, kw, vw, proj_part,
      small, part1)


def local(
    mesh,
    hidden_in,
    skip_values,
    out_grad,
    doc_lens,
    valid,
    norm1_gain,
    norm1_shift,
    query_w,
    query_b,
    key_w,
    value_w,
    value_b,
    proj_w,
    proj_b,
    norm2_gain,
    norm2_shift,
    fc_w,
    fc_b,
    out_w,
    out_b,
):
    seq_size = lax.axis_size("seq")
    seq_rank = lax.axis_index("seq")
    tok_rows = hidden_in.shape[0]
    valid_col = lax.dynamic_slice_in_dim(valid, seq_rank * tok_rows, tok_rows, 0).astype(jnp.float32)[:, None]
    normed, mixed, pair, third, lse = front(
        mesh, hidden_in, skip_values, doc_lens, valid, norm1_gain, norm1_shift, query_w, query_b, key_w, value_w, value_b, 0
    )
    output, middle_grad, mixed_grad, part, proj_part, small = mlp_block(
        mixed, hidden_in, out_grad, valid_col, proj_w, proj_b, norm2_gain, norm2_shift, fc_w, fc_b, out_w, out_b
    )
    part1 = part.reshape(-1, SUB, WID)
    summed, grad_input, grad_skip, small_z, small_all = back(
        mesh, doc_lens, valid, mixed_grad, pair, third, lse, normed, hidden_in, norm1_gain, middle_grad,
        query_w, key_w, value_w, proj_part, small, part1, 1
    )
    row0 = part1.shape[0] * SUB
    grad_out_w, grad_fc_w, grad_proj_w, grad_query_w, grad_key_w, grad_value_w = widen(
        summed.reshape(-1, WID), row0, D, fc_w.shape[1], VFRESH
    )
    grad_norm1_gain, grad_norm1_shift, grad_query_b = small_all[0], small_all[1], small_all[2]
    grad_value_b = small_all[3, :VFRESH]
    grad_proj_b, grad_norm2_gain, grad_norm2_shift, grad_out_b = (small_all[i] for i in (4, 5, 6, 7))
    grad_fc_b = small_all[8:12].reshape(-1)
    sums = small_z[12, :4]
    norm_values = jnp.sqrt(sums[:3] / (sums[3] * D) + square_eps)[None, :]
    return (
        output,
        grad_input,
        grad_skip,
        grad_norm1_gain,
        grad_norm1_shift,
        grad_query_w,
        grad_query_b,
        grad_key_w,
        grad_value_w,
        grad_value_b,
        grad_proj_w,
        grad_proj_b,
        grad_norm2_gain,
        grad_norm2_shift,
        grad_fc_w,
        grad_fc_b,
        grad_out_w,
        grad_out_b,
        norm_values,
    )


def solution(mesh):
    placed = (
        P(("dp", "seq"), None),
        P(("dp", "seq"), None),
        P(("dp", "seq"), None),
        P("dp", None),
        P("dp"),
        P(),
        P(),
        P(),
        P(),
        P(),
        P(),
        P(),
        P(),
        P(),
        P(),
        P(),
        P(),
        P(),
        P(),
        P(),
    )
    return jax.shard_map(
        functools.partial(local, mesh),
        mesh=mesh,
        in_specs=placed,
        out_specs=(
            P(("dp", "seq"), None),
            P(("dp", "seq"), None),
            P(("dp", "seq"), None),
            P(),
            P(),
            P(),
            P(),
            P(),
            P(),
            P(),
            P(),
            P(),
            P(),
            P(),
            P(),
            P(),
            P(),
            P(),
            P("dp", None),
        ),
        check_vma=False,
    )
```

```python
import functools
import math

import jax
import jax.numpy as jnp
from jax import lax
from jax.experimental import pallas as pl
from jax.experimental.pallas import tpu as pltpu
from jax.sharding import PartitionSpec as P

D = 768
HEADS = 12
HDIM = 64
VFRESH = 384


norm_eps = 1e-05
square_eps = 1e-06
tanh_coef = 0.7978845608028654
masked_score = -1e30


MESH = pl.DeviceIdType.MESH
SUB = 16
WID = 768
UNIT_BYTES = SUB * WID * 2
SHARES = ("abababababab", "ababab")
STARTS = (3.0, 50.0)
MARKS = (8.0, 13.0, 16.0, 18.0, 19.0, 22.0, 25.0, 27.0, 28.0, 40.0, 50.0)


def bits_of(n):
    return n.bit_length() - 1


def partner(dim, dp, sq):
    kind, j = dim
    step = 1 << j
    if kind == "dp":
        bit = (dp // step) % 2
        return bit, (dp + step - 2 * step * bit, sq)
    bit = (sq // step) % 2
    return bit, (dp, sq + step - 2 * step * bit)


def plan_streams(n_dp, n_seq, phases, starts):
    dpb = [("dp", j) for j in range(1, bits_of(n_dp))]
    sqb = [("seq", j) for j in range(bits_of(n_seq))]
    mid = len(dpb) // 2
    orders = {"a": dpb + sqb, "b": dpb[mid:] + dpb[:mid] + sqb, "z": sqb + dpb}
    quantum = (n_dp // 2) * n_seq
    streams = []
    for phase, (half_units, kinds) in enumerate(phases):
        total = half_units // quantum
        first = used = 0
        for i, kind in enumerate(kinds):
            upto = round(total * (i + 1) / len(kinds))
            n = (upto - used) * quantum
            used = upto
            if n:
                streams.append((phase, first, n, orders[kind], starts[phase]))
                first += n
    return streams


def schedule(streams, busy=()):
    free = {}
    for res, upto in busy:
        free[res] = upto
    out = []
    stages = []
    for phase, first, n, order, start in streams:
        seq = []
        size = n
        seq.append((("dp", 0), size))
        for d in order:
            size //= 2
            seq.append((d, size))
        for d in reversed(order):
            seq.append((d, size))
            size *= 2
        seq.append((("dp", 0), size))
        stages.append(seq)
    at = [0] * len(streams)
    waiting = [(st[4], s) for s, st in enumerate(streams)]
    pending = []

    def launch(s, t):
        d, size = stages[s][at[s]]
        b = size * UNIT_BYTES / 1e6
        if d == ("dp", 0):
            res, dur = "c", b / 0.5
        elif d[0] == "dp":
            res, dur = d, b / 0.045
        else:
            res, dur = "seq", b / 0.045 * (1 << d[1])
        st = max(t, free.get(res, 0.0))
        free[res] = st + dur
        pending.append((st + dur + 2.0, s))

    while pending or waiting:
        pending.sort()
        waiting.sort()
        if waiting and (not pending or waiting[0][0] <= pending[0][0]):
            t, s = waiting.pop(0)
            launch(s, t)
            continue
        t, s = pending.pop(0)
        out.append((t, s, at[s]))
        at[s] += 1
        if at[s] < len(stages[s]):
            launch(s, t + 0.3)
    return out


class Exchange:
    def __init__(self, streams, halves, dp, sq, parts, out, acc, recv, gat, sems):
        self.streams, self.halves = streams, halves
        self.dp, self.sq = dp, sq
        self.parts, self.out, self.acc, self.recv, self.gat = parts, out, acc, recv, gat
        self.send_sem, self.recv_sem, self.local_sem = sems
        self.cbit, self.cdev = partner(("dp", 0), dp, sq)
        self.base = [sum(halves[:p]) for p in range(len(halves))]
        self.off = [[self.base[s[0]] + s[1]] for s in streams]
        self.roff = []
        r = sum(halves)
        for phase, first, n, order, _ in streams:
            rows = [self.base[phase] + first]
            size = n
            for _ in order:
                size //= 2
                rows.append(r)
                r += size
            self.roff.append(rows)

    @staticmethod
    def recv_total(streams, halves):
        r = sum(halves)
        for phase, first, n, order, _ in streams:
            size = n
            for _ in order:
                size //= 2
                r += size
        return r

    def n_stages(self, s):
        return 2 * (len(self.streams[s][3]) + 1)

    def remote(self, s, k, src, dst, dev):
        return pltpu.make_async_remote_copy(
            src_ref=src, dst_ref=dst, send_sem=self.send_sem.at[s, k], recv_sem=self.recv_sem.at[s, k],
            device_id=dev, device_id_type=MESH)

    def copies(self, s, k):
        phase, first, n, order, _ = self.streams[s]
        depth = len(order)
        half_units, base = self.halves[phase], self.base[phase]
        here = base + first
        if k == 0:
            part = self.parts[phase]
            other = (1 - self.cbit) * half_units + first
            mine = self.cbit * half_units + first
            return (self.remote(s, k, part.at[pl.ds(other, n)], self.recv.at[pl.ds(here, n)], self.cdev),
                    pltpu.make_async_copy(part.at[pl.ds(mine, n)], self.acc.at[pl.ds(here, n)], self.local_sem.at[s, 0]))
        if k <= depth:
            half = n >> k
            bit, dev = partner(order[k - 1], self.dp, self.sq)
            at = self.off[s][k - 1]
            return (self.remote(s, k, self.acc.at[pl.ds(at + (1 - bit) * half, half)],
                                self.recv.at[pl.ds(self.roff[s][k], half)], dev), None)
        g = 2 * depth + 1 - k
        if g >= 1:
            half = n >> g
            bit, dev = partner(order[g - 1], self.dp, self.sq)
            piece = self.gat.at[pl.ds(self.off[s][g], half)]
            return (self.remote(s, k, piece, piece, dev), None)
        piece = self.gat.at[pl.ds(here, n)]
        there = self.out.at[pl.ds(2 * base + self.cbit * half_units + first, n)]
        return (self.remote(s, k, piece, there, self.cdev),
                pltpu.make_async_copy(piece, there, self.local_sem.at[s, 1]))

    def start(self, s, k):
        for c in self.copies(s, k):
            if c is not None:
                c.start()

    def finish(self, s, k):
        phase, first, n, order, _ = self.streams[s]
        depth = len(order)
        remote, local = self.copies(s, k)
        remote.wait()
        if local is not None:
            local.wait()
        if k <= depth:
            half = n >> k
            if k == 0:
                off = self.off[s][0]
            else:
                bit, _ = partner(order[k - 1], self.dp, self.sq)
                off = self.off[s][k - 1] + bit * half
                self.off[s].append(off)
            self.add(off, self.roff[s][k], half, self.gat if k == depth else self.acc)

    def add(self, off, roff, n, to):
        acc, recv = self.acc, self.recv
        step = 4 if n % 4 == 0 else (3 if n % 3 == 0 else (2 if n % 2 == 0 else 1))

        def body(i, c):
            a = pl.ds(off + i * step, step)
            b = pl.ds(roff + i * step, step)
            to[a] = acc[a] + recv[b]
            return c

        lax.fori_loop(0, n // step, body, 0)

    def step(self, s, k):
        self.finish(s, k)
        if k + 1 < self.n_stages(s):
            self.start(s, k + 1)


class Small:
    def __init__(self, n_dp, n_seq, dp, sq, buf, ssend, srecv, small_z, small_out):
        self.dims = [("seq", j) for j in range(bits_of(n_seq))] + [("dp", j) for j in range(bits_of(n_dp))]
        self.nz = bits_of(n_seq)
        self.dp, self.sq, self.buf, self.ssend, self.srecv = dp, sq, buf, ssend, srecv
        self.small_z, self.small_out = small_z, small_out
        self.done = 0

    def copy(self, i):
        _, dev = partner(self.dims[i], self.dp, self.sq)
        return pltpu.make_async_remote_copy(
            src_ref=self.buf.at[2 * i], dst_ref=self.buf.at[2 * i + 1], send_sem=self.ssend.at[i],
            recv_sem=self.srecv.at[i], device_id=dev, device_id_type=MESH)

    def begin(self, value):
        self.buf[0] = value
        self.copy(0).start()

    def step(self):
        i = self.done
        if i == len(self.dims):
            return
        self.copy(i).wait()
        total = self.buf[2 * i] + self.buf[2 * i + 1]
        self.done = i + 1
        if self.done == self.nz:
            self.small_z[...] = total
        if self.done < len(self.dims):
            self.buf[2 * self.done] = total
            self.copy(self.done).start()
        else:
            self.small_out[...] = total

    def rest(self):
        while self.done < len(self.dims):
            self.step()


def entry_barrier(n_dp, n_seq, dp, sq, all_seq):
    barrier = pltpu.get_barrier_semaphore()
    peers = [partner(("dp", j), dp, sq)[1] for j in range(bits_of(n_dp))]
    if all_seq:
        peers += [(dp, (sq + d) % n_seq) for d in range(1, n_seq)]
    else:
        peers += [partner(("seq", j), dp, sq)[1] for j in range(bits_of(n_seq))]
    for dev in peers:
        pl.semaphore_signal(barrier, inc=1, device_id=dev, device_id_type=MESH)
    return barrier, len(peers)


def matmul(former, latter):
    return jnp.dot(former, latter, preferred_element_type=jnp.float32)


def matmul_right_t(former, latter):
    return lax.dot_general(
        former, latter, (((1,), (1,)), ((), ())), preferred_element_type=jnp.float32
    )


def matmul_left_t(former, latter):
    return lax.dot_general(
        former, latter, (((0,), (0,)), ((), ())), preferred_element_type=jnp.float32
    )


FCH = 768
GELU_A = 0.044715


def flat(ref):
    return ref[...].reshape(1, -1)


def row_sum(v):
    return jnp.sum(v, axis=0, keepdims=True)


def mlp_kernel(steps, mixed, hidden, og, valid, proj_w, proj_b, n2g, n2s, fc_w, fc_b, out_w, out_b,
               output, mid_grad, mixed_grad, part, proj_part, small,
               nt_ref, xhat_ref, inv_ref, mid_ref, mlp_acc, two_acc):
    j = pl.program_id(0)

    @pl.when(j == 0)
    def _():
        x = hidden[...].astype(jnp.float32)
        attn = matmul(mixed[...], proj_w[...]) + flat(proj_b)
        middle = x + attn
        mid_ref[...] = middle
        v = valid[...]
        spread = middle - jnp.mean(middle, axis=-1, keepdims=True)
        inv = lax.rsqrt(jnp.mean(spread * spread, axis=-1, keepdims=True) + norm_eps)
        xhat = spread * inv
        xhat_ref[...] = xhat
        inv_ref[...] = jnp.broadcast_to(inv, inv_ref.shape)
        nt_ref[...] = (xhat * flat(n2g) + flat(n2s)).astype(jnp.bfloat16)
        small[...] = jnp.zeros_like(small)
        s0 = row_sum(jnp.sum(x * x, axis=-1, keepdims=True) * v)
        s1 = row_sum(jnp.sum(attn * attn, axis=-1, keepdims=True) * v)
        s3 = row_sum(v)
        lane = lax.broadcasted_iota(jnp.int32, (1, WID), 1)
        small[12:13, :] = jnp.where(lane == 0, s0, jnp.where(lane == 1, s1, jnp.where(lane == 3, s3, 0.0)))
        small[7:8, :] = row_sum(og[...].astype(jnp.float32))

    nt = nt_ref[...]
    fw = fc_w[...]
    ow = out_w[...]
    g_low = og[...]
    pre = matmul(nt, fw) + fc_b[...]
    sq = pre * pre
    t = jnp.tanh(tanh_coef * (pre + GELU_A * sq * pre))
    act = (0.5 * pre * (1.0 + t)).astype(jnp.bfloat16)
    slope = 0.5 * (1.0 + t) + 0.5 * pre * (1.0 - t * t) * (tanh_coef * (1.0 + 3.0 * GELU_A * sq))
    pre_grad = matmul_right_t(g_low, ow) * slope
    fcb = row_sum(pre_grad)
    for i in range(steps):
        @pl.when(j == i)
        def _():
            small[8 + i : 9 + i, :] = fcb
    low = pre_grad.astype(jnp.bfloat16)
    part[0, 0] = matmul_left_t(act, g_low).astype(jnp.bfloat16)
    part[0, 1] = matmul_left_t(nt, low).astype(jnp.bfloat16)
    mlp = matmul(act, ow)
    two = matmul_right_t(low, fw)

    @pl.when(j == 0)
    def _():
        mlp_acc[...] = mlp
        two_acc[...] = two

    @pl.when(j > 0)
    def _():
        mlp_acc[...] = mlp_acc[...] + mlp
        two_acc[...] = two_acc[...] + two

    @pl.when(j == steps - 1)
    def _():
        mlp_out = mlp_acc[...] + flat(out_b)
        output[...] = (mid_ref[...] + mlp_out).astype(jnp.bfloat16)
        s2 = row_sum(jnp.sum(mlp_out * mlp_out, axis=-1, keepdims=True) * valid[...])
        lane = lax.broadcasted_iota(jnp.int32, (1, WID), 1)
        small[12:13, :] = small[12:13, :] + jnp.where(lane == 2, s2, 0.0)
        two_grad = two_acc[...]
        xhat = xhat_ref[...]
        small[5:6, :] = row_sum(two_grad * xhat)
        small[6:7, :] = row_sum(two_grad)
        e = two_grad * flat(n2g)
        centre = jnp.mean(e, axis=-1, keepdims=True)
        along = jnp.mean(e * xhat, axis=-1, keepdims=True)
        grad = og[...].astype(jnp.float32) + (e - centre - xhat * along) * inv_ref[:, 0:1]
        mid_grad[...] = grad
        small[4:5, :] = row_sum(grad)
        grad_low = grad.astype(jnp.bfloat16)
        mixed_grad[...] = matmul_right_t(grad_low, proj_w[...]).astype(jnp.bfloat16)
        proj_part[...] = matmul_left_t(mixed[...], grad_low).astype(jnp.bfloat16)


def mlp_block(mixed, hidden, og, valid_col, proj_w, proj_b, n2g, n2s, fc_w, fc_b, out_w, out_b):
    rows, d = hidden.shape
    ff = fc_w.shape[1]
    steps = ff // FCH
    whole = lambda shape: pl.BlockSpec(shape, lambda j: (0,) * len(shape))
    vec = lambda v: v.reshape(1, -1)
    f32, bf = jnp.float32, jnp.bfloat16
    return pl.pallas_call(
        functools.partial(mlp_kernel, steps),
        grid=(steps,),
        in_specs=[whole((rows, d)), whole((rows, d)), whole((rows, d)), whole((rows, 1)), whole((d, d)), whole((d,)),
                  whole((d,)), whole((d,)), pl.BlockSpec((d, FCH), lambda j: (0, j)), pl.BlockSpec((1, FCH), lambda j: (0, j)),
                  pl.BlockSpec((FCH, d), lambda j: (j, 0)), whole((d,))],
        out_specs=(whole((rows, d)), whole((rows, d)), whole((rows, d)), pl.BlockSpec((1, 2, FCH, d), lambda j: (j, 0, 0, 0)),
                   whole((d, d)), whole((16, d))),
        out_shape=(jax.ShapeDtypeStruct((rows, d), bf), jax.ShapeDtypeStruct((rows, d), f32), jax.ShapeDtypeStruct((rows, d), bf),
                   jax.ShapeDtypeStruct((steps, 2, FCH, d), bf), jax.ShapeDtypeStruct((d, d), bf), jax.ShapeDtypeStruct((16, d), f32)),
        scratch_shapes=[pltpu.VMEM((rows, d), bf), pltpu.VMEM((rows, d), f32), pltpu.VMEM((rows, 128), f32),
                        pltpu.VMEM((rows, d), f32), pltpu.VMEM((rows, d), f32), pltpu.VMEM((rows, d), f32)],
        compiler_params=pltpu.CompilerParams(vmem_limit_bytes=62 * 2**20, dimension_semantics=("arbitrary",)),
        name="mlp_block",
    )(mixed, hidden, og, valid_col, proj_w, proj_b, n2g, n2s, fc_w, vec(fc_b), out_w, out_b)


PIECE = 384


def widen_kernel(cfg, src, small, small_z, gi_in, gs_in, *refs):
    pieces, n_out = cfg
    outs, vectors, (norms, gi_out, gs_out) = refs[:n_out], refs[n_out : n_out + 9], refs[n_out + 9 : n_out + 12]
    inbuf, stage, gi_buf, gs_buf, in_sem, out_sem, row_sem = refs[n_out + 12 :]
    depth = inbuf.shape[0]

    def fetch(i):
        return pltpu.make_async_copy(src.at[pl.ds(pieces[i][0], PIECE)], inbuf.at[i % depth], in_sem.at[i % depth])

    def put(i):
        slot = i % depth
        _, which, row, col, half = pieces[i]
        out = outs[which]
        if half:
            return [pltpu.make_async_copy(stage.at[slot, :, pl.ds(h * PIECE, PIECE)],
                                          out.at[pl.ds(h * PIECE, PIECE)], out_sem.at[slot, h]) for h in range(2)]
        return [pltpu.make_async_copy(stage.at[slot], out.at[pl.ds(row, PIECE), pl.ds(col, WID)], out_sem.at[slot, 0])]

    n = len(pieces)
    for i in range(min(depth, n)):
        fetch(i).start()
    row_in = [pltpu.make_async_copy(gi_in, gi_buf, row_sem.at[0]), pltpu.make_async_copy(gs_in, gs_buf, row_sem.at[1])]
    row_out = [pltpu.make_async_copy(gi_buf, gi_out, row_sem.at[2]), pltpu.make_async_copy(gs_buf, gs_out, row_sem.at[3])]
    for c in row_in:
        c.start()
    for i in range(n):
        slot = i % depth
        fetch(i).wait()
        if i >= depth:
            for c in put(i - depth):
                c.wait()

        def body(r, c):
            rows = pl.ds(r * 32, 32)
            stage[slot, rows] = inbuf[slot, rows].astype(jnp.float32)
            return c

        lax.fori_loop(0, PIECE // 32, body, 0)
        for c in put(i):
            c.start()
        if i + depth < n:
            fetch(i + depth).start()
        if i == depth:
            for a, b in zip(row_in, row_out):
                a.wait()
                b.start()
            for row, v in zip((0, 1, 2, 3, 4, 5, 6, 7), vectors):
                v[...] = small[row, 0 : v.shape[0]]
            for q in range(vectors[8].shape[0] // WID):
                vectors[8][q * WID : (q + 1) * WID] = small[8 + q, :]
            sums = small_z[12:13, 0:4]
            norms[...] = jnp.sqrt(sums[:, 0:3] / (sums[:, 3:4] * D) + square_eps)
    for i in range(max(0, n - depth), n):
        for c in put(i):
            c.wait()
    for c in row_out:
        c.wait()


def widen(summed, small, small_z, grad_input, grad_skip, row0, d, ff, vf):
    pieces = []
    for j in range(ff // FCH):
        for h in range(2):
            pieces.append((j * 2 * FCH + h * PIECE, 0, j * FCH + h * PIECE, 0, False))
        for h in range(2):
            pieces.append((j * 2 * FCH + FCH + h * PIECE, 1, h * PIECE, j * FCH, False))
    for w in range(3):
        for h in range(2):
            pieces.append((row0 + w * d + h * PIECE, 2 + w, h * PIECE, 0, False))
    pieces.append((row0 + 3 * d, 5, 0, 0, True))
    f32, bf = jnp.float32, jnp.bfloat16
    depth = 4
    hbm = pl.BlockSpec(memory_space=pl.ANY)
    vmem = pl.BlockSpec(memory_space=pltpu.VMEM)
    shapes = [(ff, d), (d, ff), (d, d), (d, d), (d, d), (d, vf)]
    vectors = [(d,), (d,), (d,), (vf,), (d,), (d,), (d,), (d,), (ff,)]
    out_shape = [jax.ShapeDtypeStruct(s, f32) for s in shapes + vectors + [(1, 3)]]
    out_shape += [jax.ShapeDtypeStruct(g.shape, bf) for g in (grad_input, grad_skip)]
    return pl.pallas_call(
        functools.partial(widen_kernel, (pieces, len(shapes))),
        in_specs=[hbm, vmem, vmem, hbm, hbm], out_specs=(hbm,) * 6 + (vmem,) * 10 + (hbm,) * 2, out_shape=tuple(out_shape),
        scratch_shapes=[pltpu.VMEM((depth, PIECE, WID), bf), pltpu.VMEM((depth, PIECE, WID), f32),
                        pltpu.VMEM(grad_input.shape, bf), pltpu.VMEM(grad_skip.shape, bf),
                        pltpu.SemaphoreType.DMA((depth,)), pltpu.SemaphoreType.DMA((depth, 2)), pltpu.SemaphoreType.DMA((4,))],
        compiler_params=pltpu.CompilerParams(vmem_limit_bytes=62 * 2**20),
        name="widen",
    )(summed, small, small_z, grad_input, grad_skip)


LANES = 128
PAIR_TILE = (0, 2, 3, 5)
THIRD_TILE = (1, 1, 4, 4)


def low_lanes():
    return lax.broadcasted_iota(jnp.int32, (1, LANES), 1) < HDIM


def turn(v):
    return pltpu.roll(v, HDIM, 1)


def pack_third(first, second, upper):
    first, second = first.astype(jnp.float32), second.astype(jnp.float32)
    if upper:
        both = jnp.where(low_lanes(), turn(first), second)
    else:
        both = jnp.where(low_lanes(), first, turn(second))
    return both.astype(jnp.bfloat16)


def unpack_third(both):
    wide = both.astype(jnp.float32)
    low = low_lanes()
    first = jnp.where(low, wide, 0.0).astype(jnp.bfloat16)
    second = jnp.where(low, turn(wide), 0.0).astype(jnp.bfloat16)
    return first, second


def join_thirds(one, two):
    one, two = one.astype(jnp.float32), two.astype(jnp.float32)
    low = low_lanes()
    first = jnp.where(low, one, turn(two)).astype(jnp.bfloat16)
    second = jnp.where(low, turn(one), two).astype(jnp.bfloat16)
    return first, second


def split_tiles(tiles, pair_dst, third_dst, rows, n_seq):
    half = rows // 2
    for r in range(n_seq):
        pair_dst(r, tiles[PAIR_TILE[r]])
        t = tiles[THIRD_TILE[r]]
        third_dst(r, pack_third(t[:half], t[half:], r % 2))


def mask_bias(lens, valid_row, first, rows, cols):
    one = lens[0, 0]
    two = one + lens[0, 1]
    i = first + lax.broadcasted_iota(jnp.int32, (rows, 1), 0)
    j = lax.broadcasted_iota(jnp.int32, (1, cols), 1)
    seg_i = (i >= one).astype(jnp.int32) + (i >= two).astype(jnp.int32)
    seg_j = (j >= one).astype(jnp.int32) + (j >= two).astype(jnp.int32)
    real = valid_row[:, 0:cols] > 0
    code = jnp.where(real, seg_j, -1)
    same = (code == seg_i) & (j <= i)
    return jnp.where(same | (i == j), 0.0, masked_score)


class Swap:
    def __init__(self, n_seq, dp, sq, send, recv, ssem, rsem):
        self.n_seq, self.dp, self.sq = n_seq, dp, sq
        self.send, self.recv, self.ssem, self.rsem = send, recv, ssem, rsem

    def copy(self, d):
        to = (self.sq + d) % self.n_seq
        return pltpu.make_async_remote_copy(
            src_ref=self.send(to), dst_ref=self.recv(self.sq), send_sem=self.ssem(d), recv_sem=self.rsem(d),
            device_id=(self.dp, to), device_id_type=MESH)

    def start(self):
        for d in range(1, self.n_seq):
            self.copy(d).start()

    def wait(self):
        for d in range(1, self.n_seq):
            self.copy(d).wait()


class Gather:
    def __init__(self, n_seq, dp, sq, send, recv, ssem, rsem):
        self.n_seq, self.dp, self.sq = n_seq, dp, sq
        self.send, self.recv, self.ssem, self.rsem = send, recv, ssem, rsem

    def copy(self, to, slot):
        return pltpu.make_async_remote_copy(
            src_ref=self.send(to), dst_ref=self.recv(slot), send_sem=self.ssem(to), recv_sem=self.rsem(slot),
            device_id=(self.dp, to), device_id_type=MESH)

    def start(self, to):
        @pl.when(self.sq != to)
        def _():
            self.copy(to, self.sq).start()

    def wait(self):
        for i in range(self.n_seq):
            @pl.when(self.sq != i)
            def _():
                self.copy(i, i).wait()


def front_kernel(cfg, lens, hidden, skip, valid_row, n1g, n1s, qw, qb, kw, vw, vb,
                 normed_out, mixed_out, pair_out, third_out, lse_out,
                 sp, st, rp, rt, smp, smt, rmp, rmt, bias, ssem, rsem, mssem, mrsem):
    n_dp, n_seq = cfg
    dp, sq = lax.axis_index("dp"), lax.axis_index("seq")
    rows = hidden.shape[0]
    half = rows // 2
    barrier = pltpu.get_barrier_semaphore()
    for d in range(1, n_seq):
        pl.semaphore_signal(barrier, inc=1, device_id=(dp, (sq + d) % n_seq), device_id_type=MESH)
    x = hidden[...].astype(jnp.float32)
    spread = x - jnp.mean(x, axis=-1, keepdims=True)
    inv = lax.rsqrt(jnp.mean(spread * spread, axis=-1, keepdims=True) + norm_eps)
    normed = (spread * inv * flat(n1g) + flat(n1s)).astype(jnp.bfloat16)
    normed_out[...] = normed
    swaps = [[Swap(n_seq, dp, sq, lambda to, t=t: sp.at[to, t], lambda me, t=t: rp.at[t, pl.ds(me * rows, rows)],
                   lambda d, t=t: ssem.at[0, t, d], lambda d, t=t: rsem.at[0, t, d]),
              Swap(n_seq, dp, sq, lambda to, t=t: st.at[to, t], lambda me, t=t: rt.at[t, me],
                   lambda d, t=t: ssem.at[1, t, d], lambda d, t=t: rsem.at[1, t, d])] for t in range(3)]
    first = True
    for t in range(3):
        if t == 0:
            full = (matmul(normed, qw[...]) + flat(qb)).astype(jnp.bfloat16)
        elif t == 1:
            full = matmul(normed, kw[...]).astype(jnp.bfloat16)
        else:
            full = (matmul(normed, vw[...]) + flat(vb)).astype(jnp.bfloat16)
        tiles = [full[:, c * LANES : (c + 1) * LANES] for c in range(full.shape[1] // LANES)]
        if t == 2:
            tiles += [skip[:, c * LANES : (c + 1) * LANES] for c in range(skip.shape[1] // LANES)]

        def pair_dst(r, v):
            sp[r, t] = v

        def third_dst(r, v):
            st[r, t] = v

        split_tiles(tiles, pair_dst, third_dst, rows, n_seq)
        if first:
            pl.semaphore_wait(barrier, n_seq - 1)
            first = False
        swaps[t][0].start()
    for t in range(3):
        swaps[t][1].start()
        rp[t, pl.ds(pl.multiple_of(sq * rows, rows), rows)] = sp[sq, t]
        rt[t, sq] = st[sq, t]
    for i in range(n_seq):
        cols = (i + 1) * rows
        bias[i * rows : (i + 1) * rows, 0:cols] = mask_bias(lens, valid_row, i * rows, rows, cols)
    back = [Gather(n_seq, dp, sq, lambda to: smp.at[to], lambda s: rmp.at[s], lambda i: mssem.at[0, i], lambda i: mrsem.at[0, i]),
            Gather(n_seq, dp, sq, lambda to: smt.at[to], lambda s: rmt.at[s], lambda i: mssem.at[1, i], lambda i: mrsem.at[1, i])]
    low = low_lanes()
    scale = 1.0 / math.sqrt(HDIM)
    keep = (jnp.where(low, scale, 0.0).astype(jnp.bfloat16), jnp.where(low, 0.0, scale).astype(jnp.bfloat16))

    def attend(q, k, v, block):
        scores = matmul_right_t(q, k) + block
        top = jnp.max(scores, axis=-1, keepdims=True)
        powered = jnp.exp(scores - top)
        total = jnp.sum(powered, axis=-1, keepdims=True)
        probs = (powered * (1.0 / total)).astype(jnp.bfloat16)
        return matmul(probs, v), top + jnp.log(total)

    for t in range(3):
        swaps[t][0].wait()
    lane = lax.broadcasted_iota(jnp.int32, (1, LANES), 1)
    for i in range(n_seq):
        here = slice(i * rows, (i + 1) * rows)
        cols = (i + 1) * rows
        block = bias[here, 0:cols]
        q, k, v = rp[0, here], rp[1, 0:cols], rp[2, 0:cols]
        o0, l0 = attend(q * keep[0], k, v, block)
        o1, l1 = attend(q * keep[1], k, v, block)
        smp[i] = jnp.where(low, o0, o1).astype(jnp.bfloat16)
        lse_out[here] = jnp.where(lane == 0, l0, l1)
        back[0].start(i)
    for t in range(3):
        swaps[t][1].wait()
        for s in range(n_seq):
            a, b = unpack_third(rt[t, s])
            third_out[t, s * rows : s * rows + half] = a
            third_out[t, s * rows + half : (s + 1) * rows] = b
    for i in range(n_seq):
        here = slice(i * rows, (i + 1) * rows)
        cols = (i + 1) * rows
        block = bias[here, 0:cols]
        o2, l2 = attend(third_out[0, here] * keep[0], third_out[1, 0:cols], third_out[2, 0:cols], block)
        smt[i] = pack_third(o2[:half], o2[half:], False)
        lse_out[here] = jnp.where(lane == 2, l2, lse_out[here])
        back[1].start(i)
    pair_out[...] = rp[...]
    rmp[sq] = smp[sq]
    rmt[sq] = smt[sq]
    back[0].wait()
    back[1].wait()
    for r in range(n_seq):
        c = PAIR_TILE[r] * LANES
        mixed_out[:, c : c + LANES] = rmp[r]
    for r in range(0, n_seq, 2):
        a, b = join_thirds(rmt[r], rmt[r + 1])
        c = THIRD_TILE[r] * LANES
        mixed_out[0:half, c : c + LANES] = a
        mixed_out[half:rows, c : c + LANES] = b


def front(mesh, hidden, skip, lens, valid, n1g, n1s, qw, qb, kw, vw, vb, collective_id):
    n_dp, n_seq = mesh.shape["dp"], mesh.shape["seq"]
    rows, d = hidden.shape
    group = rows * n_seq
    bf, f32 = jnp.bfloat16, jnp.float32
    vmem = pl.BlockSpec(memory_space=pltpu.VMEM)
    half = rows // 2
    dma = pltpu.SemaphoreType.DMA
    return pl.pallas_call(
        functools.partial(front_kernel, (n_dp, n_seq)),
        in_specs=[pl.BlockSpec(memory_space=pltpu.SMEM)] + [vmem] * 10,
        out_specs=(vmem,) * 5,
        out_shape=(jax.ShapeDtypeStruct((rows, d), bf), jax.ShapeDtypeStruct((rows, d), bf),
                   jax.ShapeDtypeStruct((3, group, LANES), bf), jax.ShapeDtypeStruct((3, group, LANES), bf),
                   jax.ShapeDtypeStruct((group, LANES), f32)),
        scratch_shapes=[
            pltpu.VMEM((n_seq, 3, rows, LANES), bf), pltpu.VMEM((n_seq, 3, half, LANES), bf),
            pltpu.VMEM((3, group, LANES), bf), pltpu.VMEM((3, n_seq, half, LANES), bf),
            pltpu.VMEM((n_seq, rows, LANES), bf), pltpu.VMEM((n_seq, half, LANES), bf),
            pltpu.VMEM((n_seq, rows, LANES), bf), pltpu.VMEM((n_seq, half, LANES), bf),
            pltpu.VMEM((group, group), f32),
            dma((2, 3, n_seq)), dma((2, 3, n_seq)), dma((2, n_seq)), dma((2, n_seq))],
        compiler_params=pltpu.CompilerParams(collective_id=collective_id, has_side_effects=True, vmem_limit_bytes=56 * 2**20),
        name="front",
    )(lens, hidden, skip, valid.reshape(1, -1), n1g, n1s, qw, qb, kw, vw, vb)


def back_kernel(cfg, lens, valid_row, mixed_grad, pair, third, lse, normed, hidden, n1g, mid_grad, qw, kw, vw, proj_part, small, part1,
                out, grad_input, grad_skip, small_z, small_out,
                gs, gst, gp, gt, gthird, bias, dk_acc, dv_acc, dsp, dst, drp, drt, rows_in, part2,
                acc, recv, gat, sbuf, gssem, grsem, dssem, drsem, send_sem, recv_sem, local_sem, ssend, srecv_sem):
    n_dp, n_seq, halves, streams, order, marks = cfg
    dp, sq = lax.axis_index("dp"), lax.axis_index("seq")
    rows, d = hidden.shape
    half = rows // 2
    bf, f32 = jnp.bfloat16, jnp.float32
    barrier, count = entry_barrier(n_dp, n_seq, dp, sq, True)
    full = mixed_grad[...]
    tiles = [full[:, c * LANES : (c + 1) * LANES] for c in range(d // LANES)]

    def pair_dst(r, v):
        gs[r] = v

    def third_dst(r, v):
        gst[r] = v

    split_tiles(tiles, pair_dst, third_dst, rows, n_seq)
    pl.semaphore_wait(barrier, count)
    swap_pair = Swap(n_seq, dp, sq, lambda to: gs.at[to], lambda me: gp.at[pl.ds(me * rows, rows)], lambda i: gssem.at[0, i], lambda i: grsem.at[0, i])
    swap_third = Swap(n_seq, dp, sq, lambda to: gst.at[to], lambda me: gt.at[me], lambda i: gssem.at[1, i], lambda i: grsem.at[1, i])
    swap_pair.start()
    swap_third.start()
    ex = Exchange(streams, halves, dp, sq, (part1, part2), out, acc, recv, gat, (send_sem, recv_sem, local_sem))
    tiny = Small(n_dp, n_seq, dp, sq, sbuf, ssend, srecv_sem, small_z, small_out)
    for s, st in enumerate(streams):
        if st[0] == 0:
            ex.start(s, 0)
    todo = list(order)

    def advance(upto):
        while todo and todo[0][0] <= upto:
            _, s, k = todo.pop(0)
            ex.step(s, k)

    gp[pl.ds(pl.multiple_of(sq * rows, rows), rows)] = gs[sq]
    gt[sq] = gst[sq]
    for i in range(n_seq):
        cols = (i + 1) * rows
        bias[i * rows : (i + 1) * rows, 0:cols] = mask_bias(lens, valid_row, i * rows, rows, cols)
    units_d = d // SUB
    part2[0:units_d] = proj_part[...].reshape(units_d, SUB, WID)
    send = [Gather(n_seq, dp, sq, lambda to: dsp.at[to], lambda s: drp.at[s], lambda i: dssem.at[0, i], lambda i: drsem.at[0, i]),
            Gather(n_seq, dp, sq, lambda to: dst.at[to], lambda s: drt.at[s], lambda i: dssem.at[1, i], lambda i: drsem.at[1, i])]
    low = low_lanes()
    scale = 1.0 / math.sqrt(HDIM)
    keep = (jnp.where(low, scale, 0.0).astype(bf), jnp.where(low, 0.0, scale).astype(bf))
    ones = (jnp.where(low, 1.0, 0.0).astype(bf), jnp.where(low, 0.0, 1.0).astype(bf))

    def backward(q, k, v, g, block, total):
        probs = jnp.exp(matmul_right_t(q, k) + block - total)
        prob_grad = matmul_right_t(g, v)
        centre = jnp.sum(probs * prob_grad, axis=-1, keepdims=True)
        score_grad = (probs * (prob_grad - centre)).astype(bf)
        return matmul(score_grad, k), matmul_left_t(score_grad, q), matmul_left_t(probs.astype(bf), g)

    mark = iter(marks)
    advance(next(mark))
    swap_pair.wait()
    for i in reversed(range(n_seq)):
        here = slice(i * rows, (i + 1) * rows)
        cols = (i + 1) * rows
        block = bias[here, 0:cols]
        q, k, v, g = pair[0, here], pair[1, 0:cols], pair[2, 0:cols], gp[here]
        dq0, dk0, dv0 = backward(q * keep[0], k, v, g * ones[0], block, lse[here, 0:1])
        dq1, dk1, dv1 = backward(q * keep[1], k, v, g * ones[1], block, lse[here, 1:2])
        if i == n_seq - 1:
            dk_acc[...] = dk0 + dk1
            dv_acc[...] = dv0 + dv1
        else:
            dk_acc[0:cols] = dk_acc[0:cols] + (dk0 + dk1)
            dv_acc[0:cols] = dv_acc[0:cols] + (dv0 + dv1)
        dsp[i, 0] = (jnp.where(low, dq0, dq1) * scale).astype(bf)
        dsp[i, 1] = dk_acc[here].astype(bf)
        dsp[i, 2] = dv_acc[here].astype(bf)
        send[0].start(i)
        advance(next(mark))
    swap_third.wait()
    for s in range(n_seq):
        a, b = unpack_third(gt[s])
        gthird[s * rows : s * rows + half] = a
        gthird[s * rows + half : (s + 1) * rows] = b
    for i in reversed(range(n_seq)):
        here = slice(i * rows, (i + 1) * rows)
        cols = (i + 1) * rows
        block = bias[here, 0:cols]
        dq, dk, dv = backward(third[0, here] * keep[0], third[1, 0:cols], third[2, 0:cols], gthird[here], block, lse[here, 2:3])
        if i == n_seq - 1:
            dk_acc[...] = dk
            dv_acc[...] = dv
        else:
            dk_acc[0:cols] = dk_acc[0:cols] + dk
            dv_acc[0:cols] = dv_acc[0:cols] + dv
        dq = dq * scale
        dst[i, 0] = pack_third(dq[:half], dq[half:], False)
        for t, a in ((1, dk_acc), (2, dv_acc)):
            dst[i, t] = pack_third(a[i * rows : i * rows + half], a[i * rows + half : (i + 1) * rows], False)
        send[1].start(i)
        advance(next(mark))
    drp[sq] = dsp[sq]
    drt[sq] = dst[sq]
    x = hidden[...].astype(f32)
    spread = x - jnp.mean(x, axis=-1, keepdims=True)
    inv = lax.rsqrt(jnp.mean(spread * spread, axis=-1, keepdims=True) + norm_eps)
    xhat = spread * inv
    send[0].wait()
    advance(next(mark))
    send[1].wait()
    for t in range(3):
        for r in range(n_seq):
            c = PAIR_TILE[r] * LANES
            rows_in[t, :, c : c + LANES] = drp[r, t]
        for r in range(0, n_seq, 2):
            a, b = join_thirds(drt[r, t], drt[r + 1, t])
            c = THIRD_TILE[r] * LANES
            rows_in[t, 0:half, c : c + LANES] = a
            rows_in[t, half:rows, c : c + LANES] = b
    nl = normed[...]
    dq, dk, dv = rows_in[0], rows_in[1], rows_in[2]
    fresh = dv[:, 0:VFRESH]
    grad_skip[...] = dv[:, VFRESH:]
    part2[units_d : 2 * units_d] = matmul_left_t(nl, dq).astype(bf).reshape(units_d, SUB, WID)
    part2[2 * units_d : 3 * units_d] = matmul_left_t(nl, dk).astype(bf).reshape(units_d, SUB, WID)
    gv = matmul_left_t(nl, fresh).astype(bf)
    uv = d // 2 // SUB
    part2[3 * units_d : 3 * units_d + uv, :, 0:VFRESH] = gv[: d // 2].reshape(uv, SUB, VFRESH)
    part2[3 * units_d : 3 * units_d + uv, :, VFRESH:] = gv[d // 2 :].reshape(uv, SUB, VFRESH)
    extra = 2 * halves[1] - 3 * units_d - uv
    if extra:
        part2[3 * units_d + uv :] = jnp.zeros((extra, SUB, WID), bf)
    for s, st in enumerate(streams):
        if st[0] == 1:
            ex.start(s, 0)
    advance(next(mark))
    normed_grad = matmul_right_t(dq, qw[...]) + matmul_right_t(dk, kw[...]) + matmul_right_t(fresh, vw[...])
    f = normed_grad * flat(n1g)
    centre = jnp.mean(f, axis=-1, keepdims=True)
    along = jnp.mean(f * xhat, axis=-1, keepdims=True)
    grad_input[...] = (mid_grad[...] + (f - centre - xhat * along) * inv).astype(bf)
    sbuf[0] = small[...]
    sbuf[0, 0:1] = row_sum(normed_grad * xhat)
    sbuf[0, 1:2] = row_sum(normed_grad)
    sbuf[0, 2:3] = row_sum(dq.astype(f32))
    sbuf[0, 3:4, 0:VFRESH] = row_sum(fresh.astype(f32))
    tiny.copy(0).start()
    gap = max(1, len(todo) // (len(tiny.dims) + 2))
    left = 0
    while todo:
        _, s, k = todo.pop(0)
        ex.step(s, k)
        left += 1
        if left % gap == 0:
            tiny.step()
    tiny.rest()


def back(mesh, lens, valid, mixed_grad, pair, third, lse, normed, hidden, n1g, mid_grad, qw, kw, vw, proj_part, small, part1, collective_id):
    n_dp, n_seq = mesh.shape["dp"], mesh.shape["seq"]
    rows, d = hidden.shape
    group = rows * n_seq
    half = rows // 2
    bf, f32 = jnp.bfloat16, jnp.float32
    quantum = n_dp * n_seq
    rows2 = 3 * d + d // 2
    units2 = -(-rows2 // SUB // quantum) * quantum
    halves = (part1.shape[0] // 2, units2 // 2)
    streams = plan_streams(n_dp, n_seq, list(zip(halves, SHARES)), STARTS)
    order = schedule(streams, (("seq", 9.0),))
    n_st = 2 * (bits_of(n_dp) + bits_of(n_seq))
    n_small = bits_of(n_dp) + bits_of(n_seq)
    ns = len(streams)
    vmem = pl.BlockSpec(memory_space=pltpu.VMEM)
    hbm = pl.BlockSpec(memory_space=pl.ANY)
    dma = pltpu.SemaphoreType.DMA
    units = lambda n: pltpu.VMEM((n, SUB, WID), bf)
    sshape = jax.ShapeDtypeStruct(small.shape, f32)
    return pl.pallas_call(
        functools.partial(back_kernel, (n_dp, n_seq, halves, streams, order, MARKS)),
        in_specs=[pl.BlockSpec(memory_space=pltpu.SMEM)] + [vmem] * 14 + [hbm],
        out_specs=(hbm, vmem, vmem, vmem, vmem),
        out_shape=(jax.ShapeDtypeStruct((2 * sum(halves), SUB, WID), bf), jax.ShapeDtypeStruct((rows, d), bf),
                   jax.ShapeDtypeStruct((rows, d - VFRESH), bf), sshape, sshape),
        scratch_shapes=[
            pltpu.VMEM((n_seq, rows, LANES), bf), pltpu.VMEM((n_seq, half, LANES), bf),
            pltpu.VMEM((group, LANES), bf), pltpu.VMEM((n_seq, half, LANES), bf), pltpu.VMEM((group, LANES), bf),
            pltpu.VMEM((group, group), f32), pltpu.VMEM((group, LANES), f32), pltpu.VMEM((group, LANES), f32),
            pltpu.VMEM((n_seq, 3, rows, LANES), bf), pltpu.VMEM((n_seq, 3, half, LANES), bf),
            pltpu.VMEM((n_seq, 3, rows, LANES), bf), pltpu.VMEM((n_seq, 3, half, LANES), bf),
            pltpu.VMEM((3, rows, d), bf), units(units2),
            units(sum(halves)), units(Exchange.recv_total(streams, halves)), units(sum(halves)),
            pltpu.VMEM((2 * n_small,) + small.shape, f32),
            dma((2, n_seq)), dma((2, n_seq)), dma((2, n_seq)), dma((2, n_seq)),
            dma((ns, n_st)), dma((ns, n_st)), dma((ns, 2)), dma((n_small,)), dma((n_small,))],
        compiler_params=pltpu.CompilerParams(collective_id=collective_id, has_side_effects=True, vmem_limit_bytes=63 * 2**20),
        name="back",
    )(lens, valid.reshape(1, -1), mixed_grad, pair, third, lse, normed, hidden, n1g, mid_grad, qw, kw, vw, proj_part,
      small, part1)


def local(
    mesh,
    hidden_in,
    skip_values,
    out_grad,
    doc_lens,
    valid,
    norm1_gain,
    norm1_shift,
    query_w,
    query_b,
    key_w,
    value_w,
    value_b,
    proj_w,
    proj_b,
    norm2_gain,
    norm2_shift,
    fc_w,
    fc_b,
    out_w,
    out_b,
):
    seq_size = lax.axis_size("seq")
    seq_rank = lax.axis_index("seq")
    tok_rows = hidden_in.shape[0]
    valid_col = lax.dynamic_slice_in_dim(valid, seq_rank * tok_rows, tok_rows, 0).astype(jnp.float32)[:, None]
    normed, mixed, pair, third, lse = front(
        mesh, hidden_in, skip_values, doc_lens, valid, norm1_gain, norm1_shift, query_w, query_b, key_w, value_w, value_b, 0
    )
    output, middle_grad, mixed_grad, part, proj_part, small = mlp_block(
        mixed, hidden_in, out_grad, valid_col, proj_w, proj_b, norm2_gain, norm2_shift, fc_w, fc_b, out_w, out_b
    )
    part1 = part.reshape(-1, SUB, WID)
    summed, grad_input, grad_skip, small_z, small_all = back(
        mesh, doc_lens, valid, mixed_grad, pair, third, lse, normed, hidden_in, norm1_gain, middle_grad,
        query_w, key_w, value_w, proj_part, small, part1, 1
    )
    row0 = part1.shape[0] * SUB
    (
        grad_out_w, grad_fc_w, grad_proj_w, grad_query_w, grad_key_w, grad_value_w,
        grad_norm1_gain, grad_norm1_shift, grad_query_b, grad_value_b, grad_proj_b, grad_norm2_gain, grad_norm2_shift,
        grad_out_b, grad_fc_b, norm_values, grad_input, grad_skip,
    ) = widen(summed.reshape(-1, WID), small_all, small_z, grad_input, grad_skip, row0, D, fc_w.shape[1], VFRESH)
    return (
        output,
        grad_input,
        grad_skip,
        grad_norm1_gain,
        grad_norm1_shift,
        grad_query_w,
        grad_query_b,
        grad_key_w,
        grad_value_w,
        grad_value_b,
        grad_proj_w,
        grad_proj_b,
        grad_norm2_gain,
        grad_norm2_shift,
        grad_fc_w,
        grad_fc_b,
        grad_out_w,
        grad_out_b,
        norm_values,
    )


def solution(mesh):
    placed = (
        P(("dp", "seq"), None),
        P(("dp", "seq"), None),
        P(("dp", "seq"), None),
        P("dp", None),
        P("dp"),
        P(),
        P(),
        P(),
        P(),
        P(),
        P(),
        P(),
        P(),
        P(),
        P(),
        P(),
        P(),
        P(),
        P(),
        P(),
    )
    return jax.shard_map(
        functools.partial(local, mesh),
        mesh=mesh,
        in_specs=placed,
        out_specs=(
            P(("dp", "seq"), None),
            P(("dp", "seq"), None),
            P(("dp", "seq"), None),
            P(),
            P(),
            P(),
            P(),
            P(),
            P(),
            P(),
            P(),
            P(),
            P(),
            P(),
            P(),
            P(),
            P(),
            P(),
            P("dp", None),
        ),
        check_vma=False,
    )
```

```python
import functools
import math

import jax
import jax.numpy as jnp
from jax import lax
from jax.experimental import pallas as pl
from jax.experimental.pallas import tpu as pltpu
from jax.sharding import PartitionSpec as P

D = 768
HEADS = 12
HDIM = 64
VFRESH = 384


norm_eps = 1e-05
square_eps = 1e-06
tanh_coef = 0.7978845608028654
masked_score = -1e30


MESH = pl.DeviceIdType.MESH
SUB = 8
WID = 768
UNIT_BYTES = SUB * WID * 2
FCH = 768
CHUNK = FCH // SUB
READY = (7.0, 10.5, 14.0, 17.5, 20.5)
START_TWO = 63.0
MARKS = (8.0, 12.0, 17.0, 24.0, 26.0, 28.0, 29.0, 30.0, 31.0, 32.0, 33.0, 34.0, 40.0, 48.0, 58.0)


def bits_of(n):
    return n.bit_length() - 1


def partner(dim, dp, sq):
    kind, j = dim
    step = 1 << j
    if kind == "dp":
        bit = (dp // step) % 2
        return bit, (dp + step - 2 * step * bit, sq)
    bit = (sq // step) % 2
    return bit, (dp, sq + step - 2 * step * bit)


def plan_streams(n_dp, n_seq, halves, steps):
    dpb = [("dp", j) for j in range(1, bits_of(n_dp))]
    sqb = [("seq", j) for j in range(bits_of(n_seq))]
    mid = len(dpb) // 2
    orders = (dpb + sqb, dpb[mid:] + dpb[:mid] + sqb)
    quantum = (n_dp // 2) * n_seq
    streams = []
    for phase, half_units in enumerate(halves):
        total = half_units // quantum
        count = max(1, total // 2)
        first = 0
        for i in range(count):
            n = (2 if i < count - 1 else total - 2 * (count - 1)) * quantum
            chunk = min(steps, (first + n - 1) // CHUNK)
            start = READY[min(chunk, len(READY) - 1)] if phase == 0 else START_TWO
            streams.append((phase, first, n, orders[i % 2], start, chunk))
            first += n
    return streams


def schedule(streams, busy=()):
    free = {}
    for res, upto in busy:
        free[res] = upto
    out = []
    stages = []
    for phase, first, n, order, start, _ in streams:
        seq = []
        size = n
        seq.append((("dp", 0), size))
        for d in order:
            size //= 2
            seq.append((d, size))
        for d in reversed(order):
            seq.append((d, size))
            size *= 2
        seq.append((("dp", 0), size))
        stages.append(seq)
    at = [0] * len(streams)
    waiting = [(st[4], s) for s, st in enumerate(streams)]
    pending = []

    def launch(s, t):
        d, size = stages[s][at[s]]
        b = size * UNIT_BYTES / 1e6
        if d == ("dp", 0):
            res, dur = "c", b / 0.5
        elif d[0] == "dp":
            res, dur = d, b / 0.045
        else:
            res, dur = "seq", b / 0.045 * (1 << d[1])
        st = max(t, free.get(res, 0.0))
        free[res] = st + dur
        pending.append((st + dur + 2.0, s))

    while pending or waiting:
        pending.sort()
        waiting.sort()
        if waiting and (not pending or waiting[0][0] <= pending[0][0]):
            t, s = waiting.pop(0)
            launch(s, t)
            continue
        t, s = pending.pop(0)
        out.append((t, s, at[s]))
        at[s] += 1
        if at[s] < len(stages[s]):
            launch(s, t + 0.3)
    return out


class Exchange:
    def __init__(self, streams, halves, dp, sq, parts, out, recv, gat, sems):
        self.streams, self.halves = streams, halves
        self.dp, self.sq = dp, sq
        self.parts, self.out, self.recv, self.gat = parts, out, recv, gat
        self.send_sem, self.recv_sem, self.local_sem = sems
        self.cbit, self.cdev = partner(("dp", 0), dp, sq)
        self.base = [sum(halves[:p]) for p in range(len(halves))]
        self.off = [[st[1]] for st in streams]
        self.roff = []
        r = 0
        for phase, first, n, order, _, _ in streams:
            rows = [r]
            r += n
            size = n
            for _ in order:
                size //= 2
                rows.append(r)
                r += size
            self.roff.append(rows)

    @staticmethod
    def recv_total(streams):
        r = 0
        for phase, first, n, order, _, _ in streams:
            r += n
            for i in range(len(order)):
                r += n >> (i + 1)
        return r

    def n_stages(self, s):
        return 2 * (len(self.streams[s][3]) + 1)

    def remote(self, s, k, src, dst, dev):
        return pltpu.make_async_remote_copy(
            src_ref=src, dst_ref=dst, send_sem=self.send_sem.at[s, k], recv_sem=self.recv_sem.at[s, k],
            device_id=dev, device_id_type=MESH)

    def copies(self, s, k):
        phase, first, n, order, _, _ = self.streams[s]
        depth = len(order)
        half_units, base = self.halves[phase], self.base[phase]
        part = self.parts[phase]
        own = self.cbit * half_units
        if k == 0:
            other = (1 - self.cbit) * half_units + first
            return self.remote(s, k, part.at[pl.ds(other, n)], self.recv.at[pl.ds(self.roff[s][0], n)], self.cdev), None
        if k <= depth:
            half = n >> k
            bit, dev = partner(order[k - 1], self.dp, self.sq)
            at = own + self.off[s][k - 1] + (1 - bit) * half
            return self.remote(s, k, part.at[pl.ds(at, half)], self.recv.at[pl.ds(self.roff[s][k], half)], dev), None
        g = 2 * depth + 1 - k
        if g >= 1:
            half = n >> g
            bit, dev = partner(order[g - 1], self.dp, self.sq)
            piece = self.gat.at[pl.ds(base + self.off[s][g], half)]
            return self.remote(s, k, piece, piece, dev), None
        piece = self.gat.at[pl.ds(base + first, n)]
        there = self.out.at[pl.ds(2 * base + own + first, n)]
        return self.remote(s, k, piece, there, self.cdev), pltpu.make_async_copy(piece, there, self.local_sem.at[s])

    def start(self, s, k):
        for c in self.copies(s, k):
            if c is not None:
                c.start()

    def finish(self, s, k):
        phase, first, n, order, _, _ = self.streams[s]
        depth = len(order)
        remote, local = self.copies(s, k)
        remote.wait()
        if local is not None:
            local.wait()
        if k <= depth:
            half = n >> k
            if k > 0:
                bit, _ = partner(order[k - 1], self.dp, self.sq)
                self.off[s].append(self.off[s][k - 1] + bit * half)
            at = self.cbit * self.halves[phase] + self.off[s][k]
            to = (self.gat, self.base[phase] + self.off[s][k]) if k == depth else (self.parts[phase], at)
            self.add(self.parts[phase], at, self.roff[s][k], half, to)

    def add(self, part, at, roff, n, to):
        recv = self.recv
        dst, first = to
        step = next(d for d in (8, 6, 4, 3, 2, 1) if n % d == 0)

        def body(i, c):
            a = pl.ds(at + i * step, step)
            b = pl.ds(roff + i * step, step)
            dst[pl.ds(first + i * step, step)] = part[a] + recv[b]
            return c

        lax.fori_loop(0, n // step, body, 0)

    def step(self, s, k):
        self.finish(s, k)
        if k + 1 < self.n_stages(s):
            self.start(s, k + 1)


class Small:
    def __init__(self, n_dp, n_seq, dp, sq, buf, ssend, srecv, small_z, small_out):
        self.dims = [("seq", j) for j in range(bits_of(n_seq))] + [("dp", j) for j in range(bits_of(n_dp))]
        self.nz = bits_of(n_seq)
        self.dp, self.sq, self.buf, self.ssend, self.srecv = dp, sq, buf, ssend, srecv
        self.small_z, self.small_out = small_z, small_out
        self.done = 0

    def copy(self, i):
        _, dev = partner(self.dims[i], self.dp, self.sq)
        return pltpu.make_async_remote_copy(
            src_ref=self.buf.at[2 * i], dst_ref=self.buf.at[2 * i + 1], send_sem=self.ssend.at[i],
            recv_sem=self.srecv.at[i], device_id=dev, device_id_type=MESH)

    def begin(self, value):
        self.buf[0] = value
        self.copy(0).start()

    def step(self):
        i = self.done
        if i == len(self.dims):
            return
        self.copy(i).wait()
        total = self.buf[2 * i] + self.buf[2 * i + 1]
        self.done = i + 1
        if self.done == self.nz:
            self.small_z[...] = total
        if self.done < len(self.dims):
            self.buf[2 * self.done] = total
            self.copy(self.done).start()
        else:
            self.small_out[...] = total

    def rest(self):
        while self.done < len(self.dims):
            self.step()


def entry_barrier(n_dp, n_seq, dp, sq, all_seq):
    barrier = pltpu.get_barrier_semaphore()
    peers = [partner(("dp", j), dp, sq)[1] for j in range(bits_of(n_dp))]
    if all_seq:
        peers += [(dp, (sq + d) % n_seq) for d in range(1, n_seq)]
    else:
        peers += [partner(("seq", j), dp, sq)[1] for j in range(bits_of(n_seq))]
    for dev in peers:
        pl.semaphore_signal(barrier, inc=1, device_id=dev, device_id_type=MESH)
    return barrier, len(peers)


def matmul(former, latter):
    return jnp.dot(former, latter, preferred_element_type=jnp.float32)


def matmul_right_t(former, latter):
    return lax.dot_general(
        former, latter, (((1,), (1,)), ((), ())), preferred_element_type=jnp.float32
    )


def matmul_left_t(former, latter):
    return lax.dot_general(
        former, latter, (((0,), (0,)), ((), ())), preferred_element_type=jnp.float32
    )


def flat(ref):
    return ref[...].reshape(1, -1)


def row_sum(v):
    return jnp.sum(v, axis=0, keepdims=True)


PIECE = 384
VPIECE = 192


def widen_kernel(cfg, src, small, small_z, gi_in, gs_in, *refs):
    pieces, n_out = cfg
    outs, vectors, (norms, gi_out, gs_out) = refs[:n_out], refs[n_out : n_out + 9], refs[n_out + 9 : n_out + 12]
    inbuf, stage, gi_buf, gs_buf, in_sem, out_sem, row_sem = refs[n_out + 12 :]
    depth = inbuf.shape[0]

    def fetch(i):
        size = VPIECE if pieces[i][4] else PIECE
        return pltpu.make_async_copy(src.at[pl.ds(pieces[i][0], size)], inbuf.at[i % depth, pl.ds(0, size)], in_sem.at[i % depth])

    def put(i):
        slot = i % depth
        _, which, row, col, split = pieces[i]
        out = outs[which]
        if split:
            return [pltpu.make_async_copy(stage.at[slot, pl.ds(0, VPIECE), pl.ds(h * VFRESH, VFRESH)],
                                          out.at[pl.ds(row + h * VFRESH, VPIECE)], out_sem.at[slot, h]) for h in range(2)]
        return [pltpu.make_async_copy(stage.at[slot], out.at[pl.ds(row, PIECE), pl.ds(col, WID)], out_sem.at[slot, 0])]

    n = len(pieces)
    for i in range(min(depth, n)):
        fetch(i).start()
    row_in = [pltpu.make_async_copy(gi_in, gi_buf, row_sem.at[0]), pltpu.make_async_copy(gs_in, gs_buf, row_sem.at[1])]
    row_out = [pltpu.make_async_copy(gi_buf, gi_out, row_sem.at[2]), pltpu.make_async_copy(gs_buf, gs_out, row_sem.at[3])]
    for c in row_in:
        c.start()
    for i in range(n):
        slot = i % depth
        fetch(i).wait()
        if i >= depth:
            for c in put(i - depth):
                c.wait()

        def body(r, c):
            rows = pl.ds(r * 32, 32)
            stage[slot, rows] = inbuf[slot, rows].astype(jnp.float32)
            return c

        lax.fori_loop(0, (VPIECE if pieces[i][4] else PIECE) // 32, body, 0)
        for c in put(i):
            c.start()
        if i + depth < n:
            fetch(i + depth).start()
        if i == depth:
            for a, b in zip(row_in, row_out):
                a.wait()
                b.start()
            for row, v in zip((0, 1, 2, 3, 4, 5, 6, 7), vectors):
                v[...] = small[row, 0 : v.shape[0]]
            for q in range(vectors[8].shape[0] // WID):
                vectors[8][q * WID : (q + 1) * WID] = small[8 + q, :]
            sums = small_z[12:13, 0:4]
            norms[...] = jnp.sqrt(sums[:, 0:3] / (sums[:, 3:4] * D) + square_eps)
    for i in range(max(0, n - depth), n):
        for c in put(i):
            c.wait()
    for c in row_out:
        c.wait()


def widen(summed, small, small_z, grad_input, grad_skip, halves, d, ff, vf):
    one, two = halves[0] * SUB, halves[1] * SUB
    pieces = []
    for j in range(ff // PIECE):
        pieces.append((j * PIECE, 0, j * PIECE, 0, False))
        pieces.append((one + j * PIECE, 1, (j % 2) * PIECE, j // 2 * FCH, False))
    for h in range(2):
        pieces.append((h * one + ff, 2, h * PIECE, 0, False))
    for w in range(2):
        for h in range(2):
            pieces.append((2 * one + w * two + h * PIECE, 3 + w, h * PIECE, 0, False))
    for h in range(2):
        pieces.append((2 * one + h * two + d, 5, h * VPIECE, 0, True))
    f32, bf = jnp.float32, jnp.bfloat16
    depth = 4
    hbm = pl.BlockSpec(memory_space=pl.ANY)
    vmem = pl.BlockSpec(memory_space=pltpu.VMEM)
    shapes = [(ff, d), (d, ff), (d, d), (d, d), (d, d), (d, vf)]
    vectors = [(d,), (d,), (d,), (vf,), (d,), (d,), (d,), (d,), (ff,)]
    out_shape = [jax.ShapeDtypeStruct(s, f32) for s in shapes + vectors + [(1, 3)]]
    out_shape += [jax.ShapeDtypeStruct(g.shape, bf) for g in (grad_input, grad_skip)]
    return pl.pallas_call(
        functools.partial(widen_kernel, (pieces, len(shapes))),
        in_specs=[hbm, vmem, vmem, hbm, hbm], out_specs=(hbm,) * 6 + (vmem,) * 10 + (hbm,) * 2, out_shape=tuple(out_shape),
        scratch_shapes=[pltpu.VMEM((depth, PIECE, WID), bf), pltpu.VMEM((depth, PIECE, WID), f32),
                        pltpu.VMEM(grad_input.shape, bf), pltpu.VMEM(grad_skip.shape, bf),
                        pltpu.SemaphoreType.DMA((depth,)), pltpu.SemaphoreType.DMA((depth, 2)), pltpu.SemaphoreType.DMA((4,))],
        compiler_params=pltpu.CompilerParams(vmem_limit_bytes=62 * 2**20),
        name="widen",
    )(summed, small, small_z, grad_input, grad_skip)


LANES = 128
PAIR_TILE = (0, 2, 3, 5)
THIRD_TILE = (1, 1, 4, 4)


def low_lanes():
    return lax.broadcasted_iota(jnp.int32, (1, LANES), 1) < HDIM


def turn(v):
    return pltpu.roll(v, HDIM, 1)


def pack_third(first, second, upper):
    first, second = first.astype(jnp.float32), second.astype(jnp.float32)
    if upper:
        both = jnp.where(low_lanes(), turn(first), second)
    else:
        both = jnp.where(low_lanes(), first, turn(second))
    return both.astype(jnp.bfloat16)


def unpack_third(both):
    wide = both.astype(jnp.float32)
    low = low_lanes()
    first = jnp.where(low, wide, 0.0).astype(jnp.bfloat16)
    second = jnp.where(low, turn(wide), 0.0).astype(jnp.bfloat16)
    return first, second


def join_thirds(one, two):
    one, two = one.astype(jnp.float32), two.astype(jnp.float32)
    low = low_lanes()
    first = jnp.where(low, one, turn(two)).astype(jnp.bfloat16)
    second = jnp.where(low, turn(one), two).astype(jnp.bfloat16)
    return first, second


def split_tiles(tiles, pair_dst, third_dst, rows, n_seq):
    half = rows // 2
    for r in range(n_seq):
        pair_dst(r, tiles[PAIR_TILE[r]])
        t = tiles[THIRD_TILE[r]]
        third_dst(r, pack_third(t[:half], t[half:], r % 2))


def mask_bias(lens, valid_row, first, rows, cols):
    one = lens[0, 0]
    two = one + lens[0, 1]
    i = first + lax.broadcasted_iota(jnp.int32, (rows, 1), 0)
    j = lax.broadcasted_iota(jnp.int32, (1, cols), 1)
    seg_i = (i >= one).astype(jnp.int32) + (i >= two).astype(jnp.int32)
    seg_j = (j >= one).astype(jnp.int32) + (j >= two).astype(jnp.int32)
    real = valid_row[:, 0:cols] > 0
    code = jnp.where(real, seg_j, -1)
    same = (code == seg_i) & (j <= i)
    return jnp.where(same | (i == j), 0.0, masked_score)


class Swap:
    def __init__(self, n_seq, dp, sq, send, recv, ssem, rsem):
        self.n_seq, self.dp, self.sq = n_seq, dp, sq
        self.send, self.recv, self.ssem, self.rsem = send, recv, ssem, rsem

    def copy(self, d):
        to = (self.sq + d) % self.n_seq
        return pltpu.make_async_remote_copy(
            src_ref=self.send(to), dst_ref=self.recv(self.sq), send_sem=self.ssem(d), recv_sem=self.rsem(d),
            device_id=(self.dp, to), device_id_type=MESH)

    def start(self):
        for d in range(1, self.n_seq):
            self.copy(d).start()

    def wait(self):
        for d in range(1, self.n_seq):
            self.copy(d).wait()


class Gather:
    def __init__(self, n_seq, dp, sq, send, recv, ssem, rsem):
        self.n_seq, self.dp, self.sq = n_seq, dp, sq
        self.send, self.recv, self.ssem, self.rsem = send, recv, ssem, rsem

    def copy(self, to, slot):
        return pltpu.make_async_remote_copy(
            src_ref=self.send(to), dst_ref=self.recv(slot), send_sem=self.ssem(to), recv_sem=self.rsem(slot),
            device_id=(self.dp, to), device_id_type=MESH)

    def start(self, to):
        @pl.when(self.sq != to)
        def _():
            self.copy(to, self.sq).start()

    def wait(self):
        for i in range(self.n_seq):
            @pl.when(self.sq != i)
            def _():
                self.copy(i, i).wait()


def front_kernel(cfg, lens, hidden, skip, valid_row, n1g, n1s, qw, qb, kw, vw, vb,
                 normed_out, mixed_out, pair_out, third_out, lse_out,
                 sp, st, rp, rt, smp, smt, rmp, rmt, bias, ssem, rsem, mssem, mrsem):
    n_dp, n_seq = cfg
    dp, sq = lax.axis_index("dp"), lax.axis_index("seq")
    rows = hidden.shape[0]
    half = rows // 2
    barrier = pltpu.get_barrier_semaphore()
    for d in range(1, n_seq):
        pl.semaphore_signal(barrier, inc=1, device_id=(dp, (sq + d) % n_seq), device_id_type=MESH)
    x = hidden[...].astype(jnp.float32)
    spread = x - jnp.mean(x, axis=-1, keepdims=True)
    inv = lax.rsqrt(jnp.mean(spread * spread, axis=-1, keepdims=True) + norm_eps)
    normed = (spread * inv * flat(n1g) + flat(n1s)).astype(jnp.bfloat16)
    normed_out[...] = normed
    swaps = [[Swap(n_seq, dp, sq, lambda to, t=t: sp.at[to, t], lambda me, t=t: rp.at[t, pl.ds(me * rows, rows)],
                   lambda d, t=t: ssem.at[0, t, d], lambda d, t=t: rsem.at[0, t, d]),
              Swap(n_seq, dp, sq, lambda to, t=t: st.at[to, t], lambda me, t=t: rt.at[t, me],
                   lambda d, t=t: ssem.at[1, t, d], lambda d, t=t: rsem.at[1, t, d])] for t in range(2)]
    swaps.append([Gather(n_seq, dp, sq, lambda to: sp.at[to, 2], lambda s: rp.at[2, pl.ds(s * rows, rows)],
                         lambda i: ssem.at[0, 2, i], lambda i: rsem.at[0, 2, i]),
                  Gather(n_seq, dp, sq, lambda to: st.at[to, 2], lambda s: rt.at[2, s],
                         lambda i: ssem.at[1, 2, i], lambda i: rsem.at[1, 2, i])])

    def lanes_of(v, tile):
        return v[:, tile * LANES : (tile + 1) * LANES]

    def place(t, r, pair, tile):
        sp[r, t] = pair
        st[r, t] = pack_third(tile[:half], tile[half:], r % 2)

    fresh_tiles = VFRESH // LANES
    reused = [r for r in range(n_seq) if PAIR_TILE[r] >= fresh_tiles]
    for r in reused:
        place(2, r, lanes_of(skip, PAIR_TILE[r] - fresh_tiles), lanes_of(skip, THIRD_TILE[r] - fresh_tiles))
    pl.semaphore_wait(barrier, n_seq - 1)
    for r in reused:
        swaps[2][0].start(r)
    for t in range(3):
        if t == 0:
            full = (matmul(normed, qw[...]) + flat(qb)).astype(jnp.bfloat16)
        elif t == 1:
            full = matmul(normed, kw[...]).astype(jnp.bfloat16)
        else:
            full = (matmul(normed, vw[...]) + flat(vb)).astype(jnp.bfloat16)
        for r in range(n_seq):
            if t < 2 or r not in reused:
                place(t, r, lanes_of(full, PAIR_TILE[r]), lanes_of(full, THIRD_TILE[r]))
        if t < 2:
            swaps[t][0].start()
        else:
            for r in range(n_seq):
                if r not in reused:
                    swaps[2][0].start(r)
    for t in range(3):
        if t < 2:
            swaps[t][1].start()
        else:
            for r in range(n_seq):
                swaps[2][1].start(r)
        rp[t, pl.ds(pl.multiple_of(sq * rows, rows), rows)] = sp[sq, t]
        rt[t, sq] = st[sq, t]
    for i in range(n_seq):
        cols = (i + 1) * rows
        bias[i * rows : (i + 1) * rows, 0:cols] = mask_bias(lens, valid_row, i * rows, rows, cols)
    back = [Gather(n_seq, dp, sq, lambda to: smp.at[to], lambda s: rmp.at[s], lambda i: mssem.at[0, i], lambda i: mrsem.at[0, i]),
            Gather(n_seq, dp, sq, lambda to: smt.at[to], lambda s: rmt.at[s], lambda i: mssem.at[1, i], lambda i: mrsem.at[1, i])]
    low = low_lanes()
    scale = 1.0 / math.sqrt(HDIM)
    keep = (jnp.where(low, scale, 0.0).astype(jnp.bfloat16), jnp.where(low, 0.0, scale).astype(jnp.bfloat16))

    def attend(q, k, v, block):
        scores = matmul_right_t(q, k) + block
        top = jnp.max(scores, axis=-1, keepdims=True)
        powered = jnp.exp(scores - top)
        total = jnp.sum(powered, axis=-1, keepdims=True)
        probs = (powered * (1.0 / total)).astype(jnp.bfloat16)
        return matmul(probs, v), top + jnp.log(total)

    for t in range(3):
        swaps[t][0].wait()
    lane = lax.broadcasted_iota(jnp.int32, (1, LANES), 1)
    for i in range(n_seq):
        here = slice(i * rows, (i + 1) * rows)
        cols = (i + 1) * rows
        block = bias[here, 0:cols]
        q, k, v = rp[0, here], rp[1, 0:cols], rp[2, 0:cols]
        o0, l0 = attend(q * keep[0], k, v, block)
        o1, l1 = attend(q * keep[1], k, v, block)
        smp[i] = jnp.where(low, o0, o1).astype(jnp.bfloat16)
        lse_out[here] = jnp.where(lane == 0, l0, l1)
        back[0].start(i)
    for t in range(3):
        swaps[t][1].wait()
        for s in range(n_seq):
            a, b = unpack_third(rt[t, s])
            third_out[t, s * rows : s * rows + half] = a
            third_out[t, s * rows + half : (s + 1) * rows] = b
    for i in range(n_seq):
        here = slice(i * rows, (i + 1) * rows)
        cols = (i + 1) * rows
        block = bias[here, 0:cols]
        o2, l2 = attend(third_out[0, here] * keep[0], third_out[1, 0:cols], third_out[2, 0:cols], block)
        smt[i] = pack_third(o2[:half], o2[half:], False)
        lse_out[here] = jnp.where(lane == 2, l2, lse_out[here])
        back[1].start(i)
    pair_out[...] = rp[...]
    rmp[sq] = smp[sq]
    rmt[sq] = smt[sq]
    back[0].wait()
    back[1].wait()
    for r in range(n_seq):
        c = PAIR_TILE[r] * LANES
        mixed_out[:, c : c + LANES] = rmp[r]
    for r in range(0, n_seq, 2):
        a, b = join_thirds(rmt[r], rmt[r + 1])
        c = THIRD_TILE[r] * LANES
        mixed_out[0:half, c : c + LANES] = a
        mixed_out[half:rows, c : c + LANES] = b


def front(mesh, hidden, skip, lens, valid, n1g, n1s, qw, qb, kw, vw, vb, collective_id):
    n_dp, n_seq = mesh.shape["dp"], mesh.shape["seq"]
    rows, d = hidden.shape
    group = rows * n_seq
    bf, f32 = jnp.bfloat16, jnp.float32
    vmem = pl.BlockSpec(memory_space=pltpu.VMEM)
    half = rows // 2
    dma = pltpu.SemaphoreType.DMA
    return pl.pallas_call(
        functools.partial(front_kernel, (n_dp, n_seq)),
        in_specs=[pl.BlockSpec(memory_space=pltpu.SMEM)] + [vmem] * 10,
        out_specs=(vmem,) * 5,
        out_shape=(jax.ShapeDtypeStruct((rows, d), bf), jax.ShapeDtypeStruct((rows, d), bf),
                   jax.ShapeDtypeStruct((3, group, LANES), bf), jax.ShapeDtypeStruct((3, group, LANES), bf),
                   jax.ShapeDtypeStruct((group, LANES), f32)),
        scratch_shapes=[
            pltpu.VMEM((n_seq, 3, rows, LANES), bf), pltpu.VMEM((n_seq, 3, half, LANES), bf),
            pltpu.VMEM((3, group, LANES), bf), pltpu.VMEM((3, n_seq, half, LANES), bf),
            pltpu.VMEM((n_seq, rows, LANES), bf), pltpu.VMEM((n_seq, half, LANES), bf),
            pltpu.VMEM((n_seq, rows, LANES), bf), pltpu.VMEM((n_seq, half, LANES), bf),
            pltpu.VMEM((group, group), f32),
            dma((2, 3, n_seq)), dma((2, 3, n_seq)), dma((2, n_seq)), dma((2, n_seq))],
        compiler_params=pltpu.CompilerParams(collective_id=collective_id, has_side_effects=True, vmem_limit_bytes=56 * 2**20),
        name="front",
    )(lens, hidden, skip, valid.reshape(1, -1), n1g, n1s, qw, qb, kw, vw, vb)


GELU_A = 0.044715


def back_kernel(cfg, lens, valid_row, mixed, hidden, og, valid_col, proj_w, proj_b, n2g, n2s, fc_b, out_b, n1g, lse, normed,
                pair_in, third_in, fc_w, out_w, qw, kw, vw,
                out, output, grad_input, grad_skip, small_z, small_out,
                nt_ref, xhat_ref, mid_ref, mlp_acc, two_acc, inv_ref, wf, wo, pair, third, part1,
                gs, gst, gp, gt, gthird, bias, dk_acc, dv_acc, dsp, dst, drp, drt, rows_in, part2,
                recv, gat, sbuf, load_sem, gssem, grsem, dssem, drsem, send_sem, recv_sem, local_sem, ssend, srecv_sem):
    n_dp, n_seq, halves, streams, order, marks, steps = cfg
    dp, sq = lax.axis_index("dp"), lax.axis_index("seq")
    rows, d = hidden.shape
    half = rows // 2
    bf, f32 = jnp.bfloat16, jnp.float32
    barrier, count = entry_barrier(n_dp, n_seq, dp, sq, True)

    def weight_copies(j):
        cols = pl.ds(j * FCH, FCH)
        return [pltpu.make_async_copy(fc_w.at[:, cols], wf.at[j % 2], load_sem.at[0, j]),
                pltpu.make_async_copy(out_w.at[cols], wo.at[j % 2], load_sem.at[1, j])]

    extra = [pltpu.make_async_copy(pair_in, pair, load_sem.at[2, 0]), pltpu.make_async_copy(third_in, third, load_sem.at[2, 1])]
    late = [pltpu.make_async_copy(qw, wf.at[0], load_sem.at[3, 0]), pltpu.make_async_copy(kw, wf.at[1], load_sem.at[3, 1]),
            pltpu.make_async_copy(vw, wo.at[0, :, pl.ds(0, VFRESH)], load_sem.at[3, 2])]
    for j in range(2):
        for copy in weight_copies(j):
            copy.start()
    for copy in extra:
        copy.start()
    x = hidden[...].astype(f32)
    attn = matmul(mixed[...], proj_w[...]) + flat(proj_b)
    middle = x + attn
    mid_ref[...] = middle
    real = valid_col[...]
    spread = middle - jnp.mean(middle, axis=-1, keepdims=True)
    inv = lax.rsqrt(jnp.mean(spread * spread, axis=-1, keepdims=True) + norm_eps)
    xhat = spread * inv
    xhat_ref[...] = xhat
    inv_ref[...] = jnp.broadcast_to(inv, inv_ref.shape)
    nt_ref[...] = (xhat * flat(n2g) + flat(n2s)).astype(bf)
    s0 = row_sum(jnp.sum(x * x, axis=-1, keepdims=True) * real)
    s1 = row_sum(jnp.sum(attn * attn, axis=-1, keepdims=True) * real)
    s3 = row_sum(real)
    word = lax.broadcasted_iota(jnp.int32, (1, WID), 1)
    sums = jnp.where(word == 0, s0, jnp.where(word == 1, s1, jnp.where(word == 3, s3, 0.0)))
    sbuf[0] = jnp.zeros_like(sbuf[0])
    sbuf[0, 7:8] = row_sum(og[...].astype(f32))
    pl.semaphore_wait(barrier, count)
    ex = Exchange(streams, halves, dp, sq, (part1, part2), out, recv, gat, (send_sem, recv_sem, local_sem))
    tiny = Small(n_dp, n_seq, dp, sq, sbuf, ssend, srecv_sem, small_z, small_out)
    todo = list(order)
    mark = iter(marks)

    def advance():
        upto = next(mark)
        while todo and todo[0][0] <= upto:
            _, s, k = todo.pop(0)
            ex.step(s, k)

    def begin(phase, chunk):
        for s, st in enumerate(streams):
            if st[0] == phase and (chunk is None or st[5] == chunk):
                ex.start(s, 0)

    h1, h2 = halves
    for j in range(steps):
        for copy in weight_copies(j):
            copy.wait()
        slot = j % 2
        pre = matmul(nt_ref[...], wf[slot]) + fc_b[:, j * FCH : (j + 1) * FCH]
        sq_pre = pre * pre
        t = jnp.tanh(tanh_coef * (pre + GELU_A * sq_pre * pre))
        act = (0.5 * pre * (1.0 + t)).astype(bf)
        slope = 0.5 * (1.0 + t) + 0.5 * pre * (1.0 - t * t) * (tanh_coef * (1.0 + 3.0 * GELU_A * sq_pre))
        pre_grad = matmul_right_t(og[...], wo[slot]) * slope
        sbuf[0, 8 + j : 9 + j] = row_sum(pre_grad)
        pre_low = pre_grad.astype(bf)
        part1[j * CHUNK : (j + 1) * CHUNK] = matmul_left_t(act, og[...]).astype(bf).reshape(CHUNK, SUB, WID)
        part1[h1 + j * CHUNK : h1 + (j + 1) * CHUNK] = matmul_left_t(nt_ref[...], pre_low).astype(bf).reshape(CHUNK, SUB, WID)
        begin(0, j)
        mlp = matmul(act, wo[slot])
        two = matmul_right_t(pre_low, wf[slot])
        if j == 0:
            mlp_acc[...] = mlp
            two_acc[...] = two
        else:
            mlp_acc[...] = mlp_acc[...] + mlp
            two_acc[...] = two_acc[...] + two
        if j + 2 < steps:
            for copy in weight_copies(j + 2):
                copy.start()
        if j > 0 and j < steps - 1:
            advance()
    for copy in late:
        copy.start()
    two_grad = two_acc[...]
    xhat = xhat_ref[...]
    sbuf[0, 5:6] = row_sum(two_grad * xhat)
    sbuf[0, 6:7] = row_sum(two_grad)
    e = two_grad * flat(n2g)
    centre = jnp.mean(e, axis=-1, keepdims=True)
    along = jnp.mean(e * xhat, axis=-1, keepdims=True)
    grad = og[...].astype(f32) + (e - centre - xhat * along) * inv_ref[:, 0:1]
    grad_low = grad.astype(bf)
    full = matmul_right_t(grad_low, proj_w[...]).astype(bf)
    for r in range(n_seq):
        c = PAIR_TILE[r] * LANES
        gs[r] = full[:, c : c + LANES]
        c = THIRD_TILE[r] * LANES
        gst[r] = pack_third(full[:half, c : c + LANES], full[half:, c : c + LANES], r % 2)
    swap_pair = Swap(n_seq, dp, sq, lambda to: gs.at[to], lambda me: gp.at[pl.ds(me * rows, rows)], lambda i: gssem.at[0, i], lambda i: grsem.at[0, i])
    swap_third = Swap(n_seq, dp, sq, lambda to: gst.at[to], lambda me: gt.at[me], lambda i: gssem.at[1, i], lambda i: grsem.at[1, i])
    swap_pair.start()
    swap_third.start()
    mlp_out = mlp_acc[...] + flat(out_b)
    output[...] = (mid_ref[...] + mlp_out).astype(bf)
    s2 = row_sum(jnp.sum(mlp_out * mlp_out, axis=-1, keepdims=True) * valid_col[...])
    sbuf[0, 12:13] = sums + jnp.where(word == 2, s2, 0.0)
    sbuf[0, 4:5] = row_sum(grad)
    mid_ref[...] = grad
    gw = matmul_left_t(mixed[...], grad_low).astype(bf)
    top = d // 2 // SUB
    at = steps * CHUNK
    part1[at : at + top] = gw[: d // 2].reshape(top, SUB, WID)
    part1[h1 + at : h1 + at + top] = gw[d // 2 :].reshape(top, SUB, WID)
    if h1 > at + top:
        for h in range(2):
            part1[h * h1 + at + top : (h + 1) * h1] = jnp.zeros((h1 - at - top, SUB, WID), bf)
    begin(0, steps)
    advance()
    gp[pl.ds(pl.multiple_of(sq * rows, rows), rows)] = gs[sq]
    gt[sq] = gst[sq]
    for i in range(n_seq):
        cols = (i + 1) * rows
        bias[i * rows : (i + 1) * rows, 0:cols] = mask_bias(lens, valid_row, i * rows, rows, cols).astype(bf)
    send = [Gather(n_seq, dp, sq, lambda to: dsp.at[to], lambda s: drp.at[s], lambda i: dssem.at[0, i], lambda i: drsem.at[0, i]),
            Gather(n_seq, dp, sq, lambda to: dst.at[to], lambda s: drt.at[s], lambda i: dssem.at[1, i], lambda i: drsem.at[1, i])]
    advance()
    for copy in extra:
        copy.wait()
    low = low_lanes()
    scale = 1.0 / math.sqrt(HDIM)
    keep = (jnp.where(low, scale, 0.0).astype(bf), jnp.where(low, 0.0, scale).astype(bf))
    ones = (jnp.where(low, 1.0, 0.0).astype(bf), jnp.where(low, 0.0, 1.0).astype(bf))

    def backward(q, k, v, g, block, total):
        probs = jnp.exp(matmul_right_t(q, k) + block - total)
        prob_grad = matmul_right_t(g, v)
        centre = jnp.sum(probs * prob_grad, axis=-1, keepdims=True)
        score_grad = (probs * (prob_grad - centre)).astype(bf)
        return matmul(score_grad, k), matmul_left_t(score_grad, q), matmul_left_t(probs.astype(bf), g)

    swap_pair.wait()
    for i in reversed(range(n_seq)):
        here = slice(i * rows, (i + 1) * rows)
        cols = (i + 1) * rows
        block = bias[here, 0:cols].astype(f32)
        q, k, v, g = pair[0, here], pair[1, 0:cols], pair[2, 0:cols], gp[here]
        dq0, dk0, dv0 = backward(q * keep[0], k, v, g * ones[0], block, lse[here, 0:1])
        dq1, dk1, dv1 = backward(q * keep[1], k, v, g * ones[1], block, lse[here, 1:2])
        if i == n_seq - 1:
            dk_acc[...] = dk0 + dk1
            dv_acc[...] = dv0 + dv1
        else:
            dk_acc[0:cols] = dk_acc[0:cols] + (dk0 + dk1)
            dv_acc[0:cols] = dv_acc[0:cols] + (dv0 + dv1)
        dsp[i, 0] = (jnp.where(low, dq0, dq1) * scale).astype(bf)
        dsp[i, 1] = dk_acc[here].astype(bf)
        dsp[i, 2] = dv_acc[here].astype(bf)
        send[0].start(i)
        advance()
    swap_third.wait()
    for s in range(n_seq):
        a, b = unpack_third(gt[s])
        gthird[s * rows : s * rows + half] = a
        gthird[s * rows + half : (s + 1) * rows] = b
    for i in reversed(range(n_seq)):
        here = slice(i * rows, (i + 1) * rows)
        cols = (i + 1) * rows
        block = bias[here, 0:cols].astype(f32)
        dq, dk, dv = backward(third[0, here] * keep[0], third[1, 0:cols], third[2, 0:cols], gthird[here], block, lse[here, 2:3])
        if i == n_seq - 1:
            dk_acc[...] = dk
            dv_acc[...] = dv
        else:
            dk_acc[0:cols] = dk_acc[0:cols] + dk
            dv_acc[0:cols] = dv_acc[0:cols] + dv
        dq = dq * scale
        dst[i, 0] = pack_third(dq[:half], dq[half:], False)
        for t, a in ((1, dk_acc), (2, dv_acc)):
            dst[i, t] = pack_third(a[i * rows : i * rows + half], a[i * rows + half : (i + 1) * rows], False)
        send[1].start(i)
        advance()
    drp[sq] = dsp[sq]
    drt[sq] = dst[sq]
    x = hidden[...].astype(f32)
    spread = x - jnp.mean(x, axis=-1, keepdims=True)
    inv = lax.rsqrt(jnp.mean(spread * spread, axis=-1, keepdims=True) + norm_eps)
    xhat = spread * inv
    advance()
    send[0].wait()
    advance()
    send[1].wait()
    for t in range(3):
        for r in range(n_seq):
            c = PAIR_TILE[r] * LANES
            rows_in[t, :, c : c + LANES] = drp[r, t]
        for r in range(0, n_seq, 2):
            a, b = join_thirds(drt[r, t], drt[r + 1, t])
            c = THIRD_TILE[r] * LANES
            rows_in[t, 0:half, c : c + LANES] = a
            rows_in[t, half:rows, c : c + LANES] = b
    nl = normed[...]
    dq, dk, dv = rows_in[0], rows_in[1], rows_in[2]
    fresh = dv[:, 0:VFRESH]
    grad_skip[...] = dv[:, VFRESH:]
    units_d = d // SUB
    uv = d // 4 // SUB
    part2[0:units_d] = matmul_left_t(nl, dq).astype(bf).reshape(units_d, SUB, WID)
    part2[h2 : h2 + units_d] = matmul_left_t(nl, dk).astype(bf).reshape(units_d, SUB, WID)
    gv = matmul_left_t(nl, fresh).astype(bf)
    for h in range(2):
        for side in range(2):
            r0 = side * (d // 2) + h * (d // 4)
            part2[h * h2 + units_d : h * h2 + units_d + uv, :, side * VFRESH : (side + 1) * VFRESH] = (
                gv[r0 : r0 + d // 4].reshape(uv, SUB, VFRESH))
        if h2 > units_d + uv:
            part2[h * h2 + units_d + uv : (h + 1) * h2] = jnp.zeros((h2 - units_d - uv, SUB, WID), bf)
    begin(1, None)
    advance()
    for copy in late:
        copy.wait()
    normed_grad = matmul_right_t(dq, wf[0]) + matmul_right_t(dk, wf[1]) + matmul_right_t(fresh, wo[0, :, 0:VFRESH])
    f = normed_grad * flat(n1g)
    centre = jnp.mean(f, axis=-1, keepdims=True)
    along = jnp.mean(f * xhat, axis=-1, keepdims=True)
    grad_input[...] = (mid_ref[...] + (f - centre - xhat * along) * inv).astype(bf)
    sbuf[0, 0:1] = row_sum(normed_grad * xhat)
    sbuf[0, 1:2] = row_sum(normed_grad)
    sbuf[0, 2:3] = row_sum(dq.astype(f32))
    sbuf[0, 3:4, 0:VFRESH] = row_sum(fresh.astype(f32))
    tiny.copy(0).start()
    gap = max(1, len(todo) // (len(tiny.dims) + 2))
    left = 0
    while todo:
        _, s, k = todo.pop(0)
        ex.step(s, k)
        left += 1
        if left % gap == 0:
            tiny.step()
    tiny.rest()


def back(mesh, lens, valid, mixed, hidden, og, valid_col, proj_w, proj_b, n2g, n2s, fc_b, out_b, n1g, lse, normed,
         pair, third, fc_w, out_w, qw, kw, vw, collective_id):
    n_dp, n_seq = mesh.shape["dp"], mesh.shape["seq"]
    rows, d = hidden.shape
    group = rows * n_seq
    half = rows // 2
    steps = fc_w.shape[1] // FCH
    bf, f32 = jnp.bfloat16, jnp.float32
    quantum = n_dp // 2 * n_seq
    needed = (steps * CHUNK + d // 2 // SUB, d // SUB + d // 4 // SUB)
    halves = tuple(-(-n // quantum) * quantum for n in needed)
    streams = plan_streams(n_dp, n_seq, halves, steps)
    order = schedule(streams)
    n_st = 2 * (bits_of(n_dp) + bits_of(n_seq))
    n_small = bits_of(n_dp) + bits_of(n_seq)
    ns = len(streams)
    vmem = pl.BlockSpec(memory_space=pltpu.VMEM)
    hbm = pl.BlockSpec(memory_space=pl.ANY)
    dma = pltpu.SemaphoreType.DMA
    units = lambda n: pltpu.VMEM((n, SUB, WID), bf)
    wide = lambda: pltpu.VMEM((rows, d), f32)
    sshape = jax.ShapeDtypeStruct((16, WID), f32)
    args = (lens, valid.reshape(1, -1), mixed, hidden, og, valid_col, proj_w, proj_b, n2g, n2s, fc_b.reshape(1, -1), out_b, n1g, lse, normed,
            pair, third, fc_w, out_w, qw, kw, vw)
    outs = pl.pallas_call(
        functools.partial(back_kernel, (n_dp, n_seq, halves, streams, order, MARKS, steps)),
        in_specs=[pl.BlockSpec(memory_space=pltpu.SMEM)] + [vmem] * 14 + [hbm] * 7,
        out_specs=(hbm, vmem, vmem, vmem, vmem, vmem),
        out_shape=(jax.ShapeDtypeStruct((2 * sum(halves), SUB, WID), bf), jax.ShapeDtypeStruct((rows, d), bf),
                   jax.ShapeDtypeStruct((rows, d), bf), jax.ShapeDtypeStruct((rows, d - VFRESH), bf), sshape, sshape),
        scratch_shapes=[
            pltpu.VMEM((rows, d), bf), wide(), wide(), wide(), wide(), pltpu.VMEM((rows, LANES), f32),
            pltpu.VMEM((2, d, FCH), bf), pltpu.VMEM((2, FCH, d), bf),
            pltpu.VMEM((3, group, LANES), bf), pltpu.VMEM((3, group, LANES), bf), units(2 * halves[0]),
            pltpu.VMEM((n_seq, rows, LANES), bf), pltpu.VMEM((n_seq, half, LANES), bf),
            pltpu.VMEM((group, LANES), bf), pltpu.VMEM((n_seq, half, LANES), bf), pltpu.VMEM((group, LANES), bf),
            pltpu.VMEM((group, group), bf), pltpu.VMEM((group, LANES), f32), pltpu.VMEM((group, LANES), f32),
            pltpu.VMEM((n_seq, 3, rows, LANES), bf), pltpu.VMEM((n_seq, 3, half, LANES), bf),
            pltpu.VMEM((n_seq, 3, rows, LANES), bf), pltpu.VMEM((n_seq, 3, half, LANES), bf),
            pltpu.VMEM((3, rows, d), bf), units(2 * halves[1]),
            units(Exchange.recv_total(streams)), units(sum(halves)),
            pltpu.VMEM((2 * n_small, 16, WID), f32), dma((4, max(4, steps))),
            dma((2, n_seq)), dma((2, n_seq)), dma((2, n_seq)), dma((2, n_seq)),
            dma((ns, n_st)), dma((ns, n_st)), dma((ns,)), dma((n_small,)), dma((n_small,))],
        compiler_params=pltpu.CompilerParams(collective_id=collective_id, has_side_effects=True, vmem_limit_bytes=67043328),
        name="back",
    )(*args)
    return outs, halves


def local(
    mesh,
    hidden_in,
    skip_values,
    out_grad,
    doc_lens,
    valid,
    norm1_gain,
    norm1_shift,
    query_w,
    query_b,
    key_w,
    value_w,
    value_b,
    proj_w,
    proj_b,
    norm2_gain,
    norm2_shift,
    fc_w,
    fc_b,
    out_w,
    out_b,
):
    seq_size = lax.axis_size("seq")
    seq_rank = lax.axis_index("seq")
    tok_rows = hidden_in.shape[0]
    valid_col = lax.dynamic_slice_in_dim(valid, seq_rank * tok_rows, tok_rows, 0).astype(jnp.float32)[:, None]
    normed, mixed, pair, third, lse = front(
        mesh, hidden_in, skip_values, doc_lens, valid, norm1_gain, norm1_shift, query_w, query_b, key_w, value_w, value_b, 0
    )
    (summed, output, grad_input, grad_skip, small_z, small_all), halves = back(
        mesh, doc_lens, valid, mixed, hidden_in, out_grad, valid_col, proj_w, proj_b, norm2_gain, norm2_shift, fc_b, out_b,
        norm1_gain, lse, normed, pair, third, fc_w, out_w, query_w, key_w, value_w, 1
    )
    (
        grad_out_w, grad_fc_w, grad_proj_w, grad_query_w, grad_key_w, grad_value_w,
        grad_norm1_gain, grad_norm1_shift, grad_query_b, grad_value_b, grad_proj_b, grad_norm2_gain, grad_norm2_shift,
        grad_out_b, grad_fc_b, norm_values, grad_input, grad_skip,
    ) = widen(summed.reshape(-1, WID), small_all, small_z, grad_input, grad_skip, halves, D, fc_w.shape[1], VFRESH)
    return (
        output,
        grad_input,
        grad_skip,
        grad_norm1_gain,
        grad_norm1_shift,
        grad_query_w,
        grad_query_b,
        grad_key_w,
        grad_value_w,
        grad_value_b,
        grad_proj_w,
        grad_proj_b,
        grad_norm2_gain,
        grad_norm2_shift,
        grad_fc_w,
        grad_fc_b,
        grad_out_w,
        grad_out_b,
        norm_values,
    )


def solution(mesh):
    placed = (
        P(("dp", "seq"), None),
        P(("dp", "seq"), None),
        P(("dp", "seq"), None),
        P("dp", None),
        P("dp"),
        P(),
        P(),
        P(),
        P(),
        P(),
        P(),
        P(),
        P(),
        P(),
        P(),
        P(),
        P(),
        P(),
        P(),
        P(),
    )
    return jax.shard_map(
        functools.partial(local, mesh),
        mesh=mesh,
        in_specs=placed,
        out_specs=(
            P(("dp", "seq"), None),
            P(("dp", "seq"), None),
            P(("dp", "seq"), None),
            P(),
            P(),
            P(),
            P(),
            P(),
            P(),
            P(),
            P(),
            P(),
            P(),
            P(),
            P(),
            P(),
            P(),
            P(),
            P("dp", None),
        ),
        check_vma=False,
    )
```

```python
import functools
import math

import jax
import jax.numpy as jnp
from jax import lax
from jax.experimental import pallas as pl
from jax.experimental.pallas import tpu as pltpu
from jax.sharding import PartitionSpec as P

D = 768
HEADS = 12
HDIM = 64
VFRESH = 384


norm_eps = 1e-05
square_eps = 1e-06
tanh_coef = 0.7978845608028654
masked_score = -1e30


MESH = pl.DeviceIdType.MESH
SUB = 8
WID = 768
UNIT_BYTES = SUB * WID * 2
FCH = 768
CHUNK = FCH // SUB
MLP_TIMES = (2.2, 1.1)
TASKS = (2.5, 2.5, 1.5, 2.3, 1.7, 1.2, 0.7, 1.6, 0.9, 0.7, 0.5, 0.8, 4.5, 3.0)
ENTRY = 3.5
MARGIN = 0.5
SIZES = ((2,) * 12 + (3,), (2,) * 4)
KINDS = (1, 1, 0, 0, 1, 1, 0, 0, 1, 1, 0, 1, 0, 2, 2, 3, 1)
HOLDS = (38.3, 64.6, 49.9, 44.9, 39.2, 11.0, 0.0, 28.0, 2.6, 7.4, 2.0, 55.0, 54.9, 0.0, 71.8, 28.5, 11.9)
LINK = 0.045
LATENCY = 2.0
AR_COST = 0.25


def bits_of(n):
    return n.bit_length() - 1


def partner(dim, dp, sq):
    kind, j = dim
    step = 1 << j
    if kind == "dp":
        bit = (dp // step) % 2
        return bit, (dp + step - 2 * step * bit, sq)
    bit = (sq // step) % 2
    return bit, (dp, sq + step - 2 * step * bit)


def plan_streams(n_dp, n_seq, halves, steps):
    dpb = [("dp", j) for j in range(1, bits_of(n_dp))]
    sqb = [("seq", j) for j in range(bits_of(n_seq))]
    mid = len(dpb) // 2
    one, two = dpb[:mid], dpb[mid:]
    orders = (one + two + sqb, two + one + sqb, one + sqb + two, two + sqb + one, sqb + one + two, sqb + two + one)
    quantum = (n_dp // 2) * n_seq
    streams = []
    for phase, half_units in enumerate(halves):
        total = half_units // quantum
        sizes = SIZES[phase]
        if sum(sizes) != total:
            sizes = (2,) * (total // 2) + (1,) * (total % 2)
        first = 0
        for size in sizes:
            n = size * quantum
            chunk = min(steps, (first + n - 1) // CHUNK)
            streams.append((phase, first, n, orders[KINDS[len(streams) % len(KINDS)]], chunk if phase == 0 else -1))
            first += n
    return streams


def schedule(streams, steps, rows):
    free = {}
    stages = []
    for phase, first, n, order, _ in streams:
        seq = [(("dp", 0), n)]
        size = n
        for d in order:
            size //= 2
            seq.append((d, size))
        for d in reversed(order):
            seq.append((d, size))
            size *= 2
        stages.append(seq + [(("dp", 0), n)])

    def flow(needs, t):
        begin = max([t] + [free.get(r, 0.0) for r, _ in needs])
        for r, dur in needs:
            free[r] = begin + dur
        return begin + max(dur for _, dur in needs) + LATENCY

    flying = []

    def launch(s, k, t):
        d, size = stages[s][k]
        b = size * UNIT_BYTES / 1e6
        if d == ("dp", 0):
            needs = [("c", b / 0.5)]
        elif d[0] == "dp":
            needs = [(d, b / LINK)]
        elif d[1] == 0:
            needs = [("end", b / LINK)]
        else:
            needs = [("mid", 2 * b / LINK), ("end", b / LINK)]
        end = flow(needs, t)
        flying.append((max(end, HOLDS[s % len(HOLDS)]) if k == 0 else end, s, k))

    block = rows * LANES * 2 / 1e6 / LINK
    arrive = {}
    durations = [MLP_TIMES[i % 2] for i in range(2 * steps)] + list(TASKS)
    n_tasks = len(durations)
    plan = [[] for _ in range(n_tasks + 1)]
    t, task = ENTRY, 0
    while task < n_tasks or flying:
        ready = None
        at_task = task - 2 * steps
        if task < n_tasks:
            needs = {3: ("grad pair",), 7: ("grad third",), 11: ("pair",), 12: ("third",)}.get(at_task, ())
            ready = max([0.0] + [arrive[x] for x in needs])
        flying.sort()
        arrived = flying and flying[0][0] + MARGIN <= t
        if ready is not None and not arrived and (ready <= t or not flying or ready <= flying[0][0]):
            t = max(t, ready) + durations[task]
            begun = []
            if at_task < 0 and task % 2 == 0:
                begun = [s for s, st in enumerate(streams) if st[0] == 0 and st[4] == task // 2]
            if at_task == 0:
                arrive["grad pair"] = flow([("mid", 4 * block), ("end", 3 * block)], t)
                arrive["grad third"] = flow([("mid", 2 * block), ("end", 1.5 * block)], t)
            if at_task == 1:
                begun = [s for s, st in enumerate(streams) if st[0] == 0 and st[4] == steps]
            if 3 <= at_task <= 6:
                arrive["pair"] = flow([("mid", 3 * block), ("end", 2.25 * block)], t) + 2.0
            if 7 <= at_task <= 10:
                arrive["third"] = flow([("mid", 1.5 * block), ("end", 1.125 * block)], t) + 2.0
            if at_task == 12:
                begun = [s for s, st in enumerate(streams) if st[0] == 1]
            for s in begun:
                launch(s, 0, t)
            task += 1
            continue
        at, s, k = flying.pop(0)
        plan[task].append((s, k))
        t = max(t, at) + AR_COST
        if k + 1 < len(stages[s]):
            launch(s, k + 1, t)
    return plan, t


class Exchange:
    def __init__(self, streams, halves, dp, sq, parts, out, recv, gat, sems):
        self.streams, self.halves = streams, halves
        self.dp, self.sq = dp, sq
        self.parts, self.out, self.recv, self.gat = parts, out, recv, gat
        self.send_sem, self.recv_sem, self.local_sem = sems
        self.cbit, self.cdev = partner(("dp", 0), dp, sq)
        self.base = [sum(halves[:p]) for p in range(len(halves))]
        self.off = [[st[1]] for st in streams]
        self.roff = []
        r = 0
        for phase, first, n, order, _ in streams:
            rows = [r]
            r += n
            size = n
            for _ in order:
                size //= 2
                rows.append(r)
                r += size
            self.roff.append(rows)

    @staticmethod
    def recv_total(streams):
        r = 0
        for phase, first, n, order, _ in streams:
            r += n
            for i in range(len(order)):
                r += n >> (i + 1)
        return r

    def n_stages(self, s):
        return 2 * (len(self.streams[s][3]) + 1)

    def remote(self, s, k, src, dst, dev):
        return pltpu.make_async_remote_copy(
            src_ref=src, dst_ref=dst, send_sem=self.send_sem.at[s, k], recv_sem=self.recv_sem.at[s, k],
            device_id=dev, device_id_type=MESH)

    def copies(self, s, k):
        phase, first, n, order, _ = self.streams[s]
        depth = len(order)
        half_units, base = self.halves[phase], self.base[phase]
        part = self.parts[phase]
        own = self.cbit * half_units
        if k == 0:
            other = (1 - self.cbit) * half_units + first
            return self.remote(s, k, part.at[pl.ds(other, n)], self.recv.at[pl.ds(self.roff[s][0], n)], self.cdev), None
        if k <= depth:
            half = n >> k
            bit, dev = partner(order[k - 1], self.dp, self.sq)
            at = own + self.off[s][k - 1] + (1 - bit) * half
            return self.remote(s, k, part.at[pl.ds(at, half)], self.recv.at[pl.ds(self.roff[s][k], half)], dev), None
        g = 2 * depth + 1 - k
        if g >= 1:
            half = n >> g
            bit, dev = partner(order[g - 1], self.dp, self.sq)
            piece = self.gat.at[pl.ds(base + self.off[s][g], half)]
            return self.remote(s, k, piece, piece, dev), None
        piece = self.gat.at[pl.ds(base + first, n)]
        there = self.out.at[pl.ds(2 * base + own + first, n)]
        return self.remote(s, k, piece, there, self.cdev), pltpu.make_async_copy(piece, there, self.local_sem.at[s])

    def start(self, s, k):
        for c in self.copies(s, k):
            if c is not None:
                c.start()

    def finish(self, s, k):
        phase, first, n, order, _ = self.streams[s]
        depth = len(order)
        remote, local = self.copies(s, k)
        remote.wait()
        if local is not None:
            local.wait()
        if k <= depth:
            half = n >> k
            if k > 0:
                bit, _ = partner(order[k - 1], self.dp, self.sq)
                self.off[s].append(self.off[s][k - 1] + bit * half)
            at = self.cbit * self.halves[phase] + self.off[s][k]
            to = (self.gat, self.base[phase] + self.off[s][k]) if k == depth else (self.parts[phase], at)
            self.add(self.parts[phase], at, self.roff[s][k], half, to)

    def add(self, part, at, roff, n, to):
        recv = self.recv
        dst, first = to
        step = next(d for d in (8, 6, 4, 3, 2, 1) if n % d == 0)

        def body(i, c):
            a = pl.ds(at + i * step, step)
            b = pl.ds(roff + i * step, step)
            dst[pl.ds(first + i * step, step)] = part[a] + recv[b]
            return c

        lax.fori_loop(0, n // step, body, 0)

    def step(self, s, k):
        self.finish(s, k)
        if k + 1 < self.n_stages(s):
            self.start(s, k + 1)


class Small:
    def __init__(self, n_dp, n_seq, dp, sq, buf, ssend, srecv, small_z, small_out):
        self.dims = [("seq", j) for j in range(bits_of(n_seq))] + [("dp", j) for j in range(bits_of(n_dp))]
        self.nz = bits_of(n_seq)
        self.dp, self.sq, self.buf, self.ssend, self.srecv = dp, sq, buf, ssend, srecv
        self.small_z, self.small_out = small_z, small_out
        self.done = 0

    def copy(self, i):
        _, dev = partner(self.dims[i], self.dp, self.sq)
        return pltpu.make_async_remote_copy(
            src_ref=self.buf.at[2 * i], dst_ref=self.buf.at[2 * i + 1], send_sem=self.ssend.at[i],
            recv_sem=self.srecv.at[i], device_id=dev, device_id_type=MESH)

    def begin(self, value):
        self.buf[0] = value
        self.copy(0).start()

    def step(self):
        i = self.done
        if i == len(self.dims):
            return
        self.copy(i).wait()
        total = self.buf[2 * i] + self.buf[2 * i + 1]
        self.done = i + 1
        if self.done == self.nz:
            self.small_z[...] = total
        if self.done < len(self.dims):
            self.buf[2 * self.done] = total
            self.copy(self.done).start()
        else:
            self.small_out[...] = total

    def rest(self):
        while self.done < len(self.dims):
            self.step()


def entry_barrier(n_dp, n_seq, dp, sq, all_seq):
    barrier = pltpu.get_barrier_semaphore()
    peers = [partner(("dp", j), dp, sq)[1] for j in range(bits_of(n_dp))]
    if all_seq:
        peers += [(dp, (sq + d) % n_seq) for d in range(1, n_seq)]
    else:
        peers += [partner(("seq", j), dp, sq)[1] for j in range(bits_of(n_seq))]
    for dev in peers:
        pl.semaphore_signal(barrier, inc=1, device_id=dev, device_id_type=MESH)
    return barrier, len(peers)


def matmul(former, latter):
    return jnp.dot(former, latter, preferred_element_type=jnp.float32)


def matmul_right_t(former, latter):
    return lax.dot_general(
        former, latter, (((1,), (1,)), ((), ())), preferred_element_type=jnp.float32
    )


def matmul_left_t(former, latter):
    return lax.dot_general(
        former, latter, (((0,), (0,)), ((), ())), preferred_element_type=jnp.float32
    )


def flat(ref):
    return ref[...].reshape(1, -1)


def row_sum(v):
    return jnp.sum(v, axis=0, keepdims=True)


PIECE = 384
VPIECE = 192


def widen_kernel(cfg, src, small, small_z, gi_in, gs_in, *refs):
    pieces, n_out = cfg
    outs, vectors, (norms, gi_out, gs_out) = refs[:n_out], refs[n_out : n_out + 9], refs[n_out + 9 : n_out + 12]
    inbuf, stage, gi_buf, gs_buf, in_sem, out_sem, row_sem = refs[n_out + 12 :]
    depth = inbuf.shape[0]

    def fetch(i):
        size = VPIECE if pieces[i][4] else PIECE
        return pltpu.make_async_copy(src.at[pl.ds(pieces[i][0], size)], inbuf.at[i % depth, pl.ds(0, size)], in_sem.at[i % depth])

    def put(i):
        slot = i % depth
        _, which, row, col, split = pieces[i]
        out = outs[which]
        if split:
            return [pltpu.make_async_copy(stage.at[slot, pl.ds(0, VPIECE), pl.ds(h * VFRESH, VFRESH)],
                                          out.at[pl.ds(row + h * VFRESH, VPIECE)], out_sem.at[slot, h]) for h in range(2)]
        return [pltpu.make_async_copy(stage.at[slot], out.at[pl.ds(row, PIECE), pl.ds(col, WID)], out_sem.at[slot, 0])]

    n = len(pieces)
    for i in range(min(depth, n)):
        fetch(i).start()
    row_in = [pltpu.make_async_copy(gi_in, gi_buf, row_sem.at[0]), pltpu.make_async_copy(gs_in, gs_buf, row_sem.at[1])]
    row_out = [pltpu.make_async_copy(gi_buf, gi_out, row_sem.at[2]), pltpu.make_async_copy(gs_buf, gs_out, row_sem.at[3])]
    for c in row_in:
        c.start()
    for i in range(n):
        slot = i % depth
        fetch(i).wait()
        if i >= depth:
            for c in put(i - depth):
                c.wait()

        def body(r, c):
            rows = pl.ds(r * 32, 32)
            stage[slot, rows] = inbuf[slot, rows].astype(jnp.float32)
            return c

        lax.fori_loop(0, (VPIECE if pieces[i][4] else PIECE) // 32, body, 0)
        for c in put(i):
            c.start()
        if i + depth < n:
            fetch(i + depth).start()
        if i == depth:
            for a, b in zip(row_in, row_out):
                a.wait()
                b.start()
            for row, v in zip((0, 1, 2, 3, 4, 5, 6, 7), vectors):
                v[...] = small[row, 0 : v.shape[0]]
            for q in range(vectors[8].shape[0] // WID):
                vectors[8][q * WID : (q + 1) * WID] = small[8 + q, :]
            sums = small_z[12:13, 0:4]
            norms[...] = jnp.sqrt(sums[:, 0:3] / (sums[:, 3:4] * D) + square_eps)
    for i in range(max(0, n - depth), n):
        for c in put(i):
            c.wait()
    for c in row_out:
        c.wait()


def widen(summed, small, small_z, grad_input, grad_skip, halves, d, ff, vf):
    one, two = halves[0] * SUB, halves[1] * SUB
    pieces = []
    for j in range(ff // PIECE):
        pieces.append((j * PIECE, 0, j * PIECE, 0, False))
        pieces.append((one + j * PIECE, 1, (j % 2) * PIECE, j // 2 * FCH, False))
    for h in range(2):
        pieces.append((h * one + ff, 2, h * PIECE, 0, False))
    for w in range(2):
        for h in range(2):
            pieces.append((2 * one + w * two + h * PIECE, 3 + w, h * PIECE, 0, False))
    for h in range(2):
        pieces.append((2 * one + h * two + d, 5, h * VPIECE, 0, True))
    f32, bf = jnp.float32, jnp.bfloat16
    depth = 4
    hbm = pl.BlockSpec(memory_space=pl.ANY)
    vmem = pl.BlockSpec(memory_space=pltpu.VMEM)
    shapes = [(ff, d), (d, ff), (d, d), (d, d), (d, d), (d, vf)]
    vectors = [(d,), (d,), (d,), (vf,), (d,), (d,), (d,), (d,), (ff,)]
    out_shape = [jax.ShapeDtypeStruct(s, f32) for s in shapes + vectors + [(1, 3)]]
    out_shape += [jax.ShapeDtypeStruct(g.shape, bf) for g in (grad_input, grad_skip)]
    return pl.pallas_call(
        functools.partial(widen_kernel, (pieces, len(shapes))),
        in_specs=[hbm, vmem, vmem, hbm, hbm], out_specs=(hbm,) * 6 + (vmem,) * 10 + (hbm,) * 2, out_shape=tuple(out_shape),
        scratch_shapes=[pltpu.VMEM((depth, PIECE, WID), bf), pltpu.VMEM((depth, PIECE, WID), f32),
                        pltpu.VMEM(grad_input.shape, bf), pltpu.VMEM(grad_skip.shape, bf),
                        pltpu.SemaphoreType.DMA((depth,)), pltpu.SemaphoreType.DMA((depth, 2)), pltpu.SemaphoreType.DMA((4,))],
        compiler_params=pltpu.CompilerParams(vmem_limit_bytes=62 * 2**20),
        name="widen",
    )(summed, small, small_z, grad_input, grad_skip)


LANES = 128
PAIR_TILE = (0, 2, 3, 5)
THIRD_TILE = (1, 1, 4, 4)


def low_lanes():
    return lax.broadcasted_iota(jnp.int32, (1, LANES), 1) < HDIM


def turn(v):
    return pltpu.roll(v, HDIM, 1)


def pack_third(first, second, upper):
    first, second = first.astype(jnp.float32), second.astype(jnp.float32)
    if upper:
        both = jnp.where(low_lanes(), turn(first), second)
    else:
        both = jnp.where(low_lanes(), first, turn(second))
    return both.astype(jnp.bfloat16)


def unpack_third(both):
    wide = both.astype(jnp.float32)
    low = low_lanes()
    first = jnp.where(low, wide, 0.0).astype(jnp.bfloat16)
    second = jnp.where(low, turn(wide), 0.0).astype(jnp.bfloat16)
    return first, second


def join_thirds(one, two):
    one, two = one.astype(jnp.float32), two.astype(jnp.float32)
    low = low_lanes()
    first = jnp.where(low, one, turn(two)).astype(jnp.bfloat16)
    second = jnp.where(low, turn(one), two).astype(jnp.bfloat16)
    return first, second


def split_tiles(tiles, pair_dst, third_dst, rows, n_seq):
    half = rows // 2
    for r in range(n_seq):
        pair_dst(r, tiles[PAIR_TILE[r]])
        t = tiles[THIRD_TILE[r]]
        third_dst(r, pack_third(t[:half], t[half:], r % 2))


def mask_bias(lens, valid_row, first, rows, cols):
    one = lens[0, 0]
    two = one + lens[0, 1]
    i = first + lax.broadcasted_iota(jnp.int32, (rows, 1), 0)
    j = lax.broadcasted_iota(jnp.int32, (1, cols), 1)
    seg_i = (i >= one).astype(jnp.int32) + (i >= two).astype(jnp.int32)
    seg_j = (j >= one).astype(jnp.int32) + (j >= two).astype(jnp.int32)
    real = valid_row[:, 0:cols] > 0
    code = jnp.where(real, seg_j, -1)
    same = (code == seg_i) & (j <= i)
    return jnp.where(same | (i == j), 0.0, masked_score)


class Swap:
    def __init__(self, n_seq, dp, sq, send, recv, ssem, rsem):
        self.n_seq, self.dp, self.sq = n_seq, dp, sq
        self.send, self.recv, self.ssem, self.rsem = send, recv, ssem, rsem

    def copy(self, d):
        to = (self.sq + d) % self.n_seq
        return pltpu.make_async_remote_copy(
            src_ref=self.send(to), dst_ref=self.recv(self.sq), send_sem=self.ssem(d), recv_sem=self.rsem(d),
            device_id=(self.dp, to), device_id_type=MESH)

    def start(self):
        for d in range(1, self.n_seq):
            self.copy(d).start()

    def wait(self):
        for d in range(1, self.n_seq):
            self.copy(d).wait()


class Gather:
    def __init__(self, n_seq, dp, sq, send, recv, ssem, rsem):
        self.n_seq, self.dp, self.sq = n_seq, dp, sq
        self.send, self.recv, self.ssem, self.rsem = send, recv, ssem, rsem

    def copy(self, to, slot):
        return pltpu.make_async_remote_copy(
            src_ref=self.send(to), dst_ref=self.recv(slot), send_sem=self.ssem(to), recv_sem=self.rsem(slot),
            device_id=(self.dp, to), device_id_type=MESH)

    def start(self, to):
        @pl.when(self.sq != to)
        def _():
            self.copy(to, self.sq).start()

    def wait(self):
        for i in range(self.n_seq):
            @pl.when(self.sq != i)
            def _():
                self.copy(i, i).wait()


def front_kernel(cfg, lens, hidden, skip, valid_row, n1g, n1s, qw, qb, kw, vw, vb,
                 normed_out, mixed_out, pair_out, third_out, lse_out,
                 sp, st, rp, rt, smp, smt, rmp, rmt, bias, ssem, rsem, mssem, mrsem):
    n_dp, n_seq = cfg
    dp, sq = lax.axis_index("dp"), lax.axis_index("seq")
    rows = hidden.shape[0]
    half = rows // 2
    barrier = pltpu.get_barrier_semaphore()
    for d in range(1, n_seq):
        pl.semaphore_signal(barrier, inc=1, device_id=(dp, (sq + d) % n_seq), device_id_type=MESH)
    x = hidden[...].astype(jnp.float32)
    spread = x - jnp.mean(x, axis=-1, keepdims=True)
    inv = lax.rsqrt(jnp.mean(spread * spread, axis=-1, keepdims=True) + norm_eps)
    normed = (spread * inv * flat(n1g) + flat(n1s)).astype(jnp.bfloat16)
    normed_out[...] = normed
    swaps = [[Swap(n_seq, dp, sq, lambda to, t=t: sp.at[to, t], lambda me, t=t: rp.at[t, pl.ds(me * rows, rows)],
                   lambda d, t=t: ssem.at[0, t, d], lambda d, t=t: rsem.at[0, t, d]),
              Swap(n_seq, dp, sq, lambda to, t=t: st.at[to, t], lambda me, t=t: rt.at[t, me],
                   lambda d, t=t: ssem.at[1, t, d], lambda d, t=t: rsem.at[1, t, d])] for t in range(2)]
    swaps.append([Gather(n_seq, dp, sq, lambda to: sp.at[to, 2], lambda s: rp.at[2, pl.ds(s * rows, rows)],
                         lambda i: ssem.at[0, 2, i], lambda i: rsem.at[0, 2, i]),
                  Gather(n_seq, dp, sq, lambda to: st.at[to, 2], lambda s: rt.at[2, s],
                         lambda i: ssem.at[1, 2, i], lambda i: rsem.at[1, 2, i])])

    def lanes_of(v, tile):
        return v[:, tile * LANES : (tile + 1) * LANES]

    def place(t, r, pair, tile):
        sp[r, t] = pair
        st[r, t] = pack_third(tile[:half], tile[half:], r % 2)

    fresh_tiles = VFRESH // LANES
    reused = [r for r in range(n_seq) if PAIR_TILE[r] >= fresh_tiles]
    for r in reused:
        place(2, r, lanes_of(skip, PAIR_TILE[r] - fresh_tiles), lanes_of(skip, THIRD_TILE[r] - fresh_tiles))
    pl.semaphore_wait(barrier, n_seq - 1)
    for r in reused:
        swaps[2][0].start(r)
    for t in range(3):
        if t == 0:
            full = (matmul(normed, qw[...]) + flat(qb)).astype(jnp.bfloat16)
        elif t == 1:
            full = matmul(normed, kw[...]).astype(jnp.bfloat16)
        else:
            full = (matmul(normed, vw[...]) + flat(vb)).astype(jnp.bfloat16)
        for r in range(n_seq):
            if t < 2 or r not in reused:
                place(t, r, lanes_of(full, PAIR_TILE[r]), lanes_of(full, THIRD_TILE[r]))
        if t < 2:
            swaps[t][0].start()
        else:
            for r in range(n_seq):
                if r not in reused:
                    swaps[2][0].start(r)
    for t in range(3):
        if t < 2:
            swaps[t][1].start()
        else:
            for r in range(n_seq):
                swaps[2][1].start(r)
        rp[t, pl.ds(pl.multiple_of(sq * rows, rows), rows)] = sp[sq, t]
        rt[t, sq] = st[sq, t]
    for i in range(n_seq):
        cols = (i + 1) * rows
        bias[i * rows : (i + 1) * rows, 0:cols] = mask_bias(lens, valid_row, i * rows, rows, cols)
    back = [Gather(n_seq, dp, sq, lambda to: smp.at[to], lambda s: rmp.at[s], lambda i: mssem.at[0, i], lambda i: mrsem.at[0, i]),
            Gather(n_seq, dp, sq, lambda to: smt.at[to], lambda s: rmt.at[s], lambda i: mssem.at[1, i], lambda i: mrsem.at[1, i])]
    low = low_lanes()
    scale = 1.0 / math.sqrt(HDIM)
    keep = (jnp.where(low, scale, 0.0).astype(jnp.bfloat16), jnp.where(low, 0.0, scale).astype(jnp.bfloat16))

    def attend(q, k, v, block):
        scores = matmul_right_t(q, k) + block
        top = jnp.max(scores, axis=-1, keepdims=True)
        powered = jnp.exp(scores - top)
        total = jnp.sum(powered, axis=-1, keepdims=True)
        probs = (powered * (1.0 / total)).astype(jnp.bfloat16)
        return matmul(probs, v), top + jnp.log(total)

    for t in range(3):
        swaps[t][0].wait()
    lane = lax.broadcasted_iota(jnp.int32, (1, LANES), 1)
    for i in range(n_seq):
        here = slice(i * rows, (i + 1) * rows)
        cols = (i + 1) * rows
        block = bias[here, 0:cols]
        q, k, v = rp[0, here], rp[1, 0:cols], rp[2, 0:cols]
        o0, l0 = attend(q * keep[0], k, v, block)
        o1, l1 = attend(q * keep[1], k, v, block)
        smp[i] = jnp.where(low, o0, o1).astype(jnp.bfloat16)
        lse_out[here] = jnp.where(lane == 0, l0, l1)
        back[0].start(i)
    for t in range(3):
        swaps[t][1].wait()
        for s in range(n_seq):
            a, b = unpack_third(rt[t, s])
            third_out[t, s * rows : s * rows + half] = a
            third_out[t, s * rows + half : (s + 1) * rows] = b
    for i in range(n_seq):
        here = slice(i * rows, (i + 1) * rows)
        cols = (i + 1) * rows
        block = bias[here, 0:cols]
        o2, l2 = attend(third_out[0, here] * keep[0], third_out[1, 0:cols], third_out[2, 0:cols], block)
        smt[i] = pack_third(o2[:half], o2[half:], False)
        lse_out[here] = jnp.where(lane == 2, l2, lse_out[here])
        back[1].start(i)
    pair_out[...] = rp[...]
    rmp[sq] = smp[sq]
    rmt[sq] = smt[sq]
    back[0].wait()
    back[1].wait()
    for r in range(n_seq):
        c = PAIR_TILE[r] * LANES
        mixed_out[:, c : c + LANES] = rmp[r]
    for r in range(0, n_seq, 2):
        a, b = join_thirds(rmt[r], rmt[r + 1])
        c = THIRD_TILE[r] * LANES
        mixed_out[0:half, c : c + LANES] = a
        mixed_out[half:rows, c : c + LANES] = b


def front(mesh, hidden, skip, lens, valid, n1g, n1s, qw, qb, kw, vw, vb, collective_id):
    n_dp, n_seq = mesh.shape["dp"], mesh.shape["seq"]
    rows, d = hidden.shape
    group = rows * n_seq
    bf, f32 = jnp.bfloat16, jnp.float32
    vmem = pl.BlockSpec(memory_space=pltpu.VMEM)
    half = rows // 2
    dma = pltpu.SemaphoreType.DMA
    return pl.pallas_call(
        functools.partial(front_kernel, (n_dp, n_seq)),
        in_specs=[pl.BlockSpec(memory_space=pltpu.SMEM)] + [vmem] * 10,
        out_specs=(vmem,) * 5,
        out_shape=(jax.ShapeDtypeStruct((rows, d), bf), jax.ShapeDtypeStruct((rows, d), bf),
                   jax.ShapeDtypeStruct((3, group, LANES), bf), jax.ShapeDtypeStruct((3, group, LANES), bf),
                   jax.ShapeDtypeStruct((group, LANES), f32)),
        scratch_shapes=[
            pltpu.VMEM((n_seq, 3, rows, LANES), bf), pltpu.VMEM((n_seq, 3, half, LANES), bf),
            pltpu.VMEM((3, group, LANES), bf), pltpu.VMEM((3, n_seq, half, LANES), bf),
            pltpu.VMEM((n_seq, rows, LANES), bf), pltpu.VMEM((n_seq, half, LANES), bf),
            pltpu.VMEM((n_seq, rows, LANES), bf), pltpu.VMEM((n_seq, half, LANES), bf),
            pltpu.VMEM((group, group), f32),
            dma((2, 3, n_seq)), dma((2, 3, n_seq)), dma((2, n_seq)), dma((2, n_seq))],
        compiler_params=pltpu.CompilerParams(collective_id=collective_id, has_side_effects=True, vmem_limit_bytes=56 * 2**20),
        name="front",
    )(lens, hidden, skip, valid.reshape(1, -1), n1g, n1s, qw, qb, kw, vw, vb)


GELU_A = 0.044715


def back_kernel(cfg, lens, valid_row, mixed, hidden, og, valid_col, proj_w, proj_b, n2g, n2s, fc_b, out_b, n1g, lse, normed,
                pair_in, third_in, fc_w, out_w, qw, kw, vw,
                out, output, grad_input, grad_skip, small_z, small_out,
                nt_ref, xhat_ref, mid_ref, mlp_acc, two_acc, inv_ref, wf, wo, pair, third, part1,
                gs, gst, gp, gt, gthird, bias, dk_acc, dv_acc, dsp, dst, drp, drt, rows_in, part2,
                recv, gat, sbuf, load_sem, gssem, grsem, dssem, drsem, send_sem, recv_sem, local_sem, ssend, srecv_sem):
    n_dp, n_seq, halves, streams, plan, steps = cfg
    dp, sq = lax.axis_index("dp"), lax.axis_index("seq")
    rows, d = hidden.shape
    half = rows // 2
    bf, f32 = jnp.bfloat16, jnp.float32
    barrier, count = entry_barrier(n_dp, n_seq, dp, sq, True)

    def weight_copies(j):
        cols = pl.ds(j * FCH, FCH)
        return [pltpu.make_async_copy(fc_w.at[:, cols], wf.at[j % 2], load_sem.at[0, j]),
                pltpu.make_async_copy(out_w.at[cols], wo.at[j % 2], load_sem.at[1, j])]

    extra = [pltpu.make_async_copy(pair_in, pair, load_sem.at[2, 0]), pltpu.make_async_copy(third_in, third, load_sem.at[2, 1])]
    late = [pltpu.make_async_copy(qw, wf.at[0], load_sem.at[3, 0]), pltpu.make_async_copy(kw, wf.at[1], load_sem.at[3, 1]),
            pltpu.make_async_copy(vw, wo.at[0, :, pl.ds(0, VFRESH)], load_sem.at[3, 2])]
    for j in range(2):
        for copy in weight_copies(j):
            copy.start()
    for copy in extra:
        copy.start()
    x = hidden[...].astype(f32)
    attn = matmul(mixed[...], proj_w[...]) + flat(proj_b)
    middle = x + attn
    mid_ref[...] = middle
    real = valid_col[...]
    spread = middle - jnp.mean(middle, axis=-1, keepdims=True)
    inv = lax.rsqrt(jnp.mean(spread * spread, axis=-1, keepdims=True) + norm_eps)
    xhat = spread * inv
    xhat_ref[...] = xhat
    inv_ref[...] = jnp.broadcast_to(inv, inv_ref.shape)
    nt_ref[...] = (xhat * flat(n2g) + flat(n2s)).astype(bf)
    s0 = row_sum(jnp.sum(x * x, axis=-1, keepdims=True) * real)
    s1 = row_sum(jnp.sum(attn * attn, axis=-1, keepdims=True) * real)
    s3 = row_sum(real)
    word = lax.broadcasted_iota(jnp.int32, (1, WID), 1)
    sums = jnp.where(word == 0, s0, jnp.where(word == 1, s1, jnp.where(word == 3, s3, 0.0)))
    sbuf[0] = jnp.zeros_like(sbuf[0])
    sbuf[0, 7:8] = row_sum(og[...].astype(f32))
    pl.semaphore_wait(barrier, count)
    ex = Exchange(streams, halves, dp, sq, (part1, part2), out, recv, gat, (send_sem, recv_sem, local_sem))
    tiny = Small(n_dp, n_seq, dp, sq, sbuf, ssend, srecv_sem, small_z, small_out)
    task = iter(range(1, len(plan)))

    def advance():
        for s, k in plan[next(task)]:
            ex.step(s, k)

    def begin(phase, chunk):
        for s, st in enumerate(streams):
            if st[0] == phase and (chunk is None or st[4] == chunk):
                ex.start(s, 0)

    h1, h2 = halves
    for j in range(steps):
        for copy in weight_copies(j):
            copy.wait()
        slot = j % 2
        pre = matmul(nt_ref[...], wf[slot]) + fc_b[:, j * FCH : (j + 1) * FCH]
        sq_pre = pre * pre
        t = jnp.tanh(tanh_coef * (pre + GELU_A * sq_pre * pre))
        act = (0.5 * pre * (1.0 + t)).astype(bf)
        slope = 0.5 * (1.0 + t) + 0.5 * pre * (1.0 - t * t) * (tanh_coef * (1.0 + 3.0 * GELU_A * sq_pre))
        pre_grad = matmul_right_t(og[...], wo[slot]) * slope
        sbuf[0, 8 + j : 9 + j] = row_sum(pre_grad)
        pre_low = pre_grad.astype(bf)
        part1[j * CHUNK : (j + 1) * CHUNK] = matmul_left_t(act, og[...]).astype(bf).reshape(CHUNK, SUB, WID)
        part1[h1 + j * CHUNK : h1 + (j + 1) * CHUNK] = matmul_left_t(nt_ref[...], pre_low).astype(bf).reshape(CHUNK, SUB, WID)
        begin(0, j)
        advance()
        mlp = matmul(act, wo[slot])
        two = matmul_right_t(pre_low, wf[slot])
        if j == 0:
            mlp_acc[...] = mlp
            two_acc[...] = two
        else:
            mlp_acc[...] = mlp_acc[...] + mlp
            two_acc[...] = two_acc[...] + two
        if j + 2 < steps:
            for copy in weight_copies(j + 2):
                copy.start()
        advance()
    for copy in late:
        copy.start()
    two_grad = two_acc[...]
    xhat = xhat_ref[...]
    sbuf[0, 5:6] = row_sum(two_grad * xhat)
    sbuf[0, 6:7] = row_sum(two_grad)
    e = two_grad * flat(n2g)
    centre = jnp.mean(e, axis=-1, keepdims=True)
    along = jnp.mean(e * xhat, axis=-1, keepdims=True)
    grad = og[...].astype(f32) + (e - centre - xhat * along) * inv_ref[:, 0:1]
    grad_low = grad.astype(bf)
    full = matmul_right_t(grad_low, proj_w[...]).astype(bf)
    for r in range(n_seq):
        c = PAIR_TILE[r] * LANES
        gs[r] = full[:, c : c + LANES]
        c = THIRD_TILE[r] * LANES
        gst[r] = pack_third(full[:half, c : c + LANES], full[half:, c : c + LANES], r % 2)
    swap_pair = Swap(n_seq, dp, sq, lambda to: gs.at[to], lambda me: gp.at[pl.ds(me * rows, rows)], lambda i: gssem.at[0, i], lambda i: grsem.at[0, i])
    swap_third = Swap(n_seq, dp, sq, lambda to: gst.at[to], lambda me: gt.at[me], lambda i: gssem.at[1, i], lambda i: grsem.at[1, i])
    swap_pair.start()
    swap_third.start()
    advance()
    mlp_out = mlp_acc[...] + flat(out_b)
    output[...] = (mid_ref[...] + mlp_out).astype(bf)
    s2 = row_sum(jnp.sum(mlp_out * mlp_out, axis=-1, keepdims=True) * valid_col[...])
    sbuf[0, 12:13] = sums + jnp.where(word == 2, s2, 0.0)
    sbuf[0, 4:5] = row_sum(grad)
    mid_ref[...] = grad
    gw = matmul_left_t(mixed[...], grad_low).astype(bf)
    top = d // 2 // SUB
    at = steps * CHUNK
    part1[at : at + top] = gw[: d // 2].reshape(top, SUB, WID)
    part1[h1 + at : h1 + at + top] = gw[d // 2 :].reshape(top, SUB, WID)
    if h1 > at + top:
        for h in range(2):
            part1[h * h1 + at + top : (h + 1) * h1] = jnp.zeros((h1 - at - top, SUB, WID), bf)
    begin(0, steps)
    advance()
    gp[pl.ds(pl.multiple_of(sq * rows, rows), rows)] = gs[sq]
    gt[sq] = gst[sq]
    for i in range(n_seq):
        cols = (i + 1) * rows
        bias[i * rows : (i + 1) * rows, 0:cols] = mask_bias(lens, valid_row, i * rows, rows, cols).astype(bf)
    send = [Gather(n_seq, dp, sq, lambda to: dsp.at[to], lambda s: drp.at[s], lambda i: dssem.at[0, i], lambda i: drsem.at[0, i]),
            Gather(n_seq, dp, sq, lambda to: dst.at[to], lambda s: drt.at[s], lambda i: dssem.at[1, i], lambda i: drsem.at[1, i])]
    advance()
    for copy in extra:
        copy.wait()
    low = low_lanes()
    scale = 1.0 / math.sqrt(HDIM)
    keep = (jnp.where(low, scale, 0.0).astype(bf), jnp.where(low, 0.0, scale).astype(bf))
    ones = (jnp.where(low, 1.0, 0.0).astype(bf), jnp.where(low, 0.0, 1.0).astype(bf))

    def backward(q, k, v, g, block, total):
        probs = jnp.exp(matmul_right_t(q, k) + block - total)
        prob_grad = matmul_right_t(g, v)
        centre = jnp.sum(probs * prob_grad, axis=-1, keepdims=True)
        score_grad = (probs * (prob_grad - centre)).astype(bf)
        return matmul(score_grad, k), matmul_left_t(score_grad, q), matmul_left_t(probs.astype(bf), g)

    swap_pair.wait()
    for i in reversed(range(n_seq)):
        here = slice(i * rows, (i + 1) * rows)
        cols = (i + 1) * rows
        block = bias[here, 0:cols].astype(f32)
        q, k, v, g = pair[0, here], pair[1, 0:cols], pair[2, 0:cols], gp[here]
        dq0, dk0, dv0 = backward(q * keep[0], k, v, g * ones[0], block, lse[here, 0:1])
        dq1, dk1, dv1 = backward(q * keep[1], k, v, g * ones[1], block, lse[here, 1:2])
        if i == n_seq - 1:
            dk_acc[...] = dk0 + dk1
            dv_acc[...] = dv0 + dv1
        else:
            dk_acc[0:cols] = dk_acc[0:cols] + (dk0 + dk1)
            dv_acc[0:cols] = dv_acc[0:cols] + (dv0 + dv1)
        dsp[i, 0] = (jnp.where(low, dq0, dq1) * scale).astype(bf)
        dsp[i, 1] = dk_acc[here].astype(bf)
        dsp[i, 2] = dv_acc[here].astype(bf)
        send[0].start(i)
        advance()
    swap_third.wait()
    for s in range(n_seq):
        a, b = unpack_third(gt[s])
        gthird[s * rows : s * rows + half] = a
        gthird[s * rows + half : (s + 1) * rows] = b
    for i in reversed(range(n_seq)):
        here = slice(i * rows, (i + 1) * rows)
        cols = (i + 1) * rows
        block = bias[here, 0:cols].astype(f32)
        dq, dk, dv = backward(third[0, here] * keep[0], third[1, 0:cols], third[2, 0:cols], gthird[here], block, lse[here, 2:3])
        if i == n_seq - 1:
            dk_acc[...] = dk
            dv_acc[...] = dv
        else:
            dk_acc[0:cols] = dk_acc[0:cols] + dk
            dv_acc[0:cols] = dv_acc[0:cols] + dv
        dq = dq * scale
        dst[i, 0] = pack_third(dq[:half], dq[half:], False)
        for t, a in ((1, dk_acc), (2, dv_acc)):
            dst[i, t] = pack_third(a[i * rows : i * rows + half], a[i * rows + half : (i + 1) * rows], False)
        send[1].start(i)
        advance()
    drp[sq] = dsp[sq]
    drt[sq] = dst[sq]
    x = hidden[...].astype(f32)
    spread = x - jnp.mean(x, axis=-1, keepdims=True)
    inv = lax.rsqrt(jnp.mean(spread * spread, axis=-1, keepdims=True) + norm_eps)
    xhat = spread * inv
    send[0].wait()
    for t in range(3):
        for r in range(n_seq):
            c = PAIR_TILE[r] * LANES
            rows_in[t, :, c : c + LANES] = drp[r, t]
    advance()
    send[1].wait()
    for t in range(3):
        for r in range(0, n_seq, 2):
            a, b = join_thirds(drt[r, t], drt[r + 1, t])
            c = THIRD_TILE[r] * LANES
            rows_in[t, 0:half, c : c + LANES] = a
            rows_in[t, half:rows, c : c + LANES] = b
    nl = normed[...]
    dq, dk, dv = rows_in[0], rows_in[1], rows_in[2]
    fresh = dv[:, 0:VFRESH]
    grad_skip[...] = dv[:, VFRESH:]
    units_d = d // SUB
    uv = d // 4 // SUB
    part2[0:units_d] = matmul_left_t(nl, dq).astype(bf).reshape(units_d, SUB, WID)
    part2[h2 : h2 + units_d] = matmul_left_t(nl, dk).astype(bf).reshape(units_d, SUB, WID)
    gv = matmul_left_t(nl, fresh).astype(bf)
    for h in range(2):
        for side in range(2):
            r0 = side * (d // 2) + h * (d // 4)
            part2[h * h2 + units_d : h * h2 + units_d + uv, :, side * VFRESH : (side + 1) * VFRESH] = (
                gv[r0 : r0 + d // 4].reshape(uv, SUB, VFRESH))
        if h2 > units_d + uv:
            part2[h * h2 + units_d + uv : (h + 1) * h2] = jnp.zeros((h2 - units_d - uv, SUB, WID), bf)
    begin(1, None)
    advance()
    for copy in late:
        copy.wait()
    normed_grad = matmul_right_t(dq, wf[0]) + matmul_right_t(dk, wf[1]) + matmul_right_t(fresh, wo[0, :, 0:VFRESH])
    f = normed_grad * flat(n1g)
    centre = jnp.mean(f, axis=-1, keepdims=True)
    along = jnp.mean(f * xhat, axis=-1, keepdims=True)
    grad_input[...] = (mid_ref[...] + (f - centre - xhat * along) * inv).astype(bf)
    sbuf[0, 0:1] = row_sum(normed_grad * xhat)
    sbuf[0, 1:2] = row_sum(normed_grad)
    sbuf[0, 2:3] = row_sum(dq.astype(f32))
    sbuf[0, 3:4, 0:VFRESH] = row_sum(fresh.astype(f32))
    tiny.copy(0).start()
    todo = plan[next(task)]
    gap = max(1, len(todo) // (len(tiny.dims) + 2))
    for left, (s, k) in enumerate(todo):
        ex.step(s, k)
        if left % gap == gap - 1:
            tiny.step()
    tiny.rest()


def back(mesh, lens, valid, mixed, hidden, og, valid_col, proj_w, proj_b, n2g, n2s, fc_b, out_b, n1g, lse, normed,
         pair, third, fc_w, out_w, qw, kw, vw, collective_id):
    n_dp, n_seq = mesh.shape["dp"], mesh.shape["seq"]
    rows, d = hidden.shape
    group = rows * n_seq
    half = rows // 2
    steps = fc_w.shape[1] // FCH
    bf, f32 = jnp.bfloat16, jnp.float32
    quantum = n_dp // 2 * n_seq
    needed = (steps * CHUNK + d // 2 // SUB, d // SUB + d // 4 // SUB)
    halves = tuple(-(-n // quantum) * quantum for n in needed)
    streams = plan_streams(n_dp, n_seq, halves, steps)
    plan, _ = schedule(streams, steps, rows)
    n_st = 2 * (bits_of(n_dp) + bits_of(n_seq))
    n_small = bits_of(n_dp) + bits_of(n_seq)
    ns = len(streams)
    vmem = pl.BlockSpec(memory_space=pltpu.VMEM)
    hbm = pl.BlockSpec(memory_space=pl.ANY)
    dma = pltpu.SemaphoreType.DMA
    units = lambda n: pltpu.VMEM((n, SUB, WID), bf)
    wide = lambda: pltpu.VMEM((rows, d), f32)
    sshape = jax.ShapeDtypeStruct((16, WID), f32)
    args = (lens, valid.reshape(1, -1), mixed, hidden, og, valid_col, proj_w, proj_b, n2g, n2s, fc_b.reshape(1, -1), out_b, n1g, lse, normed,
            pair, third, fc_w, out_w, qw, kw, vw)
    outs = pl.pallas_call(
        functools.partial(back_kernel, (n_dp, n_seq, halves, streams, plan, steps)),
        in_specs=[pl.BlockSpec(memory_space=pltpu.SMEM)] + [vmem] * 14 + [hbm] * 7,
        out_specs=(hbm, vmem, vmem, vmem, vmem, vmem),
        out_shape=(jax.ShapeDtypeStruct((2 * sum(halves), SUB, WID), bf), jax.ShapeDtypeStruct((rows, d), bf),
                   jax.ShapeDtypeStruct((rows, d), bf), jax.ShapeDtypeStruct((rows, d - VFRESH), bf), sshape, sshape),
        scratch_shapes=[
            pltpu.VMEM((rows, d), bf), wide(), wide(), wide(), wide(), pltpu.VMEM((rows, LANES), f32),
            pltpu.VMEM((2, d, FCH), bf), pltpu.VMEM((2, FCH, d), bf),
            pltpu.VMEM((3, group, LANES), bf), pltpu.VMEM((3, group, LANES), bf), units(2 * halves[0]),
            pltpu.VMEM((n_seq, rows, LANES), bf), pltpu.VMEM((n_seq, half, LANES), bf),
            pltpu.VMEM((group, LANES), bf), pltpu.VMEM((n_seq, half, LANES), bf), pltpu.VMEM((group, LANES), bf),
            pltpu.VMEM((group, group), bf), pltpu.VMEM((group, LANES), f32), pltpu.VMEM((group, LANES), f32),
            pltpu.VMEM((n_seq, 3, rows, LANES), bf), pltpu.VMEM((n_seq, 3, half, LANES), bf),
            pltpu.VMEM((n_seq, 3, rows, LANES), bf), pltpu.VMEM((n_seq, 3, half, LANES), bf),
            pltpu.VMEM((3, rows, d), bf), units(2 * halves[1]),
            units(Exchange.recv_total(streams)), units(sum(halves)),
            pltpu.VMEM((2 * n_small, 16, WID), f32), dma((4, max(4, steps))),
            dma((2, n_seq)), dma((2, n_seq)), dma((2, n_seq)), dma((2, n_seq)),
            dma((ns, n_st)), dma((ns, n_st)), dma((ns,)), dma((n_small,)), dma((n_small,))],
        compiler_params=pltpu.CompilerParams(collective_id=collective_id, has_side_effects=True, vmem_limit_bytes=67043328),
        name="back",
    )(*args)
    return outs, halves


def local(
    mesh,
    hidden_in,
    skip_values,
    out_grad,
    doc_lens,
    valid,
    norm1_gain,
    norm1_shift,
    query_w,
    query_b,
    key_w,
    value_w,
    value_b,
    proj_w,
    proj_b,
    norm2_gain,
    norm2_shift,
    fc_w,
    fc_b,
    out_w,
    out_b,
):
    seq_size = lax.axis_size("seq")
    seq_rank = lax.axis_index("seq")
    tok_rows = hidden_in.shape[0]
    valid_col = lax.dynamic_slice_in_dim(valid, seq_rank * tok_rows, tok_rows, 0).astype(jnp.float32)[:, None]
    normed, mixed, pair, third, lse = front(
        mesh, hidden_in, skip_values, doc_lens, valid, norm1_gain, norm1_shift, query_w, query_b, key_w, value_w, value_b, 0
    )
    (summed, output, grad_input, grad_skip, small_z, small_all), halves = back(
        mesh, doc_lens, valid, mixed, hidden_in, out_grad, valid_col, proj_w, proj_b, norm2_gain, norm2_shift, fc_b, out_b,
        norm1_gain, lse, normed, pair, third, fc_w, out_w, query_w, key_w, value_w, 1
    )
    (
        grad_out_w, grad_fc_w, grad_proj_w, grad_query_w, grad_key_w, grad_value_w,
        grad_norm1_gain, grad_norm1_shift, grad_query_b, grad_value_b, grad_proj_b, grad_norm2_gain, grad_norm2_shift,
        grad_out_b, grad_fc_b, norm_values, grad_input, grad_skip,
    ) = widen(summed.reshape(-1, WID), small_all, small_z, grad_input, grad_skip, halves, D, fc_w.shape[1], VFRESH)
    return (
        output,
        grad_input,
        grad_skip,
        grad_norm1_gain,
        grad_norm1_shift,
        grad_query_w,
        grad_query_b,
        grad_key_w,
        grad_value_w,
        grad_value_b,
        grad_proj_w,
        grad_proj_b,
        grad_norm2_gain,
        grad_norm2_shift,
        grad_fc_w,
        grad_fc_b,
        grad_out_w,
        grad_out_b,
        norm_values,
    )


def solution(mesh):
    placed = (
        P(("dp", "seq"), None),
        P(("dp", "seq"), None),
        P(("dp", "seq"), None),
        P("dp", None),
        P("dp"),
        P(),
        P(),
        P(),
        P(),
        P(),
        P(),
        P(),
        P(),
        P(),
        P(),
        P(),
        P(),
        P(),
        P(),
        P(),
    )
    return jax.shard_map(
        functools.partial(local, mesh),
        mesh=mesh,
        in_specs=placed,
        out_specs=(
            P(("dp", "seq"), None),
            P(("dp", "seq"), None),
            P(("dp", "seq"), None),
            P(),
            P(),
            P(),
            P(),
            P(),
            P(),
            P(),
            P(),
            P(),
            P(),
            P(),
            P(),
            P(),
            P(),
            P(),
            P("dp", None),
        ),
        check_vma=False,
    )
```

```python
import functools
import math

import jax
import jax.numpy as jnp
from jax import lax
from jax.experimental import pallas as pl
from jax.experimental.pallas import tpu as pltpu
from jax.sharding import PartitionSpec as P

D = 768
HEADS = 12
HDIM = 64
VFRESH = 384


norm_eps = 1e-05
square_eps = 1e-06
tanh_coef = 0.7978845608028654
masked_score = -1e30


MESH = pl.DeviceIdType.MESH
SUB = 8
WID = 768
UNIT_BYTES = SUB * WID * 2
FCH = 768
CHUNK = FCH // SUB
MLP_TIMES = (2.2, 1.1)
TASKS = (2.5, 2.5, 1.5, 2.3, 1.7, 1.2, 0.7, 1.6, 0.9, 0.7, 0.5, 0.8, 4.5, 3.0)
ENTRY = 3.5
MARGIN = 1.5
TASK_HOLDS = (0.0, 0.0, 0.0, 0.0, 0.0, 0.0, 0.0, 0.0, 0.0, 0.0, 0.0, 0.0, 0.0, 0.0)
SIZES = ((2, 2, 2, 2, 2, 2, 2, 2, 2, 2, 2, 2, 3), (2, 2, 2, 2))
KINDS = (1, 0, 0, 1, 1, 0, 1, 0, 0, 1, 1, 1, 0, 1, 3, 0, 2)
HOLDS = (7.9, 37.1, 25.1, 62.4, 39.0, 7.3, 27.8, 41.0, 59.4, 8.5, 57.8, 22.0, 45.0, 0, 0.8, 10.9, 45.9)
LINK = 0.045
LATENCY = 2.0
AR_COST = 0.25


def bits_of(n):
    return n.bit_length() - 1


def partner(dim, dp, sq):
    kind, j = dim
    step = 1 << j
    if kind == "dp":
        bit = (dp // step) % 2
        return bit, (dp + step - 2 * step * bit, sq)
    bit = (sq // step) % 2
    return bit, (dp, sq + step - 2 * step * bit)


def plan_streams(n_dp, n_seq, halves, steps):
    dpb = [("dp", j) for j in range(1, bits_of(n_dp))]
    sqb = [("seq", j) for j in range(bits_of(n_seq))]
    mid = len(dpb) // 2
    one, two = dpb[:mid], dpb[mid:]
    orders = (one + two + sqb, two + one + sqb, one + sqb + two, two + sqb + one, sqb + one + two, sqb + two + one)
    quantum = (n_dp // 2) * n_seq
    streams = []
    for phase, half_units in enumerate(halves):
        total = half_units // quantum
        sizes = SIZES[phase]
        if sum(sizes) != total:
            sizes = (2,) * (total // 2) + (1,) * (total % 2)
        first = 0
        for size in sizes:
            n = size * quantum
            chunk = min(steps, (first + n - 1) // CHUNK)
            streams.append((phase, first, n, orders[KINDS[len(streams) % len(KINDS)]], chunk if phase == 0 else -1))
            first += n
    return streams


def schedule(streams, steps, rows):
    free = {}
    stages = []
    for phase, first, n, order, _ in streams:
        seq = [(("dp", 0), n)]
        size = n
        for d in order:
            size //= 2
            seq.append((d, size))
        for d in reversed(order):
            seq.append((d, size))
            size *= 2
        stages.append(seq + [(("dp", 0), n)])

    def flow(needs, t):
        begin = max([t] + [free.get(r, 0.0) for r, _ in needs])
        for r, dur in needs:
            free[r] = begin + dur
        return begin + max(dur for _, dur in needs) + LATENCY

    flying = []

    def launch(s, k, t):
        d, size = stages[s][k]
        b = size * UNIT_BYTES / 1e6
        if d == ("dp", 0):
            needs = [("c", b / 0.5)]
        elif d[0] == "dp":
            needs = [(d, b / LINK)]
        elif d[1] == 0:
            needs = [("end", b / LINK)]
        else:
            needs = [("mid", 2 * b / LINK), ("end", b / LINK)]
        end = flow(needs, t)
        flying.append((max(end, HOLDS[s % len(HOLDS)]) if k == 0 else end, s, k))

    block = rows * LANES * 2 / 1e6 / LINK
    arrive = {}
    durations = [MLP_TIMES[i % 2] for i in range(2 * steps)] + list(TASKS)
    n_tasks = len(durations)
    plan = [[] for _ in range(n_tasks + 1)]
    t, task = ENTRY, 0
    while task < n_tasks or flying:
        ready = None
        at_task = task - 2 * steps
        if task < n_tasks:
            needs = {3: ("grad pair",), 7: ("grad third",), 11: ("pair",), 12: ("third",)}.get(at_task, ())
            ready = max([TASK_HOLDS[at_task] if at_task >= 0 else 0.0] + [arrive[x] for x in needs])
        flying.sort()
        arrived = flying and flying[0][0] + MARGIN <= t
        if ready is not None and not arrived and (ready <= t or not flying or ready <= flying[0][0]):
            t = max(t, ready) + durations[task]
            begun = []
            if at_task < 0 and task % 2 == 0:
                begun = [s for s, st in enumerate(streams) if st[0] == 0 and st[4] == task // 2]
            if at_task == 0:
                arrive["grad pair"] = flow([("mid", 4 * block), ("end", 3 * block)], t)
                arrive["grad third"] = flow([("mid", 2 * block), ("end", 1.5 * block)], t)
            if at_task == 1:
                begun = [s for s, st in enumerate(streams) if st[0] == 0 and st[4] == steps]
            if 3 <= at_task <= 6:
                arrive["pair"] = flow([("mid", 3 * block), ("end", 2.25 * block)], t) + 2.0
            if 7 <= at_task <= 10:
                arrive["third"] = flow([("mid", 1.5 * block), ("end", 1.125 * block)], t) + 2.0
            if at_task == 12:
                begun = [s for s, st in enumerate(streams) if st[0] == 1]
            for s in begun:
                launch(s, 0, t)
            task += 1
            continue
        at, s, k = flying.pop(0)
        plan[task].append((s, k))
        t = max(t, at) + AR_COST
        if k + 1 < len(stages[s]):
            launch(s, k + 1, t)
    return plan, t


class Exchange:
    def __init__(self, streams, halves, dp, sq, parts, out, recv, gat, sems):
        self.streams, self.halves = streams, halves
        self.dp, self.sq = dp, sq
        self.parts, self.out, self.recv, self.gat = parts, out, recv, gat
        self.send_sem, self.recv_sem, self.local_sem = sems
        self.cbit, self.cdev = partner(("dp", 0), dp, sq)
        self.base = [sum(halves[:p]) for p in range(len(halves))]
        self.off = [[st[1]] for st in streams]
        self.roff = []
        r = 0
        for phase, first, n, order, _ in streams:
            rows = [r]
            r += n
            size = n
            for _ in order:
                size //= 2
                rows.append(r)
                r += size
            self.roff.append(rows)

    @staticmethod
    def recv_total(streams):
        r = 0
        for phase, first, n, order, _ in streams:
            r += n
            for i in range(len(order)):
                r += n >> (i + 1)
        return r

    def n_stages(self, s):
        return 2 * (len(self.streams[s][3]) + 1)

    def remote(self, s, k, src, dst, dev):
        return pltpu.make_async_remote_copy(
            src_ref=src, dst_ref=dst, send_sem=self.send_sem.at[s, k], recv_sem=self.recv_sem.at[s, k],
            device_id=dev, device_id_type=MESH)

    def copies(self, s, k):
        phase, first, n, order, _ = self.streams[s]
        depth = len(order)
        half_units, base = self.halves[phase], self.base[phase]
        part = self.parts[phase]
        own = self.cbit * half_units
        if k == 0:
            other = (1 - self.cbit) * half_units + first
            return self.remote(s, k, part.at[pl.ds(other, n)], self.recv.at[pl.ds(self.roff[s][0], n)], self.cdev), None
        if k <= depth:
            half = n >> k
            bit, dev = partner(order[k - 1], self.dp, self.sq)
            at = own + self.off[s][k - 1] + (1 - bit) * half
            return self.remote(s, k, part.at[pl.ds(at, half)], self.recv.at[pl.ds(self.roff[s][k], half)], dev), None
        g = 2 * depth + 1 - k
        if g >= 1:
            half = n >> g
            bit, dev = partner(order[g - 1], self.dp, self.sq)
            piece = self.gat.at[pl.ds(base + self.off[s][g], half)]
            return self.remote(s, k, piece, piece, dev), None
        piece = self.gat.at[pl.ds(base + first, n)]
        there = self.out.at[pl.ds(2 * base + own + first, n)]
        return self.remote(s, k, piece, there, self.cdev), pltpu.make_async_copy(piece, there, self.local_sem.at[s])

    def start(self, s, k):
        for c in self.copies(s, k):
            if c is not None:
                c.start()

    def finish(self, s, k):
        phase, first, n, order, _ = self.streams[s]
        depth = len(order)
        remote, local = self.copies(s, k)
        remote.wait()
        if local is not None:
            local.wait()
        if k <= depth:
            half = n >> k
            if k > 0:
                bit, _ = partner(order[k - 1], self.dp, self.sq)
                self.off[s].append(self.off[s][k - 1] + bit * half)
            at = self.cbit * self.halves[phase] + self.off[s][k]
            to = (self.gat, self.base[phase] + self.off[s][k]) if k == depth else (self.parts[phase], at)
            self.add(self.parts[phase], at, self.roff[s][k], half, to)

    def add(self, part, at, roff, n, to):
        recv = self.recv
        dst, first = to
        step = next(d for d in (8, 6, 4, 3, 2, 1) if n % d == 0)

        def body(i, c):
            a = pl.ds(at + i * step, step)
            b = pl.ds(roff + i * step, step)
            dst[pl.ds(first + i * step, step)] = part[a] + recv[b]
            return c

        lax.fori_loop(0, n // step, body, 0)

    def step(self, s, k):
        self.finish(s, k)
        if k + 1 < self.n_stages(s):
            self.start(s, k + 1)


class Small:
    def __init__(self, n_dp, n_seq, dp, sq, buf, ssend, srecv, small_z, small_out):
        self.dims = [("seq", j) for j in range(bits_of(n_seq))] + [("dp", j) for j in range(bits_of(n_dp))]
        self.nz = bits_of(n_seq)
        self.dp, self.sq, self.buf, self.ssend, self.srecv = dp, sq, buf, ssend, srecv
        self.small_z, self.small_out = small_z, small_out
        self.done = 0

    def copy(self, i):
        _, dev = partner(self.dims[i], self.dp, self.sq)
        return pltpu.make_async_remote_copy(
            src_ref=self.buf.at[2 * i], dst_ref=self.buf.at[2 * i + 1], send_sem=self.ssend.at[i],
            recv_sem=self.srecv.at[i], device_id=dev, device_id_type=MESH)

    def begin(self, value):
        self.buf[0] = value
        self.copy(0).start()

    def step(self):
        i = self.done
        if i == len(self.dims):
            return
        self.copy(i).wait()
        total = self.buf[2 * i] + self.buf[2 * i + 1]
        self.done = i + 1
        if self.done == self.nz:
            self.small_z[...] = total
        if self.done < len(self.dims):
            self.buf[2 * self.done] = total
            self.copy(self.done).start()
        else:
            self.small_out[...] = total

    def rest(self):
        while self.done < len(self.dims):
            self.step()


def entry_barrier(n_dp, n_seq, dp, sq, all_seq):
    barrier = pltpu.get_barrier_semaphore()
    peers = [partner(("dp", j), dp, sq)[1] for j in range(bits_of(n_dp))]
    if all_seq:
        peers += [(dp, (sq + d) % n_seq) for d in range(1, n_seq)]
    else:
        peers += [partner(("seq", j), dp, sq)[1] for j in range(bits_of(n_seq))]
    for dev in peers:
        pl.semaphore_signal(barrier, inc=1, device_id=dev, device_id_type=MESH)
    return barrier, len(peers)


def matmul(former, latter):
    return jnp.dot(former, latter, preferred_element_type=jnp.float32)


def matmul_right_t(former, latter):
    return lax.dot_general(
        former, latter, (((1,), (1,)), ((), ())), preferred_element_type=jnp.float32
    )


def matmul_left_t(former, latter):
    return lax.dot_general(
        former, latter, (((0,), (0,)), ((), ())), preferred_element_type=jnp.float32
    )


def flat(ref):
    return ref[...].reshape(1, -1)


def row_sum(v):
    return jnp.sum(v, axis=0, keepdims=True)


PIECE = 384
VPIECE = 192


def widen_kernel(cfg, src, small, small_z, gi_in, gs_in, *refs):
    pieces, n_out = cfg
    outs, vectors, (norms, gi_out, gs_out) = refs[:n_out], refs[n_out : n_out + 9], refs[n_out + 9 : n_out + 12]
    inbuf, stage, gi_buf, gs_buf, in_sem, out_sem, row_sem = refs[n_out + 12 :]
    depth = inbuf.shape[0]

    def fetch(i):
        size = VPIECE if pieces[i][4] else PIECE
        return pltpu.make_async_copy(src.at[pl.ds(pieces[i][0], size)], inbuf.at[i % depth, pl.ds(0, size)], in_sem.at[i % depth])

    def put(i):
        slot = i % depth
        _, which, row, col, split = pieces[i]
        out = outs[which]
        if split:
            return [pltpu.make_async_copy(stage.at[slot, pl.ds(0, VPIECE), pl.ds(h * VFRESH, VFRESH)],
                                          out.at[pl.ds(row + h * VFRESH, VPIECE)], out_sem.at[slot, h]) for h in range(2)]
        return [pltpu.make_async_copy(stage.at[slot], out.at[pl.ds(row, PIECE), pl.ds(col, WID)], out_sem.at[slot, 0])]

    n = len(pieces)
    for i in range(min(depth, n)):
        fetch(i).start()
    row_in = [pltpu.make_async_copy(gi_in, gi_buf, row_sem.at[0]), pltpu.make_async_copy(gs_in, gs_buf, row_sem.at[1])]
    row_out = [pltpu.make_async_copy(gi_buf, gi_out, row_sem.at[2]), pltpu.make_async_copy(gs_buf, gs_out, row_sem.at[3])]
    for c in row_in:
        c.start()
    for i in range(n):
        slot = i % depth
        fetch(i).wait()
        if i >= depth:
            for c in put(i - depth):
                c.wait()

        def body(r, c):
            rows = pl.ds(r * 32, 32)
            stage[slot, rows] = inbuf[slot, rows].astype(jnp.float32)
            return c

        lax.fori_loop(0, (VPIECE if pieces[i][4] else PIECE) // 32, body, 0)
        for c in put(i):
            c.start()
        if i + depth < n:
            fetch(i + depth).start()
        if i == depth:
            for a, b in zip(row_in, row_out):
                a.wait()
                b.start()
            for row, v in zip((0, 1, 2, 3, 4, 5, 6, 7), vectors):
                v[...] = small[row, 0 : v.shape[0]]
            for q in range(vectors[8].shape[0] // WID):
                vectors[8][q * WID : (q + 1) * WID] = small[8 + q, :]
            sums = small_z[12:13, 0:4]
            norms[...] = jnp.sqrt(sums[:, 0:3] / (sums[:, 3:4] * D) + square_eps)
    for i in range(max(0, n - depth), n):
        for c in put(i):
            c.wait()
    for c in row_out:
        c.wait()


def widen(summed, small, small_z, grad_input, grad_skip, halves, d, ff, vf):
    one, two = halves[0] * SUB, halves[1] * SUB
    pieces = []
    for j in range(ff // PIECE):
        pieces.append((j * PIECE, 0, j * PIECE, 0, False))
        pieces.append((one + j * PIECE, 1, (j % 2) * PIECE, j // 2 * FCH, False))
    for h in range(2):
        pieces.append((h * one + ff, 2, h * PIECE, 0, False))
    for w in range(2):
        for h in range(2):
            pieces.append((2 * one + w * two + h * PIECE, 3 + w, h * PIECE, 0, False))
    for h in range(2):
        pieces.append((2 * one + h * two + d, 5, h * VPIECE, 0, True))
    f32, bf = jnp.float32, jnp.bfloat16
    depth = 8
    hbm = pl.BlockSpec(memory_space=pl.ANY)
    vmem = pl.BlockSpec(memory_space=pltpu.VMEM)
    shapes = [(ff, d), (d, ff), (d, d), (d, d), (d, d), (d, vf)]
    vectors = [(d,), (d,), (d,), (vf,), (d,), (d,), (d,), (d,), (ff,)]
    out_shape = [jax.ShapeDtypeStruct(s, f32) for s in shapes + vectors + [(1, 3)]]
    out_shape += [jax.ShapeDtypeStruct(g.shape, bf) for g in (grad_input, grad_skip)]
    return pl.pallas_call(
        functools.partial(widen_kernel, (pieces, len(shapes))),
        in_specs=[hbm, vmem, vmem, hbm, hbm], out_specs=(hbm,) * 6 + (vmem,) * 10 + (hbm,) * 2, out_shape=tuple(out_shape),
        scratch_shapes=[pltpu.VMEM((depth, PIECE, WID), bf), pltpu.VMEM((depth, PIECE, WID), f32),
                        pltpu.VMEM(grad_input.shape, bf), pltpu.VMEM(grad_skip.shape, bf),
                        pltpu.SemaphoreType.DMA((depth,)), pltpu.SemaphoreType.DMA((depth, 2)), pltpu.SemaphoreType.DMA((4,))],
        compiler_params=pltpu.CompilerParams(vmem_limit_bytes=62 * 2**20),
        name="widen",
    )(summed, small, small_z, grad_input, grad_skip)


LANES = 128
PAIR_TILE = (0, 2, 3, 5)
THIRD_TILE = (1, 1, 4, 4)


def low_lanes():
    return lax.broadcasted_iota(jnp.int32, (1, LANES), 1) < HDIM


def turn(v):
    return pltpu.roll(v, HDIM, 1)


def pack_third(first, second, upper):
    first, second = first.astype(jnp.float32), second.astype(jnp.float32)
    if upper:
        both = jnp.where(low_lanes(), turn(first), second)
    else:
        both = jnp.where(low_lanes(), first, turn(second))
    return both.astype(jnp.bfloat16)


def unpack_third(both):
    wide = both.astype(jnp.float32)
    low = low_lanes()
    first = jnp.where(low, wide, 0.0).astype(jnp.bfloat16)
    second = jnp.where(low, turn(wide), 0.0).astype(jnp.bfloat16)
    return first, second


def join_thirds(one, two):
    one, two = one.astype(jnp.float32), two.astype(jnp.float32)
    low = low_lanes()
    first = jnp.where(low, one, turn(two)).astype(jnp.bfloat16)
    second = jnp.where(low, turn(one), two).astype(jnp.bfloat16)
    return first, second


def split_tiles(tiles, pair_dst, third_dst, rows, n_seq):
    half = rows // 2
    for r in range(n_seq):
        pair_dst(r, tiles[PAIR_TILE[r]])
        t = tiles[THIRD_TILE[r]]
        third_dst(r, pack_third(t[:half], t[half:], r % 2))


def mask_bias(lens, valid_row, first, rows, cols):
    one = lens[0, 0]
    two = one + lens[0, 1]
    i = first + lax.broadcasted_iota(jnp.int32, (rows, 1), 0)
    j = lax.broadcasted_iota(jnp.int32, (1, cols), 1)
    seg_i = (i >= one).astype(jnp.int32) + (i >= two).astype(jnp.int32)
    seg_j = (j >= one).astype(jnp.int32) + (j >= two).astype(jnp.int32)
    real = valid_row[:, 0:cols] > 0
    code = jnp.where(real, seg_j, -1)
    same = (code == seg_i) & (j <= i)
    return jnp.where(same | (i == j), 0.0, masked_score)


class Swap:
    def __init__(self, n_seq, dp, sq, send, recv, ssem, rsem):
        self.n_seq, self.dp, self.sq = n_seq, dp, sq
        self.send, self.recv, self.ssem, self.rsem = send, recv, ssem, rsem

    def copy(self, d):
        to = (self.sq + d) % self.n_seq
        return pltpu.make_async_remote_copy(
            src_ref=self.send(to), dst_ref=self.recv(self.sq), send_sem=self.ssem(d), recv_sem=self.rsem(d),
            device_id=(self.dp, to), device_id_type=MESH)

    def start(self):
        for d in range(1, self.n_seq):
            self.copy(d).start()

    def wait(self):
        for d in range(1, self.n_seq):
            self.copy(d).wait()


class Gather:
    def __init__(self, n_seq, dp, sq, send, recv, ssem, rsem):
        self.n_seq, self.dp, self.sq = n_seq, dp, sq
        self.send, self.recv, self.ssem, self.rsem = send, recv, ssem, rsem

    def copy(self, to, slot):
        return pltpu.make_async_remote_copy(
            src_ref=self.send(to), dst_ref=self.recv(slot), send_sem=self.ssem(to), recv_sem=self.rsem(slot),
            device_id=(self.dp, to), device_id_type=MESH)

    def start(self, to):
        @pl.when(self.sq != to)
        def _():
            self.copy(to, self.sq).start()

    def wait(self):
        for i in range(self.n_seq):
            @pl.when(self.sq != i)
            def _():
                self.copy(i, i).wait()


def front_kernel(cfg, lens, hidden, skip, valid_row, n1g, n1s, qw, qb, kw, vw, vb,
                 normed_out, mixed_out, pair_out, third_out, lse_out,
                 sp, st, rp, rt, smp, smt, rmp, rmt, bias, ssem, rsem, mssem, mrsem):
    n_dp, n_seq = cfg
    dp, sq = lax.axis_index("dp"), lax.axis_index("seq")
    rows = hidden.shape[0]
    half = rows // 2
    barrier = pltpu.get_barrier_semaphore()
    for d in range(1, n_seq):
        pl.semaphore_signal(barrier, inc=1, device_id=(dp, (sq + d) % n_seq), device_id_type=MESH)
    x = hidden[...].astype(jnp.float32)
    spread = x - jnp.mean(x, axis=-1, keepdims=True)
    inv = lax.rsqrt(jnp.mean(spread * spread, axis=-1, keepdims=True) + norm_eps)
    normed = (spread * inv * flat(n1g) + flat(n1s)).astype(jnp.bfloat16)
    normed_out[...] = normed
    swaps = [[Swap(n_seq, dp, sq, lambda to, t=t: sp.at[to, t], lambda me, t=t: rp.at[t, pl.ds(me * rows, rows)],
                   lambda d, t=t: ssem.at[0, t, d], lambda d, t=t: rsem.at[0, t, d]),
              Swap(n_seq, dp, sq, lambda to, t=t: st.at[to, t], lambda me, t=t: rt.at[t, me],
                   lambda d, t=t: ssem.at[1, t, d], lambda d, t=t: rsem.at[1, t, d])] for t in range(2)]
    swaps.append([Gather(n_seq, dp, sq, lambda to: sp.at[to, 2], lambda s: rp.at[2, pl.ds(s * rows, rows)],
                         lambda i: ssem.at[0, 2, i], lambda i: rsem.at[0, 2, i]),
                  Gather(n_seq, dp, sq, lambda to: st.at[to, 2], lambda s: rt.at[2, s],
                         lambda i: ssem.at[1, 2, i], lambda i: rsem.at[1, 2, i])])

    def lanes_of(v, tile):
        return v[:, tile * LANES : (tile + 1) * LANES]

    def place(t, r, pair, tile):
        sp[r, t] = pair
        st[r, t] = pack_third(tile[:half], tile[half:], r % 2)

    fresh_tiles = VFRESH // LANES
    reused = [r for r in range(n_seq) if PAIR_TILE[r] >= fresh_tiles]
    for r in reused:
        place(2, r, lanes_of(skip, PAIR_TILE[r] - fresh_tiles), lanes_of(skip, THIRD_TILE[r] - fresh_tiles))
    pl.semaphore_wait(barrier, n_seq - 1)
    for r in reused:
        swaps[2][0].start(r)
    for t in range(3):
        if t == 0:
            full = (matmul(normed, qw[...]) + flat(qb)).astype(jnp.bfloat16)
        elif t == 1:
            full = matmul(normed, kw[...]).astype(jnp.bfloat16)
        else:
            full = (matmul(normed, vw[...]) + flat(vb)).astype(jnp.bfloat16)
        for r in range(n_seq):
            if t < 2 or r not in reused:
                place(t, r, lanes_of(full, PAIR_TILE[r]), lanes_of(full, THIRD_TILE[r]))
        if t < 2:
            swaps[t][0].start()
        else:
            for r in range(n_seq):
                if r not in reused:
                    swaps[2][0].start(r)
    for t in range(3):
        if t < 2:
            swaps[t][1].start()
        else:
            for r in range(n_seq):
                swaps[2][1].start(r)
        rp[t, pl.ds(pl.multiple_of(sq * rows, rows), rows)] = sp[sq, t]
        rt[t, sq] = st[sq, t]
    for i in range(n_seq):
        cols = (i + 1) * rows
        bias[i * rows : (i + 1) * rows, 0:cols] = mask_bias(lens, valid_row, i * rows, rows, cols)
    back = [Gather(n_seq, dp, sq, lambda to: smp.at[to], lambda s: rmp.at[s], lambda i: mssem.at[0, i], lambda i: mrsem.at[0, i]),
            Gather(n_seq, dp, sq, lambda to: smt.at[to], lambda s: rmt.at[s], lambda i: mssem.at[1, i], lambda i: mrsem.at[1, i])]
    low = low_lanes()
    scale = 1.0 / math.sqrt(HDIM)
    keep = (jnp.where(low, scale, 0.0).astype(jnp.bfloat16), jnp.where(low, 0.0, scale).astype(jnp.bfloat16))

    def attend(q, k, v, block):
        scores = matmul_right_t(q, k) + block
        top = jnp.max(scores, axis=-1, keepdims=True)
        powered = jnp.exp(scores - top)
        total = jnp.sum(powered, axis=-1, keepdims=True)
        probs = (powered * (1.0 / total)).astype(jnp.bfloat16)
        return matmul(probs, v), top + jnp.log(total)

    for t in range(3):
        swaps[t][0].wait()
    lane = lax.broadcasted_iota(jnp.int32, (1, LANES), 1)
    for i in range(n_seq):
        here = slice(i * rows, (i + 1) * rows)
        cols = (i + 1) * rows
        block = bias[here, 0:cols]
        q, k, v = rp[0, here], rp[1, 0:cols], rp[2, 0:cols]
        o0, l0 = attend(q * keep[0], k, v, block)
        o1, l1 = attend(q * keep[1], k, v, block)
        smp[i] = jnp.where(low, o0, o1).astype(jnp.bfloat16)
        lse_out[here] = jnp.where(lane == 0, l0, l1)
        back[0].start(i)
    for t in range(3):
        swaps[t][1].wait()
        for s in range(n_seq):
            a, b = unpack_third(rt[t, s])
            third_out[t, s * rows : s * rows + half] = a
            third_out[t, s * rows + half : (s + 1) * rows] = b
    for i in range(n_seq):
        here = slice(i * rows, (i + 1) * rows)
        cols = (i + 1) * rows
        block = bias[here, 0:cols]
        o2, l2 = attend(third_out[0, here] * keep[0], third_out[1, 0:cols], third_out[2, 0:cols], block)
        smt[i] = pack_third(o2[:half], o2[half:], False)
        lse_out[here] = jnp.where(lane == 2, l2, lse_out[here])
        back[1].start(i)
    pair_out[...] = rp[...]
    rmp[sq] = smp[sq]
    rmt[sq] = smt[sq]
    back[0].wait()
    back[1].wait()
    for r in range(n_seq):
        c = PAIR_TILE[r] * LANES
        mixed_out[:, c : c + LANES] = rmp[r]
    for r in range(0, n_seq, 2):
        a, b = join_thirds(rmt[r], rmt[r + 1])
        c = THIRD_TILE[r] * LANES
        mixed_out[0:half, c : c + LANES] = a
        mixed_out[half:rows, c : c + LANES] = b


def front(mesh, hidden, skip, lens, valid, n1g, n1s, qw, qb, kw, vw, vb, collective_id):
    n_dp, n_seq = mesh.shape["dp"], mesh.shape["seq"]
    rows, d = hidden.shape
    group = rows * n_seq
    bf, f32 = jnp.bfloat16, jnp.float32
    vmem = pl.BlockSpec(memory_space=pltpu.VMEM)
    half = rows // 2
    dma = pltpu.SemaphoreType.DMA
    return pl.pallas_call(
        functools.partial(front_kernel, (n_dp, n_seq)),
        in_specs=[pl.BlockSpec(memory_space=pltpu.SMEM)] + [vmem] * 10,
        out_specs=(vmem,) * 5,
        out_shape=(jax.ShapeDtypeStruct((rows, d), bf), jax.ShapeDtypeStruct((rows, d), bf),
                   jax.ShapeDtypeStruct((3, group, LANES), bf), jax.ShapeDtypeStruct((3, group, LANES), bf),
                   jax.ShapeDtypeStruct((group, LANES), f32)),
        scratch_shapes=[
            pltpu.VMEM((n_seq, 3, rows, LANES), bf), pltpu.VMEM((n_seq, 3, half, LANES), bf),
            pltpu.VMEM((3, group, LANES), bf), pltpu.VMEM((3, n_seq, half, LANES), bf),
            pltpu.VMEM((n_seq, rows, LANES), bf), pltpu.VMEM((n_seq, half, LANES), bf),
            pltpu.VMEM((n_seq, rows, LANES), bf), pltpu.VMEM((n_seq, half, LANES), bf),
            pltpu.VMEM((group, group), f32),
            dma((2, 3, n_seq)), dma((2, 3, n_seq)), dma((2, n_seq)), dma((2, n_seq))],
        compiler_params=pltpu.CompilerParams(collective_id=collective_id, has_side_effects=True, vmem_limit_bytes=56 * 2**20),
        name="front",
    )(lens, hidden, skip, valid.reshape(1, -1), n1g, n1s, qw, qb, kw, vw, vb)


GELU_A = 0.044715


def back_kernel(cfg, lens, valid_row, mixed, hidden, og, valid_col, proj_w, proj_b, n2g, n2s, fc_b, out_b, n1g, lse, normed,
                pair_in, third_in, fc_w, out_w, qw, kw, vw,
                out, output, grad_input, grad_skip, small_z, small_out,
                nt_ref, xhat_ref, mid_ref, mlp_acc, two_acc, inv_ref, wf, wo, pair, third, part1,
                gs, gst, gp, gt, gthird, bias, dk_acc, dv_acc, dsp, dst, drp, drt, rows_in, part2,
                recv, gat, sbuf, load_sem, gssem, grsem, dssem, drsem, send_sem, recv_sem, local_sem, ssend, srecv_sem):
    n_dp, n_seq, halves, streams, plan, steps = cfg
    dp, sq = lax.axis_index("dp"), lax.axis_index("seq")
    rows, d = hidden.shape
    half = rows // 2
    bf, f32 = jnp.bfloat16, jnp.float32
    barrier, count = entry_barrier(n_dp, n_seq, dp, sq, True)

    def weight_copies(j):
        cols = pl.ds(j * FCH, FCH)
        return [pltpu.make_async_copy(fc_w.at[:, cols], wf.at[j % 2], load_sem.at[0, j]),
                pltpu.make_async_copy(out_w.at[cols], wo.at[j % 2], load_sem.at[1, j])]

    extra = [pltpu.make_async_copy(pair_in, pair, load_sem.at[2, 0]), pltpu.make_async_copy(third_in, third, load_sem.at[2, 1])]
    late = [pltpu.make_async_copy(qw, wf.at[0], load_sem.at[3, 0]), pltpu.make_async_copy(kw, wf.at[1], load_sem.at[3, 1]),
            pltpu.make_async_copy(vw, wo.at[0, :, pl.ds(0, VFRESH)], load_sem.at[3, 2])]
    for j in range(2):
        for copy in weight_copies(j):
            copy.start()
    for copy in extra:
        copy.start()
    x = hidden[...].astype(f32)
    attn = matmul(mixed[...], proj_w[...]) + flat(proj_b)
    middle = x + attn
    mid_ref[...] = middle
    real = valid_col[...]
    spread = middle - jnp.mean(middle, axis=-1, keepdims=True)
    inv = lax.rsqrt(jnp.mean(spread * spread, axis=-1, keepdims=True) + norm_eps)
    xhat = spread * inv
    xhat_ref[...] = xhat
    inv_ref[...] = jnp.broadcast_to(inv, inv_ref.shape)
    nt_ref[...] = (xhat * flat(n2g) + flat(n2s)).astype(bf)
    s0 = row_sum(jnp.sum(x * x, axis=-1, keepdims=True) * real)
    s1 = row_sum(jnp.sum(attn * attn, axis=-1, keepdims=True) * real)
    s3 = row_sum(real)
    word = lax.broadcasted_iota(jnp.int32, (1, WID), 1)
    sums = jnp.where(word == 0, s0, jnp.where(word == 1, s1, jnp.where(word == 3, s3, 0.0)))
    sbuf[0] = jnp.zeros_like(sbuf[0])
    sbuf[0, 7:8] = row_sum(og[...].astype(f32))
    pl.semaphore_wait(barrier, count)
    ex = Exchange(streams, halves, dp, sq, (part1, part2), out, recv, gat, (send_sem, recv_sem, local_sem))
    tiny = Small(n_dp, n_seq, dp, sq, sbuf, ssend, srecv_sem, small_z, small_out)
    task = iter(range(1, len(plan)))

    def advance():
        for s, k in plan[next(task)]:
            ex.step(s, k)

    def begin(phase, chunk):
        for s, st in enumerate(streams):
            if st[0] == phase and (chunk is None or st[4] == chunk):
                ex.start(s, 0)

    h1, h2 = halves
    for j in range(steps):
        for copy in weight_copies(j):
            copy.wait()
        slot = j % 2
        pre = matmul(nt_ref[...], wf[slot]) + fc_b[:, j * FCH : (j + 1) * FCH]
        sq_pre = pre * pre
        t = jnp.tanh(tanh_coef * (pre + GELU_A * sq_pre * pre))
        act = (0.5 * pre * (1.0 + t)).astype(bf)
        slope = 0.5 * (1.0 + t) + 0.5 * pre * (1.0 - t * t) * (tanh_coef * (1.0 + 3.0 * GELU_A * sq_pre))
        pre_grad = matmul_right_t(og[...], wo[slot]) * slope
        sbuf[0, 8 + j : 9 + j] = row_sum(pre_grad)
        pre_low = pre_grad.astype(bf)
        part1[j * CHUNK : (j + 1) * CHUNK] = matmul_left_t(act, og[...]).astype(bf).reshape(CHUNK, SUB, WID)
        part1[h1 + j * CHUNK : h1 + (j + 1) * CHUNK] = matmul_left_t(nt_ref[...], pre_low).astype(bf).reshape(CHUNK, SUB, WID)
        begin(0, j)
        advance()
        mlp = matmul(act, wo[slot])
        two = matmul_right_t(pre_low, wf[slot])
        if j == 0:
            mlp_acc[...] = mlp
            two_acc[...] = two
        else:
            mlp_acc[...] = mlp_acc[...] + mlp
            two_acc[...] = two_acc[...] + two
        if j + 2 < steps:
            for copy in weight_copies(j + 2):
                copy.start()
        advance()
    for copy in late:
        copy.start()
    two_grad = two_acc[...]
    xhat = xhat_ref[...]
    sbuf[0, 5:6] = row_sum(two_grad * xhat)
    sbuf[0, 6:7] = row_sum(two_grad)
    e = two_grad * flat(n2g)
    centre = jnp.mean(e, axis=-1, keepdims=True)
    along = jnp.mean(e * xhat, axis=-1, keepdims=True)
    grad = og[...].astype(f32) + (e - centre - xhat * along) * inv_ref[:, 0:1]
    grad_low = grad.astype(bf)
    full = matmul_right_t(grad_low, proj_w[...]).astype(bf)
    for r in range(n_seq):
        c = PAIR_TILE[r] * LANES
        gs[r] = full[:, c : c + LANES]
        c = THIRD_TILE[r] * LANES
        gst[r] = pack_third(full[:half, c : c + LANES], full[half:, c : c + LANES], r % 2)
    swap_pair = Swap(n_seq, dp, sq, lambda to: gs.at[to], lambda me: gp.at[pl.ds(me * rows, rows)], lambda i: gssem.at[0, i], lambda i: grsem.at[0, i])
    swap_third = Swap(n_seq, dp, sq, lambda to: gst.at[to], lambda me: gt.at[me], lambda i: gssem.at[1, i], lambda i: grsem.at[1, i])
    swap_pair.start()
    swap_third.start()
    advance()
    mlp_out = mlp_acc[...] + flat(out_b)
    output[...] = (mid_ref[...] + mlp_out).astype(bf)
    s2 = row_sum(jnp.sum(mlp_out * mlp_out, axis=-1, keepdims=True) * valid_col[...])
    sbuf[0, 12:13] = sums + jnp.where(word == 2, s2, 0.0)
    sbuf[0, 4:5] = row_sum(grad)
    mid_ref[...] = grad
    gw = matmul_left_t(mixed[...], grad_low).astype(bf)
    top = d // 2 // SUB
    at = steps * CHUNK
    part1[at : at + top] = gw[: d // 2].reshape(top, SUB, WID)
    part1[h1 + at : h1 + at + top] = gw[d // 2 :].reshape(top, SUB, WID)
    if h1 > at + top:
        for h in range(2):
            part1[h * h1 + at + top : (h + 1) * h1] = jnp.zeros((h1 - at - top, SUB, WID), bf)
    begin(0, steps)
    advance()
    gp[pl.ds(pl.multiple_of(sq * rows, rows), rows)] = gs[sq]
    gt[sq] = gst[sq]
    for i in range(n_seq):
        cols = (i + 1) * rows
        bias[i * rows : (i + 1) * rows, 0:cols] = mask_bias(lens, valid_row, i * rows, rows, cols).astype(bf)
    send = [Gather(n_seq, dp, sq, lambda to: dsp.at[to], lambda s: drp.at[s], lambda i: dssem.at[0, i], lambda i: drsem.at[0, i]),
            Gather(n_seq, dp, sq, lambda to: dst.at[to], lambda s: drt.at[s], lambda i: dssem.at[1, i], lambda i: drsem.at[1, i])]
    advance()
    for copy in extra:
        copy.wait()
    low = low_lanes()
    scale = 1.0 / math.sqrt(HDIM)
    keep = (jnp.where(low, scale, 0.0).astype(bf), jnp.where(low, 0.0, scale).astype(bf))
    ones = (jnp.where(low, 1.0, 0.0).astype(bf), jnp.where(low, 0.0, 1.0).astype(bf))

    def backward(q, k, v, g, block, total):
        probs = jnp.exp(matmul_right_t(q, k) + block - total)
        prob_grad = matmul_right_t(g, v)
        centre = jnp.sum(probs * prob_grad, axis=-1, keepdims=True)
        score_grad = (probs * (prob_grad - centre)).astype(bf)
        return matmul(score_grad, k), matmul_left_t(score_grad, q), matmul_left_t(probs.astype(bf), g)

    swap_pair.wait()
    for i in reversed(range(n_seq)):
        here = slice(i * rows, (i + 1) * rows)
        cols = (i + 1) * rows
        block = bias[here, 0:cols].astype(f32)
        q, k, v, g = pair[0, here], pair[1, 0:cols], pair[2, 0:cols], gp[here]
        dq0, dk0, dv0 = backward(q * keep[0], k, v, g * ones[0], block, lse[here, 0:1])
        dq1, dk1, dv1 = backward(q * keep[1], k, v, g * ones[1], block, lse[here, 1:2])
        if i == n_seq - 1:
            dk_acc[...] = dk0 + dk1
            dv_acc[...] = dv0 + dv1
        else:
            dk_acc[0:cols] = dk_acc[0:cols] + (dk0 + dk1)
            dv_acc[0:cols] = dv_acc[0:cols] + (dv0 + dv1)
        dsp[i, 0] = (jnp.where(low, dq0, dq1) * scale).astype(bf)
        dsp[i, 1] = dk_acc[here].astype(bf)
        dsp[i, 2] = dv_acc[here].astype(bf)
        send[0].start(i)
        advance()
    swap_third.wait()
    for s in range(n_seq):
        a, b = unpack_third(gt[s])
        gthird[s * rows : s * rows + half] = a
        gthird[s * rows + half : (s + 1) * rows] = b
    for i in reversed(range(n_seq)):
        here = slice(i * rows, (i + 1) * rows)
        cols = (i + 1) * rows
        block = bias[here, 0:cols].astype(f32)
        dq, dk, dv = backward(third[0, here] * keep[0], third[1, 0:cols], third[2, 0:cols], gthird[here], block, lse[here, 2:3])
        if i == n_seq - 1:
            dk_acc[...] = dk
            dv_acc[...] = dv
        else:
            dk_acc[0:cols] = dk_acc[0:cols] + dk
            dv_acc[0:cols] = dv_acc[0:cols] + dv
        dq = dq * scale
        dst[i, 0] = pack_third(dq[:half], dq[half:], False)
        for t, a in ((1, dk_acc), (2, dv_acc)):
            dst[i, t] = pack_third(a[i * rows : i * rows + half], a[i * rows + half : (i + 1) * rows], False)
        send[1].start(i)
        advance()
    drp[sq] = dsp[sq]
    drt[sq] = dst[sq]
    x = hidden[...].astype(f32)
    spread = x - jnp.mean(x, axis=-1, keepdims=True)
    inv = lax.rsqrt(jnp.mean(spread * spread, axis=-1, keepdims=True) + norm_eps)
    xhat = spread * inv
    send[0].wait()
    for t in range(3):
        for r in range(n_seq):
            c = PAIR_TILE[r] * LANES
            rows_in[t, :, c : c + LANES] = drp[r, t]
    advance()
    send[1].wait()
    for t in range(3):
        for r in range(0, n_seq, 2):
            a, b = join_thirds(drt[r, t], drt[r + 1, t])
            c = THIRD_TILE[r] * LANES
            rows_in[t, 0:half, c : c + LANES] = a
            rows_in[t, half:rows, c : c + LANES] = b
    nl = normed[...]
    dq, dk, dv = rows_in[0], rows_in[1], rows_in[2]
    fresh = dv[:, 0:VFRESH]
    grad_skip[...] = dv[:, VFRESH:]
    units_d = d // SUB
    uv = d // 4 // SUB
    part2[0:units_d] = matmul_left_t(nl, dq).astype(bf).reshape(units_d, SUB, WID)
    part2[h2 : h2 + units_d] = matmul_left_t(nl, dk).astype(bf).reshape(units_d, SUB, WID)
    gv = matmul_left_t(nl, fresh).astype(bf)
    for h in range(2):
        for side in range(2):
            r0 = side * (d // 2) + h * (d // 4)
            part2[h * h2 + units_d : h * h2 + units_d + uv, :, side * VFRESH : (side + 1) * VFRESH] = (
                gv[r0 : r0 + d // 4].reshape(uv, SUB, VFRESH))
        if h2 > units_d + uv:
            part2[h * h2 + units_d + uv : (h + 1) * h2] = jnp.zeros((h2 - units_d - uv, SUB, WID), bf)
    begin(1, None)
    advance()
    for copy in late:
        copy.wait()
    normed_grad = matmul_right_t(dq, wf[0]) + matmul_right_t(dk, wf[1]) + matmul_right_t(fresh, wo[0, :, 0:VFRESH])
    f = normed_grad * flat(n1g)
    centre = jnp.mean(f, axis=-1, keepdims=True)
    along = jnp.mean(f * xhat, axis=-1, keepdims=True)
    grad_input[...] = (mid_ref[...] + (f - centre - xhat * along) * inv).astype(bf)
    sbuf[0, 0:1] = row_sum(normed_grad * xhat)
    sbuf[0, 1:2] = row_sum(normed_grad)
    sbuf[0, 2:3] = row_sum(dq.astype(f32))
    sbuf[0, 3:4, 0:VFRESH] = row_sum(fresh.astype(f32))
    tiny.copy(0).start()
    todo = plan[next(task)]
    gap = max(1, len(todo) // (len(tiny.dims) + 2))
    for left, (s, k) in enumerate(todo):
        ex.step(s, k)
        if left % gap == gap - 1:
            tiny.step()
    tiny.rest()


def back(mesh, lens, valid, mixed, hidden, og, valid_col, proj_w, proj_b, n2g, n2s, fc_b, out_b, n1g, lse, normed,
         pair, third, fc_w, out_w, qw, kw, vw, collective_id):
    n_dp, n_seq = mesh.shape["dp"], mesh.shape["seq"]
    rows, d = hidden.shape
    group = rows * n_seq
    half = rows // 2
    steps = fc_w.shape[1] // FCH
    bf, f32 = jnp.bfloat16, jnp.float32
    quantum = n_dp // 2 * n_seq
    needed = (steps * CHUNK + d // 2 // SUB, d // SUB + d // 4 // SUB)
    halves = tuple(-(-n // quantum) * quantum for n in needed)
    streams = plan_streams(n_dp, n_seq, halves, steps)
    plan, _ = schedule(streams, steps, rows)
    n_st = 2 * (bits_of(n_dp) + bits_of(n_seq))
    n_small = bits_of(n_dp) + bits_of(n_seq)
    ns = len(streams)
    vmem = pl.BlockSpec(memory_space=pltpu.VMEM)
    hbm = pl.BlockSpec(memory_space=pl.ANY)
    dma = pltpu.SemaphoreType.DMA
    units = lambda n: pltpu.VMEM((n, SUB, WID), bf)
    wide = lambda: pltpu.VMEM((rows, d), f32)
    sshape = jax.ShapeDtypeStruct((16, WID), f32)
    args = (lens, valid.reshape(1, -1), mixed, hidden, og, valid_col, proj_w, proj_b, n2g, n2s, fc_b.reshape(1, -1), out_b, n1g, lse, normed,
            pair, third, fc_w, out_w, qw, kw, vw)
    outs = pl.pallas_call(
        functools.partial(back_kernel, (n_dp, n_seq, halves, streams, plan, steps)),
        in_specs=[pl.BlockSpec(memory_space=pltpu.SMEM)] + [vmem] * 14 + [hbm] * 7,
        out_specs=(hbm, vmem, vmem, vmem, vmem, vmem),
        out_shape=(jax.ShapeDtypeStruct((2 * sum(halves), SUB, WID), bf), jax.ShapeDtypeStruct((rows, d), bf),
                   jax.ShapeDtypeStruct((rows, d), bf), jax.ShapeDtypeStruct((rows, d - VFRESH), bf), sshape, sshape),
        scratch_shapes=[
            pltpu.VMEM((rows, d), bf), wide(), wide(), wide(), wide(), pltpu.VMEM((rows, LANES), f32),
            pltpu.VMEM((2, d, FCH), bf), pltpu.VMEM((2, FCH, d), bf),
            pltpu.VMEM((3, group, LANES), bf), pltpu.VMEM((3, group, LANES), bf), units(2 * halves[0]),
            pltpu.VMEM((n_seq, rows, LANES), bf), pltpu.VMEM((n_seq, half, LANES), bf),
            pltpu.VMEM((group, LANES), bf), pltpu.VMEM((n_seq, half, LANES), bf), pltpu.VMEM((group, LANES), bf),
            pltpu.VMEM((group, group), bf), pltpu.VMEM((group, LANES), f32), pltpu.VMEM((group, LANES), f32),
            pltpu.VMEM((n_seq, 3, rows, LANES), bf), pltpu.VMEM((n_seq, 3, half, LANES), bf),
            pltpu.VMEM((n_seq, 3, rows, LANES), bf), pltpu.VMEM((n_seq, 3, half, LANES), bf),
            pltpu.VMEM((3, rows, d), bf), units(2 * halves[1]),
            units(Exchange.recv_total(streams)), units(sum(halves)),
            pltpu.VMEM((2 * n_small, 16, WID), f32), dma((4, max(4, steps))),
            dma((2, n_seq)), dma((2, n_seq)), dma((2, n_seq)), dma((2, n_seq)),
            dma((ns, n_st)), dma((ns, n_st)), dma((ns,)), dma((n_small,)), dma((n_small,))],
        compiler_params=pltpu.CompilerParams(collective_id=collective_id, has_side_effects=True, vmem_limit_bytes=67043328),
        name="back",
    )(*args)
    return outs, halves


def local(
    mesh,
    hidden_in,
    skip_values,
    out_grad,
    doc_lens,
    valid,
    norm1_gain,
    norm1_shift,
    query_w,
    query_b,
    key_w,
    value_w,
    value_b,
    proj_w,
    proj_b,
    norm2_gain,
    norm2_shift,
    fc_w,
    fc_b,
    out_w,
    out_b,
):
    seq_size = lax.axis_size("seq")
    seq_rank = lax.axis_index("seq")
    tok_rows = hidden_in.shape[0]
    valid_col = lax.dynamic_slice_in_dim(valid, seq_rank * tok_rows, tok_rows, 0).astype(jnp.float32)[:, None]
    normed, mixed, pair, third, lse = front(
        mesh, hidden_in, skip_values, doc_lens, valid, norm1_gain, norm1_shift, query_w, query_b, key_w, value_w, value_b, 0
    )
    (summed, output, grad_input, grad_skip, small_z, small_all), halves = back(
        mesh, doc_lens, valid, mixed, hidden_in, out_grad, valid_col, proj_w, proj_b, norm2_gain, norm2_shift, fc_b, out_b,
        norm1_gain, lse, normed, pair, third, fc_w, out_w, query_w, key_w, value_w, 1
    )
    (
        grad_out_w, grad_fc_w, grad_proj_w, grad_query_w, grad_key_w, grad_value_w,
        grad_norm1_gain, grad_norm1_shift, grad_query_b, grad_value_b, grad_proj_b, grad_norm2_gain, grad_norm2_shift,
        grad_out_b, grad_fc_b, norm_values, grad_input, grad_skip,
    ) = widen(summed.reshape(-1, WID), small_all, small_z, grad_input, grad_skip, halves, D, fc_w.shape[1], VFRESH)
    return (
        output,
        grad_input,
        grad_skip,
        grad_norm1_gain,
        grad_norm1_shift,
        grad_query_w,
        grad_query_b,
        grad_key_w,
        grad_value_w,
        grad_value_b,
        grad_proj_w,
        grad_proj_b,
        grad_norm2_gain,
        grad_norm2_shift,
        grad_fc_w,
        grad_fc_b,
        grad_out_w,
        grad_out_b,
        norm_values,
    )


def solution(mesh):
    placed = (
        P(("dp", "seq"), None),
        P(("dp", "seq"), None),
        P(("dp", "seq"), None),
        P("dp", None),
        P("dp"),
        P(),
        P(),
        P(),
        P(),
        P(),
        P(),
        P(),
        P(),
        P(),
        P(),
        P(),
        P(),
        P(),
        P(),
        P(),
    )
    return jax.shard_map(
        functools.partial(local, mesh),
        mesh=mesh,
        in_specs=placed,
        out_specs=(
            P(("dp", "seq"), None),
            P(("dp", "seq"), None),
            P(("dp", "seq"), None),
            P(),
            P(),
            P(),
            P(),
            P(),
            P(),
            P(),
            P(),
            P(),
            P(),
            P(),
            P(),
            P(),
            P(),
            P(),
            P("dp", None),
        ),
        check_vma=False,
    )
```

```python
import functools
import math

import jax
import jax.numpy as jnp
from jax import lax
from jax.experimental import pallas as pl
from jax.experimental.pallas import tpu as pltpu
from jax.sharding import PartitionSpec as P

D = 768
HEADS = 12
HDIM = 64
VFRESH = 384


norm_eps = 1e-05
square_eps = 1e-06
tanh_coef = 0.7978845608028654
masked_score = -1e30


MESH = pl.DeviceIdType.MESH
SUB = 8
WID = 768
UNIT_BYTES = SUB * WID * 2
FCH = 768
CHUNK = FCH // SUB
MLP_TIMES = (2.2, 1.1)
TASKS = (2.5, 2.5, 1.5, 2.3, 1.7, 1.2, 0.7, 1.6, 0.9, 0.7, 0.5, 0.8, 4.5, 3.0)
ENTRY = 3.5
MARGIN = 1.5
TASK_HOLDS = (0.0, 0.0, 0.0, 0.0, 0.0, 0.0, 0.0, 0.0, 0.0, 0.0, 0.0, 0.0, 0.0, 0.0)
SIZES = ((2, 2, 2, 2, 2, 2, 2, 2, 2, 2, 2, 2, 3), (2, 2, 2, 2))
KINDS = (1, 0, 0, 1, 1, 0, 1, 0, 0, 1, 1, 1, 0, 1, 3, 0, 2)
HOLDS = (7.9, 37.1, 25.1, 62.4, 39.0, 7.3, 27.8, 41.0, 59.4, 8.5, 57.8, 22.0, 45.0, 0, 0.8, 10.9, 45.9)
LINK = 0.044
LATENCY = 2.3
AR_COST = 0.35


def bits_of(n):
    return n.bit_length() - 1


def partner(dim, dp, sq):
    kind, j = dim
    step = 1 << j
    if kind == "dp":
        bit = (dp // step) % 2
        return bit, (dp + step - 2 * step * bit, sq)
    bit = (sq // step) % 2
    return bit, (dp, sq + step - 2 * step * bit)


def plan_streams(n_dp, n_seq, halves, steps):
    dpb = [("dp", j) for j in range(1, bits_of(n_dp))]
    sqb = [("seq", j) for j in range(bits_of(n_seq))]
    mid = len(dpb) // 2
    one, two = dpb[:mid], dpb[mid:]
    orders = (one + two + sqb, two + one + sqb, one + sqb + two, two + sqb + one, sqb + one + two, sqb + two + one)
    quantum = (n_dp // 2) * n_seq
    streams = []
    for phase, half_units in enumerate(halves):
        total = half_units // quantum
        sizes = SIZES[phase]
        if sum(sizes) != total:
            sizes = (2,) * (total // 2) + (1,) * (total % 2)
        first = 0
        for size in sizes:
            n = size * quantum
            chunk = min(steps, (first + n - 1) // CHUNK)
            streams.append((phase, first, n, orders[KINDS[len(streams) % len(KINDS)]], chunk if phase == 0 else -1))
            first += n
    return streams


def schedule(streams, steps, rows):
    free = {}
    stages = []
    for phase, first, n, order, _ in streams:
        seq = [(("dp", 0), n)]
        size = n
        for d in order:
            size //= 2
            seq.append((d, size))
        for d in reversed(order):
            seq.append((d, size))
            size *= 2
        stages.append(seq + [(("dp", 0), n)])

    def flow(needs, t):
        begin = max([t] + [free.get(r, 0.0) for r, _ in needs])
        for r, dur in needs:
            free[r] = begin + dur
        return begin + max(dur for _, dur in needs) + LATENCY

    flying = []

    def launch(s, k, t):
        d, size = stages[s][k]
        b = size * UNIT_BYTES / 1e6
        if d == ("dp", 0):
            needs = [("c", b / 0.5)]
        elif d[0] == "dp":
            needs = [(d, b / LINK)]
        elif d[1] == 0:
            needs = [("end", b / LINK)]
        else:
            needs = [("mid", 2 * b / LINK), ("end", b / LINK)]
        end = flow(needs, t)
        flying.append((max(end, HOLDS[s % len(HOLDS)]) if k == 0 else end, s, k))

    block = rows * LANES * 2 / 1e6 / LINK
    arrive = {}
    durations = [MLP_TIMES[i % 2] for i in range(2 * steps)] + list(TASKS)
    n_tasks = len(durations)
    plan = [[] for _ in range(n_tasks + 1)]
    t, task = ENTRY, 0
    while task < n_tasks or flying:
        ready = None
        at_task = task - 2 * steps
        if task < n_tasks:
            needs = {3: ("grad pair",), 7: ("grad third",), 11: ("pair",), 12: ("third",)}.get(at_task, ())
            ready = max([TASK_HOLDS[at_task] if at_task >= 0 else 0.0] + [arrive[x] for x in needs])
        flying.sort()
        arrived = flying and flying[0][0] + MARGIN <= t
        if ready is not None and not arrived and (ready <= t or not flying or ready <= flying[0][0]):
            t = max(t, ready) + durations[task]
            begun = []
            if at_task < 0 and task % 2 == 0:
                begun = [s for s, st in enumerate(streams) if st[0] == 0 and st[4] == task // 2]
            if at_task == 0:
                arrive["grad pair"] = flow([("mid", 4 * block), ("end", 3 * block)], t)
                arrive["grad third"] = flow([("mid", 2 * block), ("end", 1.5 * block)], t)
            if at_task == 1:
                begun = [s for s, st in enumerate(streams) if st[0] == 0 and st[4] == steps]
            if 3 <= at_task <= 6:
                arrive["pair"] = flow([("mid", 3 * block), ("end", 2.25 * block)], t) + 2.0
            if 7 <= at_task <= 10:
                arrive["third"] = flow([("mid", 1.5 * block), ("end", 1.125 * block)], t) + 2.0
            if at_task == 12:
                begun = [s for s, st in enumerate(streams) if st[0] == 1]
            for s in begun:
                launch(s, 0, t)
            task += 1
            continue
        at, s, k = flying.pop(0)
        plan[task].append((s, k))
        t = max(t, at) + AR_COST
        if k + 1 < len(stages[s]):
            launch(s, k + 1, t)
    return plan, t


class Exchange:
    def __init__(self, streams, halves, dp, sq, parts, out, recv, gat, sems):
        self.streams, self.halves = streams, halves
        self.dp, self.sq = dp, sq
        self.parts, self.out, self.recv, self.gat = parts, out, recv, gat
        self.send_sem, self.recv_sem, self.local_sem = sems
        self.cbit, self.cdev = partner(("dp", 0), dp, sq)
        self.base = [sum(halves[:p]) for p in range(len(halves))]
        self.off = [[st[1]] for st in streams]
        self.roff = []
        r = 0
        for phase, first, n, order, _ in streams:
            rows = [r]
            r += n
            size = n
            for _ in order:
                size //= 2
                rows.append(r)
                r += size
            self.roff.append(rows)

    @staticmethod
    def recv_total(streams):
        r = 0
        for phase, first, n, order, _ in streams:
            r += n
            for i in range(len(order)):
                r += n >> (i + 1)
        return r

    def n_stages(self, s):
        return 2 * (len(self.streams[s][3]) + 1)

    def remote(self, s, k, src, dst, dev):
        return pltpu.make_async_remote_copy(
            src_ref=src, dst_ref=dst, send_sem=self.send_sem.at[s, k], recv_sem=self.recv_sem.at[s, k],
            device_id=dev, device_id_type=MESH)

    def copies(self, s, k):
        phase, first, n, order, _ = self.streams[s]
        depth = len(order)
        half_units, base = self.halves[phase], self.base[phase]
        part = self.parts[phase]
        own = self.cbit * half_units
        if k == 0:
            other = (1 - self.cbit) * half_units + first
            return self.remote(s, k, part.at[pl.ds(other, n)], self.recv.at[pl.ds(self.roff[s][0], n)], self.cdev), None
        if k <= depth:
            half = n >> k
            bit, dev = partner(order[k - 1], self.dp, self.sq)
            at = own + self.off[s][k - 1] + (1 - bit) * half
            return self.remote(s, k, part.at[pl.ds(at, half)], self.recv.at[pl.ds(self.roff[s][k], half)], dev), None
        g = 2 * depth + 1 - k
        if g >= 1:
            half = n >> g
            bit, dev = partner(order[g - 1], self.dp, self.sq)
            piece = self.gat.at[pl.ds(base + self.off[s][g], half)]
            return self.remote(s, k, piece, piece, dev), None
        piece = self.gat.at[pl.ds(base + first, n)]
        there = self.out.at[pl.ds(2 * base + own + first, n)]
        return self.remote(s, k, piece, there, self.cdev), pltpu.make_async_copy(piece, there, self.local_sem.at[s])

    def start(self, s, k):
        for c in self.copies(s, k):
            if c is not None:
                c.start()

    def finish(self, s, k):
        phase, first, n, order, _ = self.streams[s]
        depth = len(order)
        remote, local = self.copies(s, k)
        remote.wait()
        if local is not None:
            local.wait()
        if k <= depth:
            half = n >> k
            if k > 0:
                bit, _ = partner(order[k - 1], self.dp, self.sq)
                self.off[s].append(self.off[s][k - 1] + bit * half)
            at = self.cbit * self.halves[phase] + self.off[s][k]
            to = (self.gat, self.base[phase] + self.off[s][k]) if k == depth else (self.parts[phase], at)
            self.add(self.parts[phase], at, self.roff[s][k], half, to)

    def add(self, part, at, roff, n, to):
        recv = self.recv
        dst, first = to
        step = next(d for d in (8, 6, 4, 3, 2, 1) if n % d == 0)

        def body(i, c):
            a = pl.ds(at + i * step, step)
            b = pl.ds(roff + i * step, step)
            dst[pl.ds(first + i * step, step)] = part[a] + recv[b]
            return c

        lax.fori_loop(0, n // step, body, 0)

    def step(self, s, k):
        self.finish(s, k)
        if k + 1 < self.n_stages(s):
            self.start(s, k + 1)


class Small:
    def __init__(self, n_dp, n_seq, dp, sq, buf, ssend, srecv, small_z, small_out):
        self.dims = [("seq", j) for j in range(bits_of(n_seq))] + [("dp", j) for j in range(bits_of(n_dp))]
        self.nz = bits_of(n_seq)
        self.dp, self.sq, self.buf, self.ssend, self.srecv = dp, sq, buf, ssend, srecv
        self.small_z, self.small_out = small_z, small_out
        self.done = 0

    def copy(self, i):
        _, dev = partner(self.dims[i], self.dp, self.sq)
        return pltpu.make_async_remote_copy(
            src_ref=self.buf.at[2 * i], dst_ref=self.buf.at[2 * i + 1], send_sem=self.ssend.at[i],
            recv_sem=self.srecv.at[i], device_id=dev, device_id_type=MESH)

    def begin(self, value):
        self.buf[0] = value
        self.copy(0).start()

    def step(self):
        i = self.done
        if i == len(self.dims):
            return
        self.copy(i).wait()
        total = self.buf[2 * i] + self.buf[2 * i + 1]
        self.done = i + 1
        if self.done == self.nz:
            self.small_z[...] = total
        if self.done < len(self.dims):
            self.buf[2 * self.done] = total
            self.copy(self.done).start()
        else:
            self.small_out[...] = total

    def rest(self):
        while self.done < len(self.dims):
            self.step()


def entry_barrier(n_dp, n_seq, dp, sq, all_seq):
    barrier = pltpu.get_barrier_semaphore()
    peers = [partner(("dp", j), dp, sq)[1] for j in range(bits_of(n_dp))]
    if all_seq:
        peers += [(dp, (sq + d) % n_seq) for d in range(1, n_seq)]
    else:
        peers += [partner(("seq", j), dp, sq)[1] for j in range(bits_of(n_seq))]
    for dev in peers:
        pl.semaphore_signal(barrier, inc=1, device_id=dev, device_id_type=MESH)
    return barrier, len(peers)


def matmul(former, latter):
    return jnp.dot(former, latter, preferred_element_type=jnp.float32)


def matmul_right_t(former, latter):
    return lax.dot_general(
        former, latter, (((1,), (1,)), ((), ())), preferred_element_type=jnp.float32
    )


def matmul_left_t(former, latter):
    return lax.dot_general(
        former, latter, (((0,), (0,)), ((), ())), preferred_element_type=jnp.float32
    )


def flat(ref):
    return ref[...].reshape(1, -1)


def row_sum(v):
    return jnp.sum(v, axis=0, keepdims=True)


PIECE = 384
VPIECE = 192


def widen_kernel(cfg, src, small, small_z, gi_in, gs_in, *refs):
    pieces, n_out = cfg
    outs, vectors, (norms, gi_out, gs_out) = refs[:n_out], refs[n_out : n_out + 9], refs[n_out + 9 : n_out + 12]
    inbuf, stage, gi_buf, gs_buf, in_sem, out_sem, row_sem = refs[n_out + 12 :]
    depth = inbuf.shape[0]

    def fetch(i):
        size = VPIECE if pieces[i][4] else PIECE
        return pltpu.make_async_copy(src.at[pl.ds(pieces[i][0], size)], inbuf.at[i % depth, pl.ds(0, size)], in_sem.at[i % depth])

    def put(i):
        slot = i % depth
        _, which, row, col, split = pieces[i]
        out = outs[which]
        if split:
            return [pltpu.make_async_copy(stage.at[slot, pl.ds(0, VPIECE), pl.ds(h * VFRESH, VFRESH)],
                                          out.at[pl.ds(row + h * VFRESH, VPIECE)], out_sem.at[slot, h]) for h in range(2)]
        return [pltpu.make_async_copy(stage.at[slot], out.at[pl.ds(row, PIECE), pl.ds(col, WID)], out_sem.at[slot, 0])]

    n = len(pieces)
    for i in range(min(depth, n)):
        fetch(i).start()
    row_in = [pltpu.make_async_copy(gi_in, gi_buf, row_sem.at[0]), pltpu.make_async_copy(gs_in, gs_buf, row_sem.at[1])]
    row_out = [pltpu.make_async_copy(gi_buf, gi_out, row_sem.at[2]), pltpu.make_async_copy(gs_buf, gs_out, row_sem.at[3])]
    for c in row_in:
        c.start()
    for i in range(n):
        slot = i % depth
        fetch(i).wait()
        if i >= depth:
            for c in put(i - depth):
                c.wait()

        def body(r, c):
            rows = pl.ds(r * 32, 32)
            stage[slot, rows] = inbuf[slot, rows].astype(jnp.float32)
            return c

        lax.fori_loop(0, (VPIECE if pieces[i][4] else PIECE) // 32, body, 0)
        for c in put(i):
            c.start()
        if i + depth < n:
            fetch(i + depth).start()
        if i == depth:
            for a, b in zip(row_in, row_out):
                a.wait()
                b.start()
            for row, v in zip((0, 1, 2, 3, 4, 5, 6, 7), vectors):
                v[...] = small[row, 0 : v.shape[0]]
            for q in range(vectors[8].shape[0] // WID):
                vectors[8][q * WID : (q + 1) * WID] = small[8 + q, :]
            sums = small_z[12:13, 0:4]
            norms[...] = jnp.sqrt(sums[:, 0:3] / (sums[:, 3:4] * D) + square_eps)
    for i in range(max(0, n - depth), n):
        for c in put(i):
            c.wait()
    for c in row_out:
        c.wait()


def widen(summed, small, small_z, grad_input, grad_skip, halves, d, ff, vf):
    one, two = halves[0] * SUB, halves[1] * SUB
    pieces = []
    for j in range(ff // PIECE):
        pieces.append((j * PIECE, 0, j * PIECE, 0, False))
        pieces.append((one + j * PIECE, 1, (j % 2) * PIECE, j // 2 * FCH, False))
    for h in range(2):
        pieces.append((h * one + ff, 2, h * PIECE, 0, False))
    for w in range(2):
        for h in range(2):
            pieces.append((2 * one + w * two + h * PIECE, 3 + w, h * PIECE, 0, False))
    for h in range(2):
        pieces.append((2 * one + h * two + d, 5, h * VPIECE, 0, True))
    f32, bf = jnp.float32, jnp.bfloat16
    depth = 8
    hbm = pl.BlockSpec(memory_space=pl.ANY)
    vmem = pl.BlockSpec(memory_space=pltpu.VMEM)
    shapes = [(ff, d), (d, ff), (d, d), (d, d), (d, d), (d, vf)]
    vectors = [(d,), (d,), (d,), (vf,), (d,), (d,), (d,), (d,), (ff,)]
    out_shape = [jax.ShapeDtypeStruct(s, f32) for s in shapes + vectors + [(1, 3)]]
    out_shape += [jax.ShapeDtypeStruct(g.shape, bf) for g in (grad_input, grad_skip)]
    return pl.pallas_call(
        functools.partial(widen_kernel, (pieces, len(shapes))),
        in_specs=[hbm, vmem, vmem, hbm, hbm], out_specs=(hbm,) * 6 + (vmem,) * 10 + (hbm,) * 2, out_shape=tuple(out_shape),
        scratch_shapes=[pltpu.VMEM((depth, PIECE, WID), bf), pltpu.VMEM((depth, PIECE, WID), f32),
                        pltpu.VMEM(grad_input.shape, bf), pltpu.VMEM(grad_skip.shape, bf),
                        pltpu.SemaphoreType.DMA((depth,)), pltpu.SemaphoreType.DMA((depth, 2)), pltpu.SemaphoreType.DMA((4,))],
        compiler_params=pltpu.CompilerParams(vmem_limit_bytes=62 * 2**20),
        name="widen",
    )(summed, small, small_z, grad_input, grad_skip)


LANES = 128
PAIR_TILE = (0, 2, 3, 5)
THIRD_TILE = (1, 1, 4, 4)


def low_lanes():
    return lax.broadcasted_iota(jnp.int32, (1, LANES), 1) < HDIM


def turn(v):
    return pltpu.roll(v, HDIM, 1)


def pack_third(first, second, upper):
    first, second = first.astype(jnp.float32), second.astype(jnp.float32)
    if upper:
        both = jnp.where(low_lanes(), turn(first), second)
    else:
        both = jnp.where(low_lanes(), first, turn(second))
    return both.astype(jnp.bfloat16)


def unpack_third(both):
    wide = both.astype(jnp.float32)
    low = low_lanes()
    first = jnp.where(low, wide, 0.0).astype(jnp.bfloat16)
    second = jnp.where(low, turn(wide), 0.0).astype(jnp.bfloat16)
    return first, second


def join_thirds(one, two):
    one, two = one.astype(jnp.float32), two.astype(jnp.float32)
    low = low_lanes()
    first = jnp.where(low, one, turn(two)).astype(jnp.bfloat16)
    second = jnp.where(low, turn(one), two).astype(jnp.bfloat16)
    return first, second


def split_tiles(tiles, pair_dst, third_dst, rows, n_seq):
    half = rows // 2
    for r in range(n_seq):
        pair_dst(r, tiles[PAIR_TILE[r]])
        t = tiles[THIRD_TILE[r]]
        third_dst(r, pack_third(t[:half], t[half:], r % 2))


def mask_bias(lens, valid_row, first, rows, cols):
    one = lens[0, 0]
    two = one + lens[0, 1]
    i = first + lax.broadcasted_iota(jnp.int32, (rows, 1), 0)
    j = lax.broadcasted_iota(jnp.int32, (1, cols), 1)
    seg_i = (i >= one).astype(jnp.int32) + (i >= two).astype(jnp.int32)
    seg_j = (j >= one).astype(jnp.int32) + (j >= two).astype(jnp.int32)
    real = valid_row[:, 0:cols] > 0
    code = jnp.where(real, seg_j, -1)
    same = (code == seg_i) & (j <= i)
    return jnp.where(same | (i == j), 0.0, masked_score)


class Swap:
    def __init__(self, n_seq, dp, sq, send, recv, ssem, rsem):
        self.n_seq, self.dp, self.sq = n_seq, dp, sq
        self.send, self.recv, self.ssem, self.rsem = send, recv, ssem, rsem

    def copy(self, d):
        to = (self.sq + d) % self.n_seq
        return pltpu.make_async_remote_copy(
            src_ref=self.send(to), dst_ref=self.recv(self.sq), send_sem=self.ssem(d), recv_sem=self.rsem(d),
            device_id=(self.dp, to), device_id_type=MESH)

    def start(self):
        for d in range(1, self.n_seq):
            self.copy(d).start()

    def wait(self):
        for d in range(1, self.n_seq):
            self.copy(d).wait()


class Gather:
    def __init__(self, n_seq, dp, sq, send, recv, ssem, rsem):
        self.n_seq, self.dp, self.sq = n_seq, dp, sq
        self.send, self.recv, self.ssem, self.rsem = send, recv, ssem, rsem

    def copy(self, to, slot):
        return pltpu.make_async_remote_copy(
            src_ref=self.send(to), dst_ref=self.recv(slot), send_sem=self.ssem(to), recv_sem=self.rsem(slot),
            device_id=(self.dp, to), device_id_type=MESH)

    def start(self, to):
        @pl.when(self.sq != to)
        def _():
            self.copy(to, self.sq).start()

    def wait(self):
        for i in range(self.n_seq):
            @pl.when(self.sq != i)
            def _():
                self.copy(i, i).wait()


def front_kernel(cfg, lens, hidden, skip, valid_row, n1g, n1s, qw, qb, kw, vw, vb,
                 normed_out, mixed_out, pair_out, third_out, lse_out,
                 sp, st, rp, rt, smp, smt, rmp, rmt, bias, ssem, rsem, mssem, mrsem):
    n_dp, n_seq = cfg
    dp, sq = lax.axis_index("dp"), lax.axis_index("seq")
    rows = hidden.shape[0]
    half = rows // 2
    barrier = pltpu.get_barrier_semaphore()
    for d in range(1, n_seq):
        pl.semaphore_signal(barrier, inc=1, device_id=(dp, (sq + d) % n_seq), device_id_type=MESH)
    x = hidden[...].astype(jnp.float32)
    spread = x - jnp.mean(x, axis=-1, keepdims=True)
    inv = lax.rsqrt(jnp.mean(spread * spread, axis=-1, keepdims=True) + norm_eps)
    normed = (spread * inv * flat(n1g) + flat(n1s)).astype(jnp.bfloat16)
    normed_out[...] = normed
    swaps = [[Swap(n_seq, dp, sq, lambda to, t=t: sp.at[to, t], lambda me, t=t: rp.at[t, pl.ds(me * rows, rows)],
                   lambda d, t=t: ssem.at[0, t, d], lambda d, t=t: rsem.at[0, t, d]),
              Swap(n_seq, dp, sq, lambda to, t=t: st.at[to, t], lambda me, t=t: rt.at[t, me],
                   lambda d, t=t: ssem.at[1, t, d], lambda d, t=t: rsem.at[1, t, d])] for t in range(2)]
    swaps.append([Gather(n_seq, dp, sq, lambda to: sp.at[to, 2], lambda s: rp.at[2, pl.ds(s * rows, rows)],
                         lambda i: ssem.at[0, 2, i], lambda i: rsem.at[0, 2, i]),
                  Gather(n_seq, dp, sq, lambda to: st.at[to, 2], lambda s: rt.at[2, s],
                         lambda i: ssem.at[1, 2, i], lambda i: rsem.at[1, 2, i])])

    def lanes_of(v, tile):
        return v[:, tile * LANES : (tile + 1) * LANES]

    def place(t, r, pair, tile):
        sp[r, t] = pair
        st[r, t] = pack_third(tile[:half], tile[half:], r % 2)

    fresh_tiles = VFRESH // LANES
    reused = [r for r in range(n_seq) if PAIR_TILE[r] >= fresh_tiles]
    for r in reused:
        place(2, r, lanes_of(skip, PAIR_TILE[r] - fresh_tiles), lanes_of(skip, THIRD_TILE[r] - fresh_tiles))
    pl.semaphore_wait(barrier, n_seq - 1)
    for r in reused:
        swaps[2][0].start(r)
    for t in range(3):
        if t == 0:
            full = (matmul(normed, qw[...]) + flat(qb)).astype(jnp.bfloat16)
        elif t == 1:
            full = matmul(normed, kw[...]).astype(jnp.bfloat16)
        else:
            full = (matmul(normed, vw[...]) + flat(vb)).astype(jnp.bfloat16)
        for r in range(n_seq):
            if t < 2 or r not in reused:
                place(t, r, lanes_of(full, PAIR_TILE[r]), lanes_of(full, THIRD_TILE[r]))
        if t < 2:
            swaps[t][0].start()
        else:
            for r in range(n_seq):
                if r not in reused:
                    swaps[2][0].start(r)
    for t in range(3):
        if t < 2:
            swaps[t][1].start()
        else:
            for r in range(n_seq):
                swaps[2][1].start(r)
        rp[t, pl.ds(pl.multiple_of(sq * rows, rows), rows)] = sp[sq, t]
        rt[t, sq] = st[sq, t]
    for i in range(n_seq):
        cols = (i + 1) * rows
        bias[i * rows : (i + 1) * rows, 0:cols] = mask_bias(lens, valid_row, i * rows, rows, cols)
    back = [Gather(n_seq, dp, sq, lambda to: smp.at[to], lambda s: rmp.at[s], lambda i: mssem.at[0, i], lambda i: mrsem.at[0, i]),
            Gather(n_seq, dp, sq, lambda to: smt.at[to], lambda s: rmt.at[s], lambda i: mssem.at[1, i], lambda i: mrsem.at[1, i])]
    low = low_lanes()
    scale = 1.0 / math.sqrt(HDIM)
    keep = (jnp.where(low, scale, 0.0).astype(jnp.bfloat16), jnp.where(low, 0.0, scale).astype(jnp.bfloat16))

    def attend(q, k, v, block):
        scores = matmul_right_t(q, k) + block
        top = jnp.max(scores, axis=-1, keepdims=True)
        powered = jnp.exp(scores - top)
        total = jnp.sum(powered, axis=-1, keepdims=True)
        probs = (powered * (1.0 / total)).astype(jnp.bfloat16)
        return matmul(probs, v), top + jnp.log(total)

    for t in range(3):
        swaps[t][0].wait()
    lane = lax.broadcasted_iota(jnp.int32, (1, LANES), 1)
    for i in range(n_seq):
        here = slice(i * rows, (i + 1) * rows)
        cols = (i + 1) * rows
        block = bias[here, 0:cols]
        q, k, v = rp[0, here], rp[1, 0:cols], rp[2, 0:cols]
        o0, l0 = attend(q * keep[0], k, v, block)
        o1, l1 = attend(q * keep[1], k, v, block)
        smp[i] = jnp.where(low, o0, o1).astype(jnp.bfloat16)
        lse_out[here] = jnp.where(lane == 0, l0, l1)
        back[0].start(i)
    for t in range(3):
        swaps[t][1].wait()
        for s in range(n_seq):
            a, b = unpack_third(rt[t, s])
            third_out[t, s * rows : s * rows + half] = a
            third_out[t, s * rows + half : (s + 1) * rows] = b
    for i in range(n_seq):
        here = slice(i * rows, (i + 1) * rows)
        cols = (i + 1) * rows
        block = bias[here, 0:cols]
        o2, l2 = attend(third_out[0, here] * keep[0], third_out[1, 0:cols], third_out[2, 0:cols], block)
        smt[i] = pack_third(o2[:half], o2[half:], False)
        lse_out[here] = jnp.where(lane == 2, l2, lse_out[here])
        back[1].start(i)
    pair_out[...] = rp[...]
    rmp[sq] = smp[sq]
    rmt[sq] = smt[sq]
    back[0].wait()
    back[1].wait()
    for r in range(n_seq):
        c = PAIR_TILE[r] * LANES
        mixed_out[:, c : c + LANES] = rmp[r]
    for r in range(0, n_seq, 2):
        a, b = join_thirds(rmt[r], rmt[r + 1])
        c = THIRD_TILE[r] * LANES
        mixed_out[0:half, c : c + LANES] = a
        mixed_out[half:rows, c : c + LANES] = b


def front(mesh, hidden, skip, lens, valid, n1g, n1s, qw, qb, kw, vw, vb, collective_id):
    n_dp, n_seq = mesh.shape["dp"], mesh.shape["seq"]
    rows, d = hidden.shape
    group = rows * n_seq
    bf, f32 = jnp.bfloat16, jnp.float32
    vmem = pl.BlockSpec(memory_space=pltpu.VMEM)
    half = rows // 2
    dma = pltpu.SemaphoreType.DMA
    return pl.pallas_call(
        functools.partial(front_kernel, (n_dp, n_seq)),
        in_specs=[pl.BlockSpec(memory_space=pltpu.SMEM)] + [vmem] * 10,
        out_specs=(vmem,) * 5,
        out_shape=(jax.ShapeDtypeStruct((rows, d), bf), jax.ShapeDtypeStruct((rows, d), bf),
                   jax.ShapeDtypeStruct((3, group, LANES), bf), jax.ShapeDtypeStruct((3, group, LANES), bf),
                   jax.ShapeDtypeStruct((group, LANES), f32)),
        scratch_shapes=[
            pltpu.VMEM((n_seq, 3, rows, LANES), bf), pltpu.VMEM((n_seq, 3, half, LANES), bf),
            pltpu.VMEM((3, group, LANES), bf), pltpu.VMEM((3, n_seq, half, LANES), bf),
            pltpu.VMEM((n_seq, rows, LANES), bf), pltpu.VMEM((n_seq, half, LANES), bf),
            pltpu.VMEM((n_seq, rows, LANES), bf), pltpu.VMEM((n_seq, half, LANES), bf),
            pltpu.VMEM((group, group), f32),
            dma((2, 3, n_seq)), dma((2, 3, n_seq)), dma((2, n_seq)), dma((2, n_seq))],
        compiler_params=pltpu.CompilerParams(collective_id=collective_id, has_side_effects=True, vmem_limit_bytes=56 * 2**20),
        name="front",
    )(lens, hidden, skip, valid.reshape(1, -1), n1g, n1s, qw, qb, kw, vw, vb)


GELU_A = 0.044715


def back_kernel(cfg, lens, valid_row, mixed, hidden, og, valid_col, proj_w, proj_b, n2g, n2s, fc_b, out_b, n1g, lse, normed,
                pair_in, third_in, fc_w, out_w, qw, kw, vw,
                out, output, grad_input, grad_skip, small_z, small_out,
                nt_ref, xhat_ref, mid_ref, mlp_acc, two_acc, inv_ref, wf, wo, pair, third, part1,
                gs, gst, gp, gt, gthird, bias, dk_acc, dv_acc, dsp, dst, drp, drt, rows_in, part2,
                recv, gat, sbuf, load_sem, gssem, grsem, dssem, drsem, send_sem, recv_sem, local_sem, ssend, srecv_sem):
    n_dp, n_seq, halves, streams, plan, steps = cfg
    dp, sq = lax.axis_index("dp"), lax.axis_index("seq")
    rows, d = hidden.shape
    half = rows // 2
    bf, f32 = jnp.bfloat16, jnp.float32
    barrier, count = entry_barrier(n_dp, n_seq, dp, sq, True)

    def weight_copies(j):
        cols = pl.ds(j * FCH, FCH)
        return [pltpu.make_async_copy(fc_w.at[:, cols], wf.at[j % 2], load_sem.at[0, j]),
                pltpu.make_async_copy(out_w.at[cols], wo.at[j % 2], load_sem.at[1, j])]

    extra = [pltpu.make_async_copy(pair_in, pair, load_sem.at[2, 0]), pltpu.make_async_copy(third_in, third, load_sem.at[2, 1])]
    late = [pltpu.make_async_copy(qw, wf.at[0], load_sem.at[3, 0]), pltpu.make_async_copy(kw, wf.at[1], load_sem.at[3, 1]),
            pltpu.make_async_copy(vw, wo.at[0, :, pl.ds(0, VFRESH)], load_sem.at[3, 2])]
    for j in range(2):
        for copy in weight_copies(j):
            copy.start()
    for copy in extra:
        copy.start()
    x = hidden[...].astype(f32)
    attn = matmul(mixed[...], proj_w[...]) + flat(proj_b)
    middle = x + attn
    mid_ref[...] = middle
    real = valid_col[...]
    spread = middle - jnp.mean(middle, axis=-1, keepdims=True)
    inv = lax.rsqrt(jnp.mean(spread * spread, axis=-1, keepdims=True) + norm_eps)
    xhat = spread * inv
    xhat_ref[...] = xhat
    inv_ref[...] = jnp.broadcast_to(inv, inv_ref.shape)
    nt_ref[...] = (xhat * flat(n2g) + flat(n2s)).astype(bf)
    s0 = row_sum(jnp.sum(x * x, axis=-1, keepdims=True) * real)
    s1 = row_sum(jnp.sum(attn * attn, axis=-1, keepdims=True) * real)
    s3 = row_sum(real)
    word = lax.broadcasted_iota(jnp.int32, (1, WID), 1)
    sums = jnp.where(word == 0, s0, jnp.where(word == 1, s1, jnp.where(word == 3, s3, 0.0)))
    sbuf[0] = jnp.zeros_like(sbuf[0])
    sbuf[0, 7:8] = row_sum(og[...].astype(f32))
    pl.semaphore_wait(barrier, count)
    ex = Exchange(streams, halves, dp, sq, (part1, part2), out, recv, gat, (send_sem, recv_sem, local_sem))
    tiny = Small(n_dp, n_seq, dp, sq, sbuf, ssend, srecv_sem, small_z, small_out)
    task = iter(range(1, len(plan)))

    def advance():
        for s, k in plan[next(task)]:
            ex.step(s, k)

    def begin(phase, chunk):
        for s, st in enumerate(streams):
            if st[0] == phase and (chunk is None or st[4] == chunk):
                ex.start(s, 0)

    h1, h2 = halves
    for j in range(steps):
        for copy in weight_copies(j):
            copy.wait()
        slot = j % 2
        pre = matmul(nt_ref[...], wf[slot]) + fc_b[:, j * FCH : (j + 1) * FCH]
        sq_pre = pre * pre
        t = jnp.tanh(tanh_coef * (pre + GELU_A * sq_pre * pre))
        act = (0.5 * pre * (1.0 + t)).astype(bf)
        slope = 0.5 * (1.0 + t) + 0.5 * pre * (1.0 - t * t) * (tanh_coef * (1.0 + 3.0 * GELU_A * sq_pre))
        pre_grad = matmul_right_t(og[...], wo[slot]) * slope
        sbuf[0, 8 + j : 9 + j] = row_sum(pre_grad)
        pre_low = pre_grad.astype(bf)
        part1[j * CHUNK : (j + 1) * CHUNK] = matmul_left_t(act, og[...]).astype(bf).reshape(CHUNK, SUB, WID)
        part1[h1 + j * CHUNK : h1 + (j + 1) * CHUNK] = matmul_left_t(nt_ref[...], pre_low).astype(bf).reshape(CHUNK, SUB, WID)
        begin(0, j)
        advance()
        mlp = matmul(act, wo[slot])
        two = matmul_right_t(pre_low, wf[slot])
        if j == 0:
            mlp_acc[...] = mlp
            two_acc[...] = two
        else:
            mlp_acc[...] = mlp_acc[...] + mlp
            two_acc[...] = two_acc[...] + two
        if j + 2 < steps:
            for copy in weight_copies(j + 2):
                copy.start()
        advance()
    for copy in late:
        copy.start()
    two_grad = two_acc[...]
    xhat = xhat_ref[...]
    sbuf[0, 5:6] = row_sum(two_grad * xhat)
    sbuf[0, 6:7] = row_sum(two_grad)
    e = two_grad * flat(n2g)
    centre = jnp.mean(e, axis=-1, keepdims=True)
    along = jnp.mean(e * xhat, axis=-1, keepdims=True)
    grad = og[...].astype(f32) + (e - centre - xhat * along) * inv_ref[:, 0:1]
    grad_low = grad.astype(bf)
    full = matmul_right_t(grad_low, proj_w[...]).astype(bf)
    for r in range(n_seq):
        c = PAIR_TILE[r] * LANES
        gs[r] = full[:, c : c + LANES]
        c = THIRD_TILE[r] * LANES
        gst[r] = pack_third(full[:half, c : c + LANES], full[half:, c : c + LANES], r % 2)
    swap_pair = Swap(n_seq, dp, sq, lambda to: gs.at[to], lambda me: gp.at[pl.ds(me * rows, rows)], lambda i: gssem.at[0, i], lambda i: grsem.at[0, i])
    swap_third = Swap(n_seq, dp, sq, lambda to: gst.at[to], lambda me: gt.at[me], lambda i: gssem.at[1, i], lambda i: grsem.at[1, i])
    swap_pair.start()
    swap_third.start()
    advance()
    mlp_out = mlp_acc[...] + flat(out_b)
    output[...] = (mid_ref[...] + mlp_out).astype(bf)
    s2 = row_sum(jnp.sum(mlp_out * mlp_out, axis=-1, keepdims=True) * valid_col[...])
    sbuf[0, 12:13] = sums + jnp.where(word == 2, s2, 0.0)
    sbuf[0, 4:5] = row_sum(grad)
    mid_ref[...] = grad
    gw = matmul_left_t(mixed[...], grad_low).astype(bf)
    top = d // 2 // SUB
    at = steps * CHUNK
    part1[at : at + top] = gw[: d // 2].reshape(top, SUB, WID)
    part1[h1 + at : h1 + at + top] = gw[d // 2 :].reshape(top, SUB, WID)
    if h1 > at + top:
        for h in range(2):
            part1[h * h1 + at + top : (h + 1) * h1] = jnp.zeros((h1 - at - top, SUB, WID), bf)
    begin(0, steps)
    advance()
    gp[pl.ds(pl.multiple_of(sq * rows, rows), rows)] = gs[sq]
    gt[sq] = gst[sq]
    for i in range(n_seq):
        cols = (i + 1) * rows
        bias[i * rows : (i + 1) * rows, 0:cols] = mask_bias(lens, valid_row, i * rows, rows, cols).astype(bf)
    send = [Gather(n_seq, dp, sq, lambda to: dsp.at[to], lambda s: drp.at[s], lambda i: dssem.at[0, i], lambda i: drsem.at[0, i]),
            Gather(n_seq, dp, sq, lambda to: dst.at[to], lambda s: drt.at[s], lambda i: dssem.at[1, i], lambda i: drsem.at[1, i])]
    advance()
    for copy in extra:
        copy.wait()
    low = low_lanes()
    scale = 1.0 / math.sqrt(HDIM)
    keep = (jnp.where(low, scale, 0.0).astype(bf), jnp.where(low, 0.0, scale).astype(bf))
    ones = (jnp.where(low, 1.0, 0.0).astype(bf), jnp.where(low, 0.0, 1.0).astype(bf))

    def backward(q, k, v, g, block, total):
        probs = jnp.exp(matmul_right_t(q, k) + block - total)
        prob_grad = matmul_right_t(g, v)
        centre = jnp.sum(probs * prob_grad, axis=-1, keepdims=True)
        score_grad = (probs * (prob_grad - centre)).astype(bf)
        return matmul(score_grad, k), matmul_left_t(score_grad, q), matmul_left_t(probs.astype(bf), g)

    swap_pair.wait()
    for i in reversed(range(n_seq)):
        here = slice(i * rows, (i + 1) * rows)
        cols = (i + 1) * rows
        block = bias[here, 0:cols].astype(f32)
        q, k, v, g = pair[0, here], pair[1, 0:cols], pair[2, 0:cols], gp[here]
        dq0, dk0, dv0 = backward(q * keep[0], k, v, g * ones[0], block, lse[here, 0:1])
        dq1, dk1, dv1 = backward(q * keep[1], k, v, g * ones[1], block, lse[here, 1:2])
        if i == n_seq - 1:
            dk_acc[...] = dk0 + dk1
            dv_acc[...] = dv0 + dv1
        else:
            dk_acc[0:cols] = dk_acc[0:cols] + (dk0 + dk1)
            dv_acc[0:cols] = dv_acc[0:cols] + (dv0 + dv1)
        dsp[i, 0] = (jnp.where(low, dq0, dq1) * scale).astype(bf)
        dsp[i, 1] = dk_acc[here].astype(bf)
        dsp[i, 2] = dv_acc[here].astype(bf)
        send[0].start(i)
        advance()
    swap_third.wait()
    for s in range(n_seq):
        a, b = unpack_third(gt[s])
        gthird[s * rows : s * rows + half] = a
        gthird[s * rows + half : (s + 1) * rows] = b
    for i in reversed(range(n_seq)):
        here = slice(i * rows, (i + 1) * rows)
        cols = (i + 1) * rows
        block = bias[here, 0:cols].astype(f32)
        dq, dk, dv = backward(third[0, here] * keep[0], third[1, 0:cols], third[2, 0:cols], gthird[here], block, lse[here, 2:3])
        if i == n_seq - 1:
            dk_acc[...] = dk
            dv_acc[...] = dv
        else:
            dk_acc[0:cols] = dk_acc[0:cols] + dk
            dv_acc[0:cols] = dv_acc[0:cols] + dv
        dq = dq * scale
        dst[i, 0] = pack_third(dq[:half], dq[half:], False)
        for t, a in ((1, dk_acc), (2, dv_acc)):
            dst[i, t] = pack_third(a[i * rows : i * rows + half], a[i * rows + half : (i + 1) * rows], False)
        send[1].start(i)
        advance()
    drp[sq] = dsp[sq]
    drt[sq] = dst[sq]
    x = hidden[...].astype(f32)
    spread = x - jnp.mean(x, axis=-1, keepdims=True)
    inv = lax.rsqrt(jnp.mean(spread * spread, axis=-1, keepdims=True) + norm_eps)
    xhat = spread * inv
    send[0].wait()
    for t in range(3):
        for r in range(n_seq):
            c = PAIR_TILE[r] * LANES
            rows_in[t, :, c : c + LANES] = drp[r, t]
    advance()
    send[1].wait()
    for t in range(3):
        for r in range(0, n_seq, 2):
            a, b = join_thirds(drt[r, t], drt[r + 1, t])
            c = THIRD_TILE[r] * LANES
            rows_in[t, 0:half, c : c + LANES] = a
            rows_in[t, half:rows, c : c + LANES] = b
    nl = normed[...]
    dq, dk, dv = rows_in[0], rows_in[1], rows_in[2]
    fresh = dv[:, 0:VFRESH]
    grad_skip[...] = dv[:, VFRESH:]
    units_d = d // SUB
    uv = d // 4 // SUB
    part2[0:units_d] = matmul_left_t(nl, dq).astype(bf).reshape(units_d, SUB, WID)
    part2[h2 : h2 + units_d] = matmul_left_t(nl, dk).astype(bf).reshape(units_d, SUB, WID)
    gv = matmul_left_t(nl, fresh).astype(bf)
    for h in range(2):
        for side in range(2):
            r0 = side * (d // 2) + h * (d // 4)
            part2[h * h2 + units_d : h * h2 + units_d + uv, :, side * VFRESH : (side + 1) * VFRESH] = (
                gv[r0 : r0 + d // 4].reshape(uv, SUB, VFRESH))
        if h2 > units_d + uv:
            part2[h * h2 + units_d + uv : (h + 1) * h2] = jnp.zeros((h2 - units_d - uv, SUB, WID), bf)
    begin(1, None)
    advance()
    for copy in late:
        copy.wait()
    normed_grad = matmul_right_t(dq, wf[0]) + matmul_right_t(dk, wf[1]) + matmul_right_t(fresh, wo[0, :, 0:VFRESH])
    f = normed_grad * flat(n1g)
    centre = jnp.mean(f, axis=-1, keepdims=True)
    along = jnp.mean(f * xhat, axis=-1, keepdims=True)
    grad_input[...] = (mid_ref[...] + (f - centre - xhat * along) * inv).astype(bf)
    sbuf[0, 0:1] = row_sum(normed_grad * xhat)
    sbuf[0, 1:2] = row_sum(normed_grad)
    sbuf[0, 2:3] = row_sum(dq.astype(f32))
    sbuf[0, 3:4, 0:VFRESH] = row_sum(fresh.astype(f32))
    tiny.copy(0).start()
    todo = plan[next(task)]
    gap = max(1, len(todo) // (len(tiny.dims) + 2))
    for left, (s, k) in enumerate(todo):
        ex.step(s, k)
        if left % gap == gap - 1:
            tiny.step()
    tiny.rest()


def back(mesh, lens, valid, mixed, hidden, og, valid_col, proj_w, proj_b, n2g, n2s, fc_b, out_b, n1g, lse, normed,
         pair, third, fc_w, out_w, qw, kw, vw, collective_id):
    n_dp, n_seq = mesh.shape["dp"], mesh.shape["seq"]
    rows, d = hidden.shape
    group = rows * n_seq
    half = rows // 2
    steps = fc_w.shape[1] // FCH
    bf, f32 = jnp.bfloat16, jnp.float32
    quantum = n_dp // 2 * n_seq
    needed = (steps * CHUNK + d // 2 // SUB, d // SUB + d // 4 // SUB)
    halves = tuple(-(-n // quantum) * quantum for n in needed)
    streams = plan_streams(n_dp, n_seq, halves, steps)
    plan, _ = schedule(streams, steps, rows)
    n_st = 2 * (bits_of(n_dp) + bits_of(n_seq))
    n_small = bits_of(n_dp) + bits_of(n_seq)
    ns = len(streams)
    vmem = pl.BlockSpec(memory_space=pltpu.VMEM)
    hbm = pl.BlockSpec(memory_space=pl.ANY)
    dma = pltpu.SemaphoreType.DMA
    units = lambda n: pltpu.VMEM((n, SUB, WID), bf)
    wide = lambda: pltpu.VMEM((rows, d), f32)
    sshape = jax.ShapeDtypeStruct((16, WID), f32)
    args = (lens, valid.reshape(1, -1), mixed, hidden, og, valid_col, proj_w, proj_b, n2g, n2s, fc_b.reshape(1, -1), out_b, n1g, lse, normed,
            pair, third, fc_w, out_w, qw, kw, vw)
    outs = pl.pallas_call(
        functools.partial(back_kernel, (n_dp, n_seq, halves, streams, plan, steps)),
        in_specs=[pl.BlockSpec(memory_space=pltpu.SMEM)] + [vmem] * 14 + [hbm] * 7,
        out_specs=(hbm, vmem, vmem, vmem, vmem, vmem),
        out_shape=(jax.ShapeDtypeStruct((2 * sum(halves), SUB, WID), bf), jax.ShapeDtypeStruct((rows, d), bf),
                   jax.ShapeDtypeStruct((rows, d), bf), jax.ShapeDtypeStruct((rows, d - VFRESH), bf), sshape, sshape),
        scratch_shapes=[
            pltpu.VMEM((rows, d), bf), wide(), wide(), wide(), wide(), pltpu.VMEM((rows, LANES), f32),
            pltpu.VMEM((2, d, FCH), bf), pltpu.VMEM((2, FCH, d), bf),
            pltpu.VMEM((3, group, LANES), bf), pltpu.VMEM((3, group, LANES), bf), units(2 * halves[0]),
            pltpu.VMEM((n_seq, rows, LANES), bf), pltpu.VMEM((n_seq, half, LANES), bf),
            pltpu.VMEM((group, LANES), bf), pltpu.VMEM((n_seq, half, LANES), bf), pltpu.VMEM((group, LANES), bf),
            pltpu.VMEM((group, group), bf), pltpu.VMEM((group, LANES), f32), pltpu.VMEM((group, LANES), f32),
            pltpu.VMEM((n_seq, 3, rows, LANES), bf), pltpu.VMEM((n_seq, 3, half, LANES), bf),
            pltpu.VMEM((n_seq, 3, rows, LANES), bf), pltpu.VMEM((n_seq, 3, half, LANES), bf),
            pltpu.VMEM((3, rows, d), bf), units(2 * halves[1]),
            units(Exchange.recv_total(streams)), units(sum(halves)),
            pltpu.VMEM((2 * n_small, 16, WID), f32), dma((4, max(4, steps))),
            dma((2, n_seq)), dma((2, n_seq)), dma((2, n_seq)), dma((2, n_seq)),
            dma((ns, n_st)), dma((ns, n_st)), dma((ns,)), dma((n_small,)), dma((n_small,))],
        compiler_params=pltpu.CompilerParams(collective_id=collective_id, has_side_effects=True, vmem_limit_bytes=67043328),
        name="back",
    )(*args)
    return outs, halves


def local(
    mesh,
    hidden_in,
    skip_values,
    out_grad,
    doc_lens,
    valid,
    norm1_gain,
    norm1_shift,
    query_w,
    query_b,
    key_w,
    value_w,
    value_b,
    proj_w,
    proj_b,
    norm2_gain,
    norm2_shift,
    fc_w,
    fc_b,
    out_w,
    out_b,
):
    seq_size = lax.axis_size("seq")
    seq_rank = lax.axis_index("seq")
    tok_rows = hidden_in.shape[0]
    valid_col = lax.dynamic_slice_in_dim(valid, seq_rank * tok_rows, tok_rows, 0).astype(jnp.float32)[:, None]
    normed, mixed, pair, third, lse = front(
        mesh, hidden_in, skip_values, doc_lens, valid, norm1_gain, norm1_shift, query_w, query_b, key_w, value_w, value_b, 0
    )
    (summed, output, grad_input, grad_skip, small_z, small_all), halves = back(
        mesh, doc_lens, valid, mixed, hidden_in, out_grad, valid_col, proj_w, proj_b, norm2_gain, norm2_shift, fc_b, out_b,
        norm1_gain, lse, normed, pair, third, fc_w, out_w, query_w, key_w, value_w, 1
    )
    (
        grad_out_w, grad_fc_w, grad_proj_w, grad_query_w, grad_key_w, grad_value_w,
        grad_norm1_gain, grad_norm1_shift, grad_query_b, grad_value_b, grad_proj_b, grad_norm2_gain, grad_norm2_shift,
        grad_out_b, grad_fc_b, norm_values, grad_input, grad_skip,
    ) = widen(summed.reshape(-1, WID), small_all, small_z, grad_input, grad_skip, halves, D, fc_w.shape[1], VFRESH)
    return (
        output,
        grad_input,
        grad_skip,
        grad_norm1_gain,
        grad_norm1_shift,
        grad_query_w,
        grad_query_b,
        grad_key_w,
        grad_value_w,
        grad_value_b,
        grad_proj_w,
        grad_proj_b,
        grad_norm2_gain,
        grad_norm2_shift,
        grad_fc_w,
        grad_fc_b,
        grad_out_w,
        grad_out_b,
        norm_values,
    )


def solution(mesh):
    placed = (
        P(("dp", "seq"), None),
        P(("dp", "seq"), None),
        P(("dp", "seq"), None),
        P("dp", None),
        P("dp"),
        P(),
        P(),
        P(),
        P(),
        P(),
        P(),
        P(),
        P(),
        P(),
        P(),
        P(),
        P(),
        P(),
        P(),
        P(),
    )
    return jax.shard_map(
        functools.partial(local, mesh),
        mesh=mesh,
        in_specs=placed,
        out_specs=(
            P(("dp", "seq"), None),
            P(("dp", "seq"), None),
            P(("dp", "seq"), None),
            P(),
            P(),
            P(),
            P(),
            P(),
            P(),
            P(),
            P(),
            P(),
            P(),
            P(),
            P(),
            P(),
            P(),
            P(),
            P("dp", None),
        ),
        check_vma=False,
    )
```
